32 devices in a mesh: ctx: 8 (over y, x, core), fsdp: 4 (over z).
Axes of the slice: x: 2, y: 2, z: 4, core: 2. Of those that a mesh axis runs over, the one named last changes fastest.
Arguments:
- tokens: bfloat16 [4, 2048, 2048], P('fsdp', 'ctx'), may hold values from -6 to 6
- cotangent: bfloat16 [4, 2048, 2048], P('fsdp', 'ctx'), may hold values from -6 to 6
- doc_starts: int32 [4, 8], P('fsdp'), may hold values from 0 to 2047, as said below
- deal_order: int32 [16], replicated, may hold values from 0 to 15, as said below
- query_key_value_weight: bfloat16 [2048, 1536], P('fsdp'), may hold values from -0.125 to 0.125
- w_out: bfloat16 [1024, 2048], P('fsdp'), may hold values from -1.5 to 1.5
- w_gate: bfloat16 [2048, 1024], P('fsdp'), may hold values from -0.125 to 0.125
- w_up: bfloat16 [2048, 1024], P('fsdp'), may hold values from -0.125 to 0.125
- w_down: bfloat16 [1024, 2048], P('fsdp'), may hold values from -0.1875 to 0.1875
- gain_attn: bfloat16 [2048], P('fsdp'), may hold values from 0.5 to 1.5
- gain_ffn: bfloat16 [2048], P('fsdp'), may hold values from 0.5 to 1.5
- gain_qk: bfloat16 [2, 64], P(None, 'fsdp'), may hold values from 1 to 2
Outputs:
- mixed_out: bfloat16 [4, 2048, 2048], P('fsdp', 'ctx')
- tokens_grad: float32 [4, 2048, 2048], P('fsdp', 'ctx')
- w_qkv_grad: float32 [2048, 1536], P('fsdp')
- w_out_grad: float32 [1024, 2048], P('fsdp')
- w_gate_grad: float32 [2048, 1024], P('fsdp')
- w_up_grad: float32 [2048, 1024], P('fsdp')
- w_down_grad: float32 [1024, 2048], P('fsdp')
- gain_attn_grad: float32 [2048], P('fsdp')
- gain_ffn_grad: float32 [2048], P('fsdp')
- gain_qk_grad: float32 [2, 64], P(None, 'fsdp')
The draws below stay inside these ranges and needn't reach their ends.
Inputs may be any that keep to these rules, and one draw needn't show every extreme that they name: `doc_starts`: in each pack the first entry is 0 and entries rise; every document (from its start to the next start, the last one to 2048) holds 1 to 1024 tokens, one document of each pack holds exactly 1024, and the last document of each pack holds one token, so its start is 2047. `deal_order`: A permutation of the 16 blocks of a pack; the blocks at stored places 2 c and 2 c + 1 add up to 15.
All inputs are finite; a program needn't handle non-finite values.
Results may differ from the reference program's by a relative error of at most 0.017.
The reference program's roundings to bfloat16 on the way count: a program that leaves them out, or rounds other values in their place, can miss the bound.
Values may be sent and summed in bfloat16 or wider, within the bound.
A program may use at most 192 MiB of HBM per device.

```python
import jax
import jax.numpy as jnp
from jax import lax

MODEL_WIDTH = 2048
QUERY_HEADS = 16
KEY_VALUE_HEADS = 4
HEAD_SIZE = 64
FF = 1024
TOK_DEV = 256
NDOC = 8
PACKS = 4
PACK_LENGTH = 2048
NBLK = 16
DOCMAX = 1024


def one_pack(pack_key):
    remain = PACK_LENGTH - 1 - DOCMAX
    chosen = jax.random.permutation(jax.random.fold_in(pack_key, 1), remain - 1)[:NDOC - 3] + 1
    cut_points = jnp.sort(chosen).astype(jnp.int32)
    bounds = jnp.concatenate([jnp.zeros((1,), jnp.int32), cut_points, jnp.full((1,), remain, jnp.int32)])
    others = bounds[1:] - bounds[:-1]
    long_slot = jax.random.randint(jax.random.fold_in(pack_key, 2), (), 0, NDOC - 1)
    places = jnp.arange(NDOC - 1, dtype=jnp.int32)
    source = jnp.clip(jnp.where(places > long_slot, places - 1, places), 0, NDOC - 3)
    leading = jnp.where(places == long_slot, DOCMAX, others[source]).astype(jnp.int32)
    lengths = jnp.concatenate([leading, jnp.ones((1,), jnp.int32)])
    return (jnp.cumsum(lengths) - lengths).astype(jnp.int32)


def draw_doc_starts(key, part):
    pack_keys = jax.random.split(jax.random.fold_in(key, 7), PACKS)
    return jax.vmap(one_pack)(pack_keys)


def draw_deal_order(key, part):
    half_count = NBLK // 2
    pair_order = jax.random.permutation(jax.random.fold_in(key, 11), half_count).astype(jnp.int32)
    flip_bits = jax.random.randint(jax.random.fold_in(key, 12), (half_count,), 0, 2)
    mirror = NBLK - 1 - pair_order
    first_block = jnp.where(flip_bits == 1, mirror, pair_order)
    second_block = jnp.where(flip_bits == 1, pair_order, mirror)
    return jnp.stack([first_block, second_block], axis=1).reshape(NBLK).astype(jnp.int32)


def levels(rng, extent, cuts, least, high):
    def one(dim, blocks):
        steps = jax.random.uniform(jax.random.fold_in(jax.random.fold_in(rng, 6), dim), (blocks,), jnp.float32, least / len(cuts), high / len(cuts))
        return jnp.repeat(jnp.exp(steps), extent[dim] // blocks).reshape((-1,) + (1,) * (len(extent) - dim - 1))

    factor_of = one(*cuts[0])
    for cut in cuts[1:]:
        factor_of = factor_of * one(*cut)
    return factor_of


def bell_draw(key, shape, spread, bound, cuts=(), kind=jnp.bfloat16):
    entries = spread * jax.random.normal(key, shape, jnp.float32)
    if cuts:
        entries = entries * levels(key, shape, cuts, -0.22, 0.18)
    return jnp.clip(entries, -bound, bound).astype(kind)


def setup_inputs(seed: int = 0) -> dict:
    seeds = jax.random.split(jax.random.key(seed), 13)
    return {
        "tokens": bell_draw(seeds[0], (PACKS, PACK_LENGTH, MODEL_WIDTH), 1.0, 6.0, ((0, 4), (1, 8))),
        "cotangent": bell_draw(seeds[1], (PACKS, PACK_LENGTH, MODEL_WIDTH), 1.0, 6.0, ((0, 4), (1, 8))),
        "doc_starts": draw_doc_starts(jax.random.fold_in(seeds[12], 71), 0),
        "deal_order": draw_deal_order(jax.random.fold_in(seeds[12], 71), 0),
        "query_key_value_weight": bell_draw(seeds[4], (MODEL_WIDTH, (QUERY_HEADS + 2 * KEY_VALUE_HEADS) * HEAD_SIZE), MODEL_WIDTH ** -0.5, 0.125, ((0, 4),)),
        "w_out": bell_draw(seeds[5], (QUERY_HEADS * HEAD_SIZE, MODEL_WIDTH), (QUERY_HEADS * HEAD_SIZE // 64) ** -0.5, 1.5, ((0, 4),)),
        "w_gate": bell_draw(seeds[6], (MODEL_WIDTH, FF), MODEL_WIDTH ** -0.5, 0.125, ((0, 4),)),
        "w_up": bell_draw(seeds[7], (MODEL_WIDTH, FF), MODEL_WIDTH ** -0.5, 0.125, ((0, 4),)),
        "w_down": bell_draw(seeds[8], (FF, MODEL_WIDTH), FF ** -0.5, 0.1875, ((0, 4),)),
        "gain_attn": jnp.clip(1.0 + 0.1 * jax.random.normal(seeds[9], (MODEL_WIDTH,), jnp.float32), 0.5, 1.5).astype(jnp.bfloat16),
        "gain_ffn": jnp.clip(1.0 + 0.1 * jax.random.normal(seeds[10], (MODEL_WIDTH,), jnp.float32), 0.5, 1.5).astype(jnp.bfloat16),
        "gain_qk": jnp.clip(1.0 + 1.0 * jax.random.uniform(seeds[11], (2, HEAD_SIZE), jnp.float32) ** levels(seeds[11], (2, HEAD_SIZE), ((1, 4),), -0.2, 0.2), 1.0, 2.0).astype(jnp.bfloat16),
    }


EPSILON = 1e-06
THETA = 10000.0

@jax.custom_vjp
def low(v):
    return lax.optimization_barrier(v.astype(jnp.bfloat16)).astype(jnp.float32)

@jax.custom_vjp
def low_back(v):
    return v

def low_keep(v):
    return (low(v), None)

def low_pass(kept, grad):
    return (grad,)

def back_keep(v):
    return (v, None)

def back_low(kept, grad):
    return (low(grad),)
low.defvjp(low_keep, low_pass)
low_back.defvjp(back_keep, back_low)

def exact_dot(left, right):
    return jnp.dot(left, right, precision=lax.Precision.HIGHEST)

def rms_scale(values, gain_vec):
    return values * lax.rsqrt(lax.optimization_barrier(jnp.mean(values * values, axis=-1, keepdims=True)) + EPSILON) * gain_vec

def rotate(values, cosines, sine_vals):
    half_dim = values.shape[-1] // 2
    first_half = values[..., :half_dim]
    second_half = values[..., half_dim:]
    return jnp.concatenate([first_half * cosines - second_half * sine_vals, second_half * cosines + first_half * sine_vals], axis=-1)

def rotary_tables(position, doc_begin):
    offsets = (position - doc_begin).astype(jnp.float32)
    frequency = THETA ** (-jnp.arange(0, HEAD_SIZE // 2, dtype=jnp.float32) * 2.0 / HEAD_SIZE)
    angles = offsets[:, None] * frequency[None, :]
    return (jnp.cos(angles)[:, None, :], jnp.sin(angles)[:, None, :])

def pack_places(deal_order, start_row):
    block_len = TOK_DEV // 2
    stored = jnp.arange(PACK_LENGTH, dtype=jnp.int32)
    position = (deal_order[stored // block_len] * block_len + stored % block_len).astype(jnp.int32)
    doc_begin = lax.optimization_barrier(jnp.max(jnp.where(start_row[None, :] <= position[:, None], start_row[None, :], 0), axis=1))
    return (position, doc_begin.astype(jnp.int32))

def attend_block(query_heads_rows, q_place, q_begin, key_mat, value_mat, k_place, k_begin):
    query_row_block = query_heads_rows.shape[0]
    grouped_heads = query_heads_rows.reshape(query_row_block, KEY_VALUE_HEADS, QUERY_HEADS // KEY_VALUE_HEADS, HEAD_SIZE)
    scores = jnp.einsum('qkgd,tkd->kgqt', grouped_heads, key_mat, precision=lax.Precision.HIGHEST) * HEAD_SIZE ** (-0.5)
    allowed = (q_begin[:, None] == k_begin[None, :]) & (k_place[None, :] <= q_place[:, None])
    scores = low_back(jnp.where(allowed[None, None], scores, -1e+30))
    row_max = lax.optimization_barrier(jnp.max(scores, axis=-1, keepdims=True))
    exp_scores = jnp.exp(scores - row_max)
    soft_probs = low(exp_scores / lax.optimization_barrier(jnp.sum(exp_scores, axis=-1, keepdims=True)))
    mixture = jnp.einsum('kgqt,tkd->qkgd', soft_probs, value_mat, precision=lax.Precision.HIGHEST)
    return mixture.reshape(query_row_block, QUERY_HEADS * HEAD_SIZE)

def pack_forward(pack_in, params, position, doc_begin):
    query_key_value_weight, w_out, w_gate, w_up, w_down, gain_attn, gain_ffn, gain_qk = params
    normed = low(rms_scale(pack_in, gain_attn))
    projected_rows = low_back(exact_dot(normed, query_key_value_weight))
    query_heads_rows = projected_rows[:, :QUERY_HEADS * HEAD_SIZE].reshape(PACK_LENGTH, QUERY_HEADS, HEAD_SIZE)
    key_portion = projected_rows[:, QUERY_HEADS * HEAD_SIZE:(QUERY_HEADS + KEY_VALUE_HEADS) * HEAD_SIZE].reshape(PACK_LENGTH, KEY_VALUE_HEADS, HEAD_SIZE)
    value_portion = projected_rows[:, (QUERY_HEADS + KEY_VALUE_HEADS) * HEAD_SIZE:].reshape(PACK_LENGTH, KEY_VALUE_HEADS, HEAD_SIZE)
    cosines, sine_vals = rotary_tables(position, doc_begin)
    query_heads_rows = low(rotate(rms_scale(query_heads_rows, gain_qk[0]), cosines, sine_vals))
    key_portion = low(rotate(rms_scale(key_portion, gain_qk[1]), cosines, sine_vals))
    value_portion = low(value_portion)
    query_block = min(512, PACK_LENGTH)
    block_total = PACK_LENGTH // query_block

    def one_block(pieces):
        return attend_block(pieces[0], pieces[1], pieces[2], key_portion, value_portion, position, doc_begin)
    attended = lax.map(jax.checkpoint(one_block), (query_heads_rows.reshape(block_total, query_block, QUERY_HEADS, HEAD_SIZE), position.reshape(block_total, query_block), doc_begin.reshape(block_total, query_block)))
    attended = low(low_back(attended.reshape(PACK_LENGTH, QUERY_HEADS * HEAD_SIZE)))
    branch = low_back(exact_dot(attended, w_out))
    hidden_in = pack_in + branch
    normed_ffn = low(rms_scale(hidden_in, gain_ffn))
    gate_act = low_back(exact_dot(normed_ffn, w_gate))
    upward = low_back(exact_dot(normed_ffn, w_up))
    hidden = low(gate_act * jax.nn.sigmoid(gate_act) * upward)
    return hidden_in + exact_dot(hidden, w_down)

def reference(tokens, cotangent, doc_starts, deal_order, query_key_value_weight, w_out, w_gate, w_up, w_down, gain_attn, gain_ffn, gain_qk):
    params = tuple((weight.astype(jnp.float32) for weight in (query_key_value_weight, w_out, w_gate, w_up, w_down, gain_attn, gain_ffn, gain_qk)))

    def per_pack(totals, pieces):
        pack_in, pack_cot, start_row = pieces
        position, doc_begin = pack_places(deal_order, start_row)

        def forward(inputs, weights):
            return pack_forward(inputs, weights, position, doc_begin)
        result, pullback = jax.vjp(forward, pack_in.astype(jnp.float32), params)
        input_grad, weight_grads = pullback(pack_cot.astype(jnp.float32))
        totals = jax.tree.map(lambda left_term, right_term: left_term + right_term, totals, weight_grads)
        return (totals, (result.astype(jnp.bfloat16), input_grad))
    zeros_init = tuple((jnp.zeros(weight.shape, jnp.float32) for weight in params))
    totals, outputs = lax.scan(per_pack, zeros_init, (tokens, cotangent, doc_starts))
    return (outputs[0], outputs[1], totals[0], totals[1], totals[2], totals[3], totals[4], totals[5], totals[6], totals[7])
```

```python
import functools
import math

import jax
import jax.numpy as jnp
from jax import lax
from jax.experimental import pallas as pl
from jax.experimental.pallas import tpu as pltpu
from jax.sharding import PartitionSpec as P

QUERY_HEADS = 16
KEY_VALUE_HEADS = 4
HEAD_SIZE = 64


EPSILON = 1e-06
THETA = 10000.0


def times_transposed(left, right):
    return lax.dot_general(
        left, right, (((1,), (1,)), ((), ())), preferred_element_type=jnp.float32
    )


def transposed_times(left, right):
    return lax.dot_general(
        left, right, (((0,), (0,)), ((), ())), preferred_element_type=jnp.float32
    )


def norm_forward(values, gain_vec):
    inverse = lax.rsqrt(jnp.mean(values * values, axis=-1, keepdims=True) + EPSILON)
    return (values * inverse * gain_vec, inverse)


def norm_backward(values, inverse, gain_vec, grad_out):
    scaled = grad_out * gain_vec
    grad_in = inverse * (
        scaled - values * inverse * inverse * jnp.mean(scaled * values, axis=-1, keepdims=True)
    )
    return (grad_in, grad_out * values * inverse)


def rotate(values, cosines, sine_vals):
    half_dim = values.shape[-1] // 2
    first_half = values[..., :half_dim]
    second_half = values[..., half_dim:]
    return jnp.concatenate(
        [
            first_half * cosines - second_half * sine_vals,
            second_half * cosines + first_half * sine_vals,
        ],
        axis=-1,
    )


def rotate_back(grad_out, cosines, sine_vals):
    half_dim = grad_out.shape[-1] // 2
    first_half = grad_out[..., :half_dim]
    second_half = grad_out[..., half_dim:]
    return jnp.concatenate(
        [
            first_half * cosines + second_half * sine_vals,
            second_half * cosines - first_half * sine_vals,
        ],
        axis=-1,
    )


def rotary_tables(position, doc_begin):
    offsets = (position - doc_begin).astype(jnp.float32)
    frequency = THETA ** (-jnp.arange(0, HEAD_SIZE // 2, dtype=jnp.float32) * 2.0 / HEAD_SIZE)
    angles = offsets[:, None] * frequency[None, :]
    return (jnp.cos(angles)[:, None, :], jnp.sin(angles)[:, None, :])


MESH = pl.DeviceIdType.MESH
DMA = pltpu.SemaphoreType.DMA
HBM_SPEC = pl.BlockSpec(memory_space=pl.ANY)
SPACING = 2


def plane_shape(ctx_count):
    chips = ctx_count // 2
    bits = chips.bit_length() - 1
    assert 2**bits == chips and ctx_count == 2 * chips
    return chips, bits


class Place:
    def __init__(self, ctx_count, fsdp_count):
        self.chips, self.bits = plane_shape(ctx_count)
        self.fsdp_count = fsdp_count
        self.ctx = lax.axis_index("ctx")
        self.z = lax.axis_index("fsdp")
        self.core = self.ctx % 2
        chip = self.ctx // 2
        self.bit = [(chip // 2**j) % 2 for j in range(self.bits)]
        self.across = [self.ctx + (1 - 2 * self.bit[j]) * 2 * 2**j for j in range(self.bits)]
        self.partner = self.ctx + 1 - 2 * self.core
        self.orders = (list(range(self.bits)), list(reversed(range(self.bits))))

    def at(self, free=(), other=None):
        return tuple(
            slice(None) if j in free else (1 - self.bit[j] if j == other else self.bit[j])
            for j in reversed(range(self.bits))
        )

    def barrier(self, plane=True, line=True, near=False):
        sem = pltpu.get_barrier_semaphore()
        count = 0
        if plane:
            for p in self.across + [self.partner]:
                pl.semaphore_signal(sem, inc=1, device_id={"ctx": p}, device_id_type=MESH)
                count += 1
        if line:
            for k in range(1, self.fsdp_count):
                pl.semaphore_signal(
                    sem,
                    inc=1,
                    device_id={"fsdp": (self.z + k) % self.fsdp_count},
                    device_id_type=MESH,
                )
                count += 1
        pl.semaphore_wait(sem, count)


def remote(src, dst, send, recv, **where):
    return pltpu.make_async_remote_copy(
        src, dst, send, recv, device_id=where, device_id_type=MESH
    )


def run_ticks(jobs, spacing=SPACING):
    depth = max(len(job) for job in jobs)
    for tick in range(len(jobs) + spacing * (depth - 1)):
        for j in reversed(range(depth)):
            t = tick - spacing * j
            if 0 <= t < len(jobs) and j < len(jobs[t]):
                jobs[t][j]()


def column_half(ref, half):
    n = ref.shape[-1] // 2
    return pl.ds(half * n, n)


def gather_kernel(nf, nc, count, *refs):
    shards, small = refs[:count], refs[count]
    outs, small_out = refs[count + 1 : 2 * count + 1], refs[2 * count + 1]
    stages = refs[2 * count + 2 : 3 * count + 3]
    up_s, up_r, down_s, down_r, ps, pr, cs, cr, ss, sr, load_sem, store_sem = refs[3 * count + 3 :]
    me = Place(nc, nf)
    z = me.z
    loads = [
        pltpu.make_async_copy(src, dst, load_sem.at[i])
        for i, (src, dst) in enumerate(zip(list(shards) + [small], stages))
    ]
    stores = [
        pltpu.make_async_copy(stages[i], dst.at[z], store_sem.at[i])
        for i, dst in enumerate(list(outs) + [small_out])
    ]
    for load in loads:
        load.start()
    me.barrier()

    def source(k):
        pairs = jnp.minimum(z, nf - 1 - z)
        near = (k + 1) // 2
        near_source = z - near if k % 2 == 1 else z + near
        far = k - pairs
        far_source = jnp.where(2 * z < nf - 1, z + far, z - far)
        return jnp.where(k <= 2 * pairs, near_source, far_source)

    sources = [None] + [source(k) for k in range(1, nf)]

    def line_copy(i, src_z, src, up):
        to = z + 1 if up else z - 1
        sems = (up_s, up_r) if up else (down_s, down_r)
        return remote(
            src,
            outs[i].at[(src_z, me.core) + me.at()],
            sems[0].at[i, src_z],
            sems[1].at[i, src_z],
            fsdp=to,
        )

    def line_start(i, src_z, src, up, condition):
        @pl.when(condition)
        def _():
            line_copy(i, src_z, src, up).start()

    def small_copy(k):
        return remote(small, small_out.at[z], ss.at[k], sr.at[k], fsdp=(z + k) % nf)

    for k in range(1, nf):
        small_copy(k).start()
    for i in range(count):
        mine = shards[i].at[(me.core,) + me.at()]
        line_start(i, z, mine, True, z + 1 < nf)
        line_start(i, z, mine, False, z > 0)

    def line_stage(i, k):
        src_z = sources[k]
        here = outs[i].at[(src_z, me.core) + me.at()]
        below = src_z < z

        @pl.when(below)
        def _():
            line_copy(i, src_z, here, True).wait_recv()

        @pl.when(jnp.logical_not(below))
        def _():
            line_copy(i, src_z, here, False).wait_recv()

        line_start(i, src_z, here, True, jnp.logical_and(below, z + 1 < nf))
        line_start(i, src_z, here, False, jnp.logical_and(src_z > z, z > 0))

    def plane_copy(i, k, half, j):
        order = me.orders[half]
        ref = outs[i].at[
            (sources[k], me.core) + me.at(order[:j]) + (slice(None), column_half(outs[i], half))
        ]
        return remote(
            ref, ref, ps.at[half, i, k, j], pr.at[half, i, k, j], ctx=me.across[order[j]]
        )

    def core_copy(i, k):
        ref = outs[i].at[sources[k], me.core]
        return remote(ref, ref, cs.at[i, k], cr.at[i, k], ctx=me.partner)

    def plane_stage(i, k, j):
        if j == 0:
            line_stage(i, k)
        else:
            for half in (0, 1):
                plane_copy(i, k, half, j - 1).wait_recv()
        if j < me.bits:
            for half in (0, 1):
                plane_copy(i, k, half, j).start()
        else:
            core_copy(i, k).start()

    order = [(i, k) for i in range(count) for k in range(1, nf)]
    jobs = [
        [functools.partial(plane_stage, i, k, j) for j in range(me.bits + 1)]
        + [core_copy(i, k).wait_recv]
        for i, k in order
    ]
    for load, store in zip(loads, stores):
        load.wait()
        store.start()
    run_ticks(jobs)
    for k in range(1, nf):
        small_copy(k).wait_recv()
        small_copy(k).wait_send()
    for i in range(count):
        @pl.when(z + 1 < nf)
        def _():
            line_copy(i, z, shards[i].at[(me.core,) + me.at()], True).wait_send()

        @pl.when(z > 0)
        def _():
            line_copy(i, z, shards[i].at[(me.core,) + me.at()], False).wait_send()

    for i, k in order:
        src_z = sources[k]
        here = outs[i].at[(src_z, me.core) + me.at()]

        @pl.when(jnp.logical_and(src_z < z, z + 1 < nf))
        def _():
            line_copy(i, src_z, here, True).wait_send()

        @pl.when(jnp.logical_and(src_z > z, z > 0))
        def _():
            line_copy(i, src_z, here, False).wait_send()

        for half in (0, 1):
            for j in range(me.bits):
                plane_copy(i, k, half, j).wait_send()
        core_copy(i, k).wait_send()
    for store in stores:
        store.wait()


def gather_weights(nf, nc, shards, small):
    _, bits = plane_shape(nc)
    count = len(shards)
    views = [w.reshape((2,) * (1 + bits) + (w.shape[0] // nc, w.shape[1])) for w in shards]
    arrays = views + [small]
    outs = pl.pallas_call(
        functools.partial(gather_kernel, nf, nc, count),
        out_shape=[jax.ShapeDtypeStruct((nf,) + v.shape, v.dtype) for v in arrays],
        in_specs=[HBM_SPEC] * (count + 1),
        out_specs=[HBM_SPEC] * (count + 1),
        scratch_shapes=[pltpu.VMEM(v.shape, v.dtype) for v in arrays]
        + [DMA((count, nf))] * 4
        + [DMA((2, count, nf, bits))] * 2
        + [DMA((count, nf))] * 2
        + [DMA((nf,))] * 2
        + [DMA((count + 1,))] * 2,
        compiler_params=pltpu.CompilerParams(collective_id=0, has_side_effects=True),
        name="gather_weights",
    )(*arrays)
    return [o.reshape(nf * w.shape[0], w.shape[1]) for o, w in zip(outs, shards)], outs[count]


def gather_pair_kernel(nf, nc, pair, out, stage, ps, pr, cs, cr, load_sem, store_sem):
    me = Place(nc, nf)
    load = pltpu.make_async_copy(pair, stage, load_sem)
    load.start()
    me.barrier(line=False)

    def plane_copy(half, j):
        order = me.orders[half]
        where = (slice(None), column_half(out, half))
        dst = out.at[me.at(order[:j]) + (me.core,) + where]
        src = pair.at[where] if j == 0 else dst
        return remote(src, dst, ps.at[half, j], pr.at[half, j], ctx=me.across[order[j]])

    own_core = remote(pair, out.at[me.at() + (me.core,)], cs.at[0, 0], cr.at[0, 0], ctx=me.partner)

    def core_copy(half, j):
        order = me.orders[half]
        ref = out.at[
            me.at(order[:j], other=order[j]) + (me.core, slice(None), column_half(out, half))
        ]
        return remote(ref, ref, cs.at[half, j + 1], cr.at[half, j + 1], ctx=me.partner)

    for half in (0, 1):
        plane_copy(half, 0).start()
    own_core.start()
    load.wait()
    store = pltpu.make_async_copy(stage, out.at[me.at() + (me.core,)], store_sem)
    store.start()
    store.wait()
    for j in range(me.bits):
        for half in (0, 1):
            plane_copy(half, j).wait_recv()
        if j + 1 < me.bits:
            for half in (0, 1):
                plane_copy(half, j + 1).start()
        for half in (0, 1):
            core_copy(half, j).start()
    own_core.wait()
    for j in range(me.bits):
        for half in (0, 1):
            plane_copy(half, j).wait_send()
            core_copy(half, j).wait()


def gather_pair(nf, nc, pair):
    _, bits = plane_shape(nc)
    out = pl.pallas_call(
        functools.partial(gather_pair_kernel, nf, nc),
        out_shape=jax.ShapeDtypeStruct((2,) * (bits + 1) + pair.shape, pair.dtype),
        in_specs=[HBM_SPEC],
        out_specs=HBM_SPEC,
        scratch_shapes=[pltpu.VMEM(pair.shape, pair.dtype)]
        + [DMA((2, bits))] * 2
        + [DMA((2, bits + 1))] * 2
        + [DMA, DMA],
        compiler_params=pltpu.CompilerParams(collective_id=1, has_side_effects=True),
        name="gather_pair",
    )(pair)
    return out.reshape(nc * pair.shape[0], pair.shape[1])


def scatter_pair_kernel(nf, nc, grads, out, held, core_in, *refs):
    _, bits = plane_shape(nc)
    ins = refs[: 2 * bits]
    cs, cr, ps, pr, load_sem = refs[2 * bits :]
    me = Place(nc, nf)
    every = tuple(slice(None) for _ in range(bits))
    load = pltpu.make_async_copy(grads.at[every + (me.core,)], held, load_sem)
    load.start()
    me.barrier(line=False)
    core_copy = remote(
        grads.at[every + (1 - me.core,)], core_in, cs, cr, ctx=me.partner
    )
    core_copy.start()
    load.wait()
    core_copy.wait_recv()
    rows, width = held.shape[-2:]
    halves = [pl.ds(0, width // 2), pl.ds(width // 2, width // 2)]

    def add(index, source, source_index, cols):
        held[index + (slice(None), cols)] = (
            held[index + (slice(None), cols)].astype(jnp.float32)
            + source[source_index].astype(jnp.float32)
        ).astype(held.dtype)

    def every_chip(free):
        todo = [()]
        for j in reversed(range(bits)):
            todo = [t + (v,) for t in todo for v in ((0, 1) if j in free else (me.bit[j],))]
        return todo

    def plane_copy(half, j):
        order = me.orders[half]
        src = held.at[me.at(order[j + 1 :], other=order[j]) + (slice(None), halves[half])]
        return remote(
            src, ins[2 * j + half], ps.at[half, j], pr.at[half, j], ctx=me.across[order[j]]
        )

    for index in every_chip(range(bits)):
        add(index, core_in, index, pl.ds(0, width))
    for half in (0, 1):
        plane_copy(half, 0).start()
    for j in range(bits):
        for half in (0, 1):
            order = me.orders[half]
            plane_copy(half, j).wait_recv()
            free = order[j + 1 :]
            todo = [()]
            for b in reversed(range(bits)):
                if b in free:
                    todo = [t + (v,) for t in todo for v in (0, 1)]
            for chip, part in zip(every_chip(free), todo):
                add(chip, ins[2 * j + half], part, halves[half])
            if j + 1 < bits:
                plane_copy(half, j + 1).start()
    out[...] = held[me.at()]
    core_copy.wait_send()
    for j in range(bits):
        for half in (0, 1):
            plane_copy(half, j).wait_send()


def scatter_pair(nf, nc, grads):
    chips, bits = plane_shape(nc)
    rows, width = grads.shape[0] // nc, grads.shape[1]
    view = grads.reshape((2,) * (bits + 1) + (rows, width))
    return pl.pallas_call(
        functools.partial(scatter_pair_kernel, nf, nc),
        out_shape=jax.ShapeDtypeStruct((rows, width), grads.dtype),
        in_specs=[HBM_SPEC],
        out_specs=pl.BlockSpec(memory_space=pltpu.VMEM),
        scratch_shapes=[pltpu.VMEM((2,) * bits + (rows, width), grads.dtype)] * 2
        + [
            pltpu.VMEM((2,) * (bits - 1 - j) + (rows, width // 2), grads.dtype)
            for j in range(bits)
            for _ in (0, 1)
        ]
        + [DMA, DMA]
        + [DMA((2, bits))] * 2
        + [DMA],
        compiler_params=pltpu.CompilerParams(collective_id=2, has_side_effects=True),
        name="scatter_pair",
    )(view)


def reduce_kernel(nf, nc, count, *refs):
    _, bits = plane_shape(nc)
    parts, small = refs[:count], refs[count]
    outs, small_out = refs[count + 1 : 2 * count + 1], refs[2 * count + 1]
    rest = list(refs[2 * count + 2 :])
    held = [rest.pop(0) for _ in range(count)]
    ins = [[[rest.pop(0) for _ in (0, 1)] for _ in range(bits)] for _ in range(count)]
    line_in = [rest.pop(0) for _ in range(count)]
    final = [rest.pop(0) for _ in range(count)]
    small_sum, small_in, small_line = rest.pop(0), rest.pop(0), rest.pop(0)
    (load_sem, ps, pr, ls, lr, gs, gr, cs, cr, own_sem, ss, sr, sls, slr) = rest
    me = Place(nc, nf)
    z = me.z
    loads = [pltpu.make_async_copy(parts[i], held[i], load_sem.at[i]) for i in range(count)]
    for load in loads:
        load.start()
    me.barrier()

    def target(k):
        return (z + k) % nf

    def plane_copy(i, k, half, j):
        order = me.orders[half]
        ref = parts[i] if j == 0 else held[i]
        src = ref.at[
            (target(k),)
            + me.at(order[j + 1 :], other=order[j])
            + (slice(None), column_half(ref, half))
        ]
        return remote(
            src,
            ins[i][j][half].at[k],
            ps.at[half, i, k, j],
            pr.at[half, i, k, j],
            ctx=me.across[order[j]],
        )

    def chips_of(free):
        places, local = [()], [()]
        for b in reversed(range(bits)):
            if b in free:
                places = [t + (v,) for t in places for v in (0, 1)]
                local = [t + (v,) for t in local for v in (0, 1)]
            else:
                places = [t + (me.bit[b],) for t in places]
        return list(zip(places, local))

    def add(i, k, half, j):
        free = me.orders[half][j + 1 :]
        rows, width = held[i].shape[-2], held[i].shape[-1] // 2
        step = min(rows, 32)
        cols = pl.ds(half * width, width)
        for place, local in chips_of(free):

            def body(t, carry, place=place, local=local):
                at = pl.ds(pl.multiple_of(t * step, step), step)
                where = (target(k),) + place + (at, cols)
                total = held[i][where].astype(jnp.float32) + ins[i][j][half][
                    (k,) + local + (at,)
                ].astype(jnp.float32)
                held[i][where] = total.astype(held[i].dtype)
                return carry

            lax.fori_loop(0, rows // step, body, 0)

    def line_copy(i, k):
        return remote(
            held[i].at[(target(k),) + me.at()],
            line_in[i].at[k],
            ls.at[i, k],
            lr.at[i, k],
            fsdp=target(k),
        )

    def stage(i, k, j):
        if j > 0:
            for half in (0, 1):
                plane_copy(i, k, half, j - 1).wait_recv()
                add(i, k, half, j - 1)
        if j < bits:
            for half in (0, 1):
                plane_copy(i, k, half, j).start()
        elif k != 0:
            line_copy(i, k).start()

    def own_copy(i):
        return pltpu.make_async_copy(final[i], outs[i].at[(me.core,) + me.at()], own_sem.at[i])

    def gather_copy(i, half, j):
        order = me.orders[half]
        cols = column_half(final[i], half)
        dst = outs[i].at[(me.core,) + me.at(order[:j]) + (slice(None), cols)]
        src = final[i].at[:, cols] if j == 0 else dst
        return remote(
            src, dst, gs.at[half, i, j], gr.at[half, i, j], ctx=me.across[order[j]]
        )

    def core_copy(i):
        ref = outs[i].at[me.core]
        return remote(ref, ref, cs.at[i], cr.at[i], ctx=me.partner)

    def total(i):
        for k in range(1, nf):
            line_copy(i, k).wait_recv()
        rows = final[i].shape[0]
        step = min(rows, 32)

        def body(t, carry):
            at = pl.ds(pl.multiple_of(t * step, step), step)
            value = held[i][(z,) + me.at() + (at,)].astype(jnp.float32)
            for k in range(1, nf):
                value = value + line_in[i][k, at].astype(jnp.float32)
            final[i][at] = value.astype(final[i].dtype)
            return carry

        lax.fori_loop(0, rows // step, body, 0)
        own_copy(i).start()

    def gather_stage(i, j):
        if j == 0:
            own_copy(i).wait()
        else:
            for half in (0, 1):
                gather_copy(i, half, j - 1).wait_recv()
        if j < bits:
            for half in (0, 1):
                gather_copy(i, half, j).start()
        else:
            core_copy(i).start()

    across = [me.partner] + me.across

    def small_copy(s):
        return remote(small_sum.at[s], small_in.at[s], ss.at[s], sr.at[s], ctx=across[s])

    def small_line_copy(k):
        return remote(
            small_sum.at[bits + 1], small_line.at[z], sls.at[k], slr.at[k], fsdp=target(k)
        )

    def small_stage(s):
        if s > 0:
            small_copy(s - 1).wait_recv()
            small_sum[s] = small_sum[s - 1] + small_in[s - 1]
        if s <= bits:
            small_copy(s).start()
        else:
            for k in range(1, nf):
                small_line_copy(k).start()
            small_line[z] = small_sum[s]

    small_sum[0] = small[...]
    jobs = []
    for i in range(count):
        for k in list(range(1, nf)) + [0]:
            job = [functools.partial(stage, i, k, j) for j in range(bits + 1)]
            if k == 0:
                job += [functools.partial(total, i)]
                job += [functools.partial(gather_stage, i, j) for j in range(bits + 1)]
                job += [core_copy(i).wait_recv]
            jobs.append(job)
    small_job = [functools.partial(small_stage, s) for s in range(bits + 2)]
    for load in loads:
        load.wait()
    run_ticks([small_job] + jobs)
    for k in range(1, nf):
        small_line_copy(k).wait_recv()
    value = small_line[0]
    for k in range(1, nf):
        value = value + small_line[k]
    small_out[...] = value
    for s in range(bits + 1):
        small_copy(s).wait_send()
    for k in range(1, nf):
        small_line_copy(k).wait_send()
    for i in range(count):
        for k in range(nf):
            for half in (0, 1):
                for j in range(bits):
                    plane_copy(i, k, half, j).wait_send()
            if k:
                line_copy(i, k).wait_send()
        for half in (0, 1):
            for j in range(bits):
                gather_copy(i, half, j).wait_send()
        core_copy(i).wait_send()


def reduce_gradients(nf, nc, parts, small):
    _, bits = plane_shape(nc)
    count = len(parts)
    views = [
        p.reshape((nf,) + (2,) * bits + (p.shape[0] // (nf * 2**bits), p.shape[1])) for p in parts
    ]
    pieces = [v.shape[-2:] for v in views]
    vmem = pl.BlockSpec(memory_space=pltpu.VMEM)
    outs = pl.pallas_call(
        functools.partial(reduce_kernel, nf, nc, count),
        out_shape=[
            jax.ShapeDtypeStruct((2,) * (bits + 1) + piece, jnp.bfloat16) for piece in pieces
        ]
        + [jax.ShapeDtypeStruct(small.shape, jnp.float32)],
        in_specs=[HBM_SPEC] * count + [vmem],
        out_specs=[HBM_SPEC] * count + [vmem],
        scratch_shapes=[pltpu.VMEM(v.shape, jnp.bfloat16) for v in views]
        + [
            pltpu.VMEM((nf,) + (2,) * (bits - 1 - j) + (rows, width // 2), jnp.bfloat16)
            for rows, width in pieces
            for j in range(bits)
            for _ in (0, 1)
        ]
        + [pltpu.VMEM((nf,) + piece, jnp.bfloat16) for piece in pieces]
        + [pltpu.VMEM(piece, jnp.bfloat16) for piece in pieces]
        + [
            pltpu.VMEM((bits + 2,) + small.shape, jnp.float32),
            pltpu.VMEM((bits + 1,) + small.shape, jnp.float32),
            pltpu.VMEM((nf,) + small.shape, jnp.float32),
        ]
        + [DMA((count,))]
        + [DMA((2, count, nf, bits))] * 2
        + [DMA((count, nf))] * 2
        + [DMA((2, count, bits))] * 2
        + [DMA((count,))] * 2
        + [DMA((count,))]
        + [DMA((bits + 1,))] * 2
        + [DMA((nf,))] * 2,
        compiler_params=pltpu.CompilerParams(collective_id=3, has_side_effects=True),
        name="reduce_gradients",
    )(*views, small)
    return [
        o.reshape(p.shape[0] // nf * 2, p.shape[1]) for o, p in zip(outs, parts)
    ], outs[count]


def per_device(
    tokens,
    cotangent,
    doc_starts,
    deal_order,
    query_key_value_weight,
    w_out,
    w_gate,
    w_up,
    w_down,
    gain_attn,
    gain_ffn,
    gain_qk,
):
    ctx_count = lax.axis_size("ctx")
    fsdp_count = lax.axis_size("fsdp")
    ctx_rank = lax.axis_index("ctx")
    model_shard = gain_attn.shape[0]
    qk_shard = gain_qk.shape[1]
    gains = pack_rows([gain_attn, gain_ffn, gain_qk], 8)
    (qkv_full, out_full, gate_full, up_full, down_full), gains = gather_weights(
        fsdp_count, ctx_count, [query_key_value_weight, w_out, w_gate, w_up, w_down], gains
    )
    gains = gains.reshape(fsdp_count, -1)
    attn_gain = gains[:, :model_shard].reshape(-1)
    ffn_gain = gains[:, model_shard : 2 * model_shard].reshape(-1)
    qk_gain = gains[:, 2 * model_shard : 2 * model_shard + 2 * qk_shard]
    qk_gain = jnp.swapaxes(qk_gain.reshape(fsdp_count, 2, qk_shard), 0, 1).reshape(2, -1)
    query_gain, key_gain = qk_gain[0], qk_gain[1]
    pack_in = tokens[0].astype(jnp.float32)
    token_rows = pack_in.shape[0]
    block_len = token_rows // 2
    full_len = token_rows * ctx_count
    key_value_width = KEY_VALUE_HEADS * HEAD_SIZE
    group_width = QUERY_HEADS // KEY_VALUE_HEADS
    inv_root = HEAD_SIZE ** (-0.5)
    start_row = doc_starts[0]
    stored = jnp.arange(full_len, dtype=jnp.int32)
    key_place = (
        jnp.repeat(deal_order, block_len, total_repeat_length=full_len) * block_len
        + stored % block_len
    )
    key_begin = jnp.max(
        jnp.where(start_row[None, :] <= key_place[:, None], start_row[None, :], 0), axis=1
    )
    query_place = lax.dynamic_slice_in_dim(key_place, ctx_rank * token_rows, token_rows)
    query_begin = lax.dynamic_slice_in_dim(key_begin, ctx_rank * token_rows, token_rows)
    cosines, sine_vals = rotary_tables(query_place, query_begin)
    normed, attn_inverse = norm_forward(pack_in, attn_gain)
    normed_low = normed.astype(jnp.bfloat16)
    projected_rows = jnp.dot(normed_low, qkv_full, preferred_element_type=jnp.float32)
    query_raw = projected_rows[:, : QUERY_HEADS * HEAD_SIZE].reshape(
        token_rows, QUERY_HEADS, HEAD_SIZE
    )
    unrotated_key = projected_rows[
        :, QUERY_HEADS * HEAD_SIZE : (QUERY_HEADS + KEY_VALUE_HEADS) * HEAD_SIZE
    ].reshape(token_rows, KEY_VALUE_HEADS, HEAD_SIZE)
    unprojected_value = projected_rows[:, (QUERY_HEADS + KEY_VALUE_HEADS) * HEAD_SIZE :]
    query_normed, query_inverse = norm_forward(query_raw, query_gain)
    key_normed, key_inverse = norm_forward(unrotated_key, key_gain)
    query_heads_rows = rotate(query_normed, cosines, sine_vals).astype(jnp.bfloat16)
    key_local = rotate(key_normed, cosines, sine_vals).astype(jnp.bfloat16)
    local_pair = jnp.concatenate(
        [key_local.reshape(token_rows, key_value_width), unprojected_value.astype(jnp.bfloat16)],
        axis=1,
    )
    every_pair = gather_pair(fsdp_count, ctx_count, local_pair)
    key_block_index = math.gcd(full_len, 512)
    block_total = full_len // key_block_index
    key_block_list = (
        every_pair[:, :key_value_width].reshape(
            block_total, key_block_index, KEY_VALUE_HEADS, HEAD_SIZE
        ),
        key_place.reshape(block_total, key_block_index),
        key_begin.reshape(block_total, key_block_index),
        every_pair[:, key_value_width:].reshape(
            block_total, key_block_index, KEY_VALUE_HEADS, HEAD_SIZE
        ),
    )
    grouped_heads = query_heads_rows.reshape(token_rows, KEY_VALUE_HEADS, group_width, HEAD_SIZE)

    def block_scores(key_tile, place_tile, begin_tile):
        raw_scores = (
            jnp.einsum(
                "qkgd,tkd->kgqt", grouped_heads, key_tile, preferred_element_type=jnp.float32
            )
            * inv_root
        )
        allowed = (query_begin[:, None] == begin_tile[None, :]) & (
            place_tile[None, :] <= query_place[:, None]
        )
        return jnp.where(allowed[None, None], raw_scores, -1e30)

    def stats_step(carry, tiles):
        row_max, row_sum = carry
        scores = block_scores(tiles[0], tiles[1], tiles[2])
        new_max = jnp.maximum(row_max, jnp.max(scores, axis=-1))
        row_sum = row_sum * jnp.exp(row_max - new_max) + jnp.sum(
            jnp.exp(scores - new_max[..., None]), axis=-1
        )
        return ((new_max, row_sum), None)

    initial_maximum = jnp.full((KEY_VALUE_HEADS, group_width, token_rows), -1e30, jnp.float32)
    initial_sum = jnp.zeros((KEY_VALUE_HEADS, group_width, token_rows), jnp.float32)
    (row_max, row_sum), unused = lax.scan(
        stats_step, (initial_maximum, initial_sum), key_block_list
    )

    def block_probs(tiles):
        scores = block_scores(tiles[0], tiles[1], tiles[2])
        return jnp.exp(scores - row_max[..., None]) / row_sum[..., None]

    def output_update(running, tiles):
        soft_probs = block_probs(tiles).astype(jnp.bfloat16)
        return (
            running
            + jnp.einsum(
                "kgqt,tkd->qkgd", soft_probs, tiles[3], preferred_element_type=jnp.float32
            ),
            None,
        )

    attended_sum, unused = lax.scan(
        output_update,
        jnp.zeros((token_rows, KEY_VALUE_HEADS, group_width, HEAD_SIZE), jnp.float32),
        key_block_list,
    )
    attended = attended_sum.reshape(token_rows, QUERY_HEADS * HEAD_SIZE).astype(jnp.bfloat16)
    hidden_in = pack_in + jnp.dot(attended, out_full, preferred_element_type=jnp.float32)
    normed_ffn, ffn_inverse = norm_forward(hidden_in, ffn_gain)
    normed_ffn_low = normed_ffn.astype(jnp.bfloat16)
    gate_act = jnp.dot(normed_ffn_low, gate_full, preferred_element_type=jnp.float32)
    upward = jnp.dot(normed_ffn_low, up_full, preferred_element_type=jnp.float32)
    sigmoid_gate = jax.nn.sigmoid(gate_act)
    hidden = (gate_act * sigmoid_gate * upward).astype(jnp.bfloat16)
    mixed_out = (hidden_in + jnp.dot(hidden, down_full, preferred_element_type=jnp.float32)).astype(
        jnp.bfloat16
    )
    grad_mixed = cotangent[0]
    grad_hidden = times_transposed(grad_mixed, down_full)
    grad_gate = (
        grad_hidden * upward * sigmoid_gate * (1.0 + gate_act * (1.0 - sigmoid_gate))
    ).astype(jnp.bfloat16)
    grad_up = (grad_hidden * gate_act * sigmoid_gate).astype(jnp.bfloat16)
    grad_normed_ffn = times_transposed(grad_gate, gate_full) + times_transposed(grad_up, up_full)
    grad_resid_part, ffn_gain_part = norm_backward(
        hidden_in, ffn_inverse, ffn_gain, grad_normed_ffn
    )
    grad_resid = grad_mixed.astype(jnp.float32) + grad_resid_part
    grad_branch = grad_resid.astype(jnp.bfloat16)
    attended_gradient = times_transposed(grad_branch, out_full).astype(jnp.bfloat16)
    grouped_gradient = attended_gradient.reshape(
        token_rows, KEY_VALUE_HEADS, group_width, HEAD_SIZE
    )

    def delta_update(running, tiles):
        soft_probs = block_probs(tiles)
        grad_probs = jnp.einsum(
            "qkgd,tkd->kgqt", grouped_gradient, tiles[3], preferred_element_type=jnp.float32
        )
        return (running + jnp.sum(soft_probs * grad_probs, axis=-1), None)

    row_delta, unused = lax.scan(
        delta_update,
        jnp.zeros((KEY_VALUE_HEADS, group_width, token_rows), jnp.float32),
        key_block_list,
    )

    def gradient_update(running, tiles):
        soft_probs = block_probs(tiles)
        grad_probs = jnp.einsum(
            "qkgd,tkd->kgqt", grouped_gradient, tiles[3], preferred_element_type=jnp.float32
        )
        grad_scores = (soft_probs * (grad_probs - row_delta[..., None])).astype(jnp.bfloat16)
        running = running + jnp.einsum(
            "kgqt,tkd->qkgd", grad_scores, tiles[0], preferred_element_type=jnp.float32
        )
        grad_keys = (
            jnp.einsum(
                "kgqt,qkgd->tkd", grad_scores, grouped_heads, preferred_element_type=jnp.float32
            )
            * inv_root
        )
        grad_values = jnp.einsum(
            "kgqt,qkgd->tkd",
            soft_probs.astype(jnp.bfloat16),
            grouped_gradient,
            preferred_element_type=jnp.float32,
        )
        return (
            running,
            jnp.concatenate(
                [
                    grad_keys.reshape(key_block_index, key_value_width),
                    grad_values.reshape(key_block_index, key_value_width),
                ],
                axis=1,
            ),
        )

    query_running, pair_grads = lax.scan(
        gradient_update,
        jnp.zeros((token_rows, KEY_VALUE_HEADS, group_width, HEAD_SIZE), jnp.float32),
        key_block_list,
    )
    grad_query_rot = query_running.reshape(token_rows, QUERY_HEADS, HEAD_SIZE) * inv_root
    local_gradients = scatter_pair(
        fsdp_count, ctx_count, pair_grads.reshape(full_len, 2 * key_value_width).astype(jnp.bfloat16)
    ).astype(jnp.float32)
    rotated_key_gradient = local_gradients[:, :key_value_width].reshape(
        token_rows, KEY_VALUE_HEADS, HEAD_SIZE
    )
    grad_value = local_gradients[:, key_value_width:]
    grad_query, query_gain_part = norm_backward(
        query_raw, query_inverse, query_gain, rotate_back(grad_query_rot, cosines, sine_vals)
    )
    grad_key, key_gain_part = norm_backward(
        unrotated_key, key_inverse, key_gain, rotate_back(rotated_key_gradient, cosines, sine_vals)
    )
    grad_projected = jnp.concatenate(
        [
            grad_query.reshape(token_rows, QUERY_HEADS * HEAD_SIZE),
            grad_key.reshape(token_rows, key_value_width),
            grad_value,
        ],
        axis=1,
    ).astype(jnp.bfloat16)
    grad_normed = times_transposed(grad_projected, qkv_full)
    grad_input_part, attn_gain_part = norm_backward(pack_in, attn_inverse, attn_gain, grad_normed)
    tokens_grad = grad_resid + grad_input_part

    core = ctx_rank % 2
    swap = [(i, i + 1 - 2 * (i % 2)) for i in range(ctx_count)]

    def both(values):
        return jnp.concatenate([values, lax.ppermute(values, "ctx", swap)], axis=0)

    def core_part(values, which):
        view = values.reshape(token_rows, fsdp_count, 2, -1)
        return lax.dynamic_index_in_dim(view, which, 2, keepdims=False).reshape(token_rows, -1)

    def both_part(values):
        mine = core_part(values, core)
        other = lax.ppermute(core_part(values, 1 - core), "ctx", swap)
        return jnp.concatenate([mine, other], axis=0)

    ffn_rows = both_part(normed_ffn_low)
    parts = [
        transposed_times(left, right).astype(jnp.bfloat16)
        for left, right in (
            (both_part(hidden), both(grad_mixed)),
            (ffn_rows, both(grad_gate)),
            (ffn_rows, both(grad_up)),
            (both_part(attended), both(grad_branch)),
            (both_part(normed_low), both(grad_projected)),
        )
    ]
    gain_sums = pack_rows(
        [
            jnp.sum(attn_gain_part, axis=0),
            jnp.sum(ffn_gain_part, axis=0),
            jnp.sum(query_gain_part, axis=(0, 1)),
            jnp.sum(key_gain_part, axis=(0, 1)),
        ],
        8,
    )
    (down_grad, gate_grad, up_grad, out_grad, qkv_grad), gain_sums = reduce_gradients(
        fsdp_count, ctx_count, parts, gain_sums
    )
    gain_sums = gain_sums.reshape(-1)
    model = model_shard * fsdp_count
    rank = lax.axis_index("fsdp")
    attn_gain_grad = lax.dynamic_slice_in_dim(gain_sums, rank * model_shard, model_shard)
    ffn_gain_grad = lax.dynamic_slice_in_dim(gain_sums, model + rank * model_shard, model_shard)
    qk_gain_grad = lax.dynamic_slice_in_dim(
        gain_sums[2 * model : 2 * model + 2 * HEAD_SIZE].reshape(2, HEAD_SIZE),
        rank * qk_shard,
        qk_shard,
        axis=1,
    )
    return (
        mixed_out[None],
        tokens_grad[None],
        qkv_grad.astype(jnp.float32),
        out_grad.astype(jnp.float32),
        gate_grad.astype(jnp.float32),
        up_grad.astype(jnp.float32),
        down_grad.astype(jnp.float32),
        attn_gain_grad,
        ffn_gain_grad,
        qk_gain_grad,
    )


def pack_rows(arrays, multiple):
    flat = jnp.concatenate([a.astype(jnp.float32).reshape(-1) for a in arrays])
    size = multiple * 128
    return jnp.pad(flat, (0, -flat.shape[0] % size)).reshape(-1, 128)


def solution(mesh):
    return jax.shard_map(
        per_device,
        mesh=mesh,
        in_specs=(
            P("fsdp", "ctx", None),
            P("fsdp", "ctx", None),
            P("fsdp", None),
            P(),
            P("fsdp", None),
            P("fsdp", None),
            P("fsdp", None),
            P("fsdp", None),
            P("fsdp", None),
            P("fsdp"),
            P("fsdp"),
            P(None, "fsdp"),
        ),
        out_specs=(
            P("fsdp", "ctx", None),
            P("fsdp", "ctx", None),
            P("fsdp", None),
            P("fsdp", None),
            P("fsdp", None),
            P("fsdp", None),
            P("fsdp", None),
            P("fsdp"),
            P("fsdp"),
            P(None, "fsdp"),
        ),
        check_vma=False,
    )
```

```python
import functools

import jax
import jax.numpy as jnp
from jax import lax
from jax.experimental import pallas as pl
from jax.experimental.pallas import tpu as pltpu
from jax.sharding import PartitionSpec as P

QUERY_HEADS = 16
KEY_VALUE_HEADS = 4
HEAD_SIZE = 64


EPSILON = 1e-06
THETA = 10000.0

MESH = pl.DeviceIdType.MESH
DMA = pltpu.SemaphoreType.DMA
HBM_SPEC = pl.BlockSpec(memory_space=pl.ANY)
SPACING = 2


def plane_shape(ctx_count):
    chips = ctx_count // 2
    bits = chips.bit_length() - 1
    assert 2**bits == chips and ctx_count == 2 * chips
    return chips, bits


class Place:
    def __init__(self, ctx_count, fsdp_count):
        self.chips, self.bits = plane_shape(ctx_count)
        self.fsdp_count = fsdp_count
        self.ctx = lax.axis_index("ctx")
        self.z = lax.axis_index("fsdp")
        self.core = self.ctx % 2
        chip = self.ctx // 2
        self.bit = [(chip // 2**j) % 2 for j in range(self.bits)]
        self.across = [self.ctx + (1 - 2 * self.bit[j]) * 2 * 2**j for j in range(self.bits)]
        self.partner = self.ctx + 1 - 2 * self.core
        self.orders = (list(range(self.bits)), list(reversed(range(self.bits))))

    def at(self, free=(), other=None):
        return tuple(
            slice(None) if j in free else (1 - self.bit[j] if j == other else self.bit[j])
            for j in reversed(range(self.bits))
        )

    def barrier(self, plane=True, line=True, near=False):
        sem = pltpu.get_barrier_semaphore()
        count = 0
        if plane:
            for p in self.across + [self.partner]:
                pl.semaphore_signal(sem, inc=1, device_id={"ctx": p}, device_id_type=MESH)
                count += 1
        if line:
            for k in range(1, self.fsdp_count):
                pl.semaphore_signal(
                    sem,
                    inc=1,
                    device_id={"fsdp": (self.z + k) % self.fsdp_count},
                    device_id_type=MESH,
                )
                count += 1
        pl.semaphore_wait(sem, count)


def remote(src, dst, send, recv, **where):
    return pltpu.make_async_remote_copy(
        src, dst, send, recv, device_id=where, device_id_type=MESH
    )


def run_ticks(jobs, spacing=SPACING):
    depth = max(len(job) for job in jobs)
    for tick in range(len(jobs) + spacing * (depth - 1)):
        for j in reversed(range(depth)):
            t = tick - spacing * j
            if 0 <= t < len(jobs) and j < len(jobs[t]):
                jobs[t][j]()


def column_half(ref, half):
    n = ref.shape[-1] // 2
    return pl.ds(half * n, n)


def gather_kernel(nf, nc, count, *refs):
    shards, small = refs[:count], refs[count]
    outs, small_out = refs[count + 1 : 2 * count + 1], refs[2 * count + 1]
    stages = refs[2 * count + 2 : 3 * count + 3]
    up_s, up_r, down_s, down_r, ps, pr, cs, cr, ss, sr, load_sem, store_sem = refs[3 * count + 3 :]
    me = Place(nc, nf)
    z = me.z
    loads = [
        pltpu.make_async_copy(src, dst, load_sem.at[i])
        for i, (src, dst) in enumerate(zip(list(shards) + [small], stages))
    ]
    stores = [
        pltpu.make_async_copy(stages[i], dst.at[z], store_sem.at[i])
        for i, dst in enumerate(list(outs) + [small_out])
    ]
    for load in loads:
        load.start()
    me.barrier()

    def source(k):
        pairs = jnp.minimum(z, nf - 1 - z)
        near = (k + 1) // 2
        near_source = z - near if k % 2 == 1 else z + near
        far = k - pairs
        far_source = jnp.where(2 * z < nf - 1, z + far, z - far)
        return jnp.where(k <= 2 * pairs, near_source, far_source)

    sources = [None] + [source(k) for k in range(1, nf)]

    def line_copy(i, src_z, src, up):
        to = z + 1 if up else z - 1
        sems = (up_s, up_r) if up else (down_s, down_r)
        return remote(
            src,
            outs[i].at[(src_z, me.core) + me.at()],
            sems[0].at[i, src_z],
            sems[1].at[i, src_z],
            fsdp=to,
        )

    def line_start(i, src_z, src, up, condition):
        @pl.when(condition)
        def _():
            line_copy(i, src_z, src, up).start()

    def small_copy(k):
        return remote(small, small_out.at[z], ss.at[k], sr.at[k], fsdp=(z + k) % nf)

    for k in range(1, nf):
        small_copy(k).start()
    for i in range(count):
        mine = shards[i].at[(me.core,) + me.at()]
        line_start(i, z, mine, True, z + 1 < nf)
        line_start(i, z, mine, False, z > 0)

    def line_stage(i, k):
        src_z = sources[k]
        here = outs[i].at[(src_z, me.core) + me.at()]
        below = src_z < z

        @pl.when(below)
        def _():
            line_copy(i, src_z, here, True).wait_recv()

        @pl.when(jnp.logical_not(below))
        def _():
            line_copy(i, src_z, here, False).wait_recv()

        line_start(i, src_z, here, True, jnp.logical_and(below, z + 1 < nf))
        line_start(i, src_z, here, False, jnp.logical_and(src_z > z, z > 0))

    def plane_copy(i, k, half, j):
        order = me.orders[half]
        ref = outs[i].at[
            (sources[k], me.core) + me.at(order[:j]) + (slice(None), column_half(outs[i], half))
        ]
        return remote(
            ref, ref, ps.at[half, i, k, j], pr.at[half, i, k, j], ctx=me.across[order[j]]
        )

    def core_copy(i, k):
        ref = outs[i].at[sources[k], me.core]
        return remote(ref, ref, cs.at[i, k], cr.at[i, k], ctx=me.partner)

    def plane_stage(i, k, j):
        if j == 0:
            line_stage(i, k)
        else:
            for half in (0, 1):
                plane_copy(i, k, half, j - 1).wait_recv()
        if j < me.bits:
            for half in (0, 1):
                plane_copy(i, k, half, j).start()
        else:
            core_copy(i, k).start()

    order = [(i, k) for i in range(count) for k in range(1, nf)]
    jobs = [
        [functools.partial(plane_stage, i, k, j) for j in range(me.bits + 1)]
        + [core_copy(i, k).wait_recv]
        for i, k in order
    ]
    for load, store in zip(loads, stores):
        load.wait()
        store.start()
    run_ticks(jobs)
    for k in range(1, nf):
        small_copy(k).wait_recv()
        small_copy(k).wait_send()
    for i in range(count):
        @pl.when(z + 1 < nf)
        def _():
            line_copy(i, z, shards[i].at[(me.core,) + me.at()], True).wait_send()

        @pl.when(z > 0)
        def _():
            line_copy(i, z, shards[i].at[(me.core,) + me.at()], False).wait_send()

    for i, k in order:
        src_z = sources[k]
        here = outs[i].at[(src_z, me.core) + me.at()]

        @pl.when(jnp.logical_and(src_z < z, z + 1 < nf))
        def _():
            line_copy(i, src_z, here, True).wait_send()

        @pl.when(jnp.logical_and(src_z > z, z > 0))
        def _():
            line_copy(i, src_z, here, False).wait_send()

        for half in (0, 1):
            for j in range(me.bits):
                plane_copy(i, k, half, j).wait_send()
        core_copy(i, k).wait_send()
    for store in stores:
        store.wait()


def gather_weights(nf, nc, shards, small):
    _, bits = plane_shape(nc)
    count = len(shards)
    views = [w.reshape((2,) * (1 + bits) + (w.shape[0] // nc, w.shape[1])) for w in shards]
    arrays = views + [small]
    outs = pl.pallas_call(
        functools.partial(gather_kernel, nf, nc, count),
        out_shape=[jax.ShapeDtypeStruct((nf,) + v.shape, v.dtype) for v in arrays],
        in_specs=[HBM_SPEC] * (count + 1),
        out_specs=[HBM_SPEC] * (count + 1),
        scratch_shapes=[pltpu.VMEM(v.shape, v.dtype) for v in arrays]
        + [DMA((count, nf))] * 4
        + [DMA((2, count, nf, bits))] * 2
        + [DMA((count, nf))] * 2
        + [DMA((nf,))] * 2
        + [DMA((count + 1,))] * 2,
        compiler_params=pltpu.CompilerParams(collective_id=0, has_side_effects=True),
        name="gather_weights",
    )(*arrays)
    return [o.reshape(nf * w.shape[0], w.shape[1]) for o, w in zip(outs, shards)], outs[count]


def gather_pair_kernel(nf, nc, pair, out, stage, ps, pr, cs, cr, load_sem, store_sem):
    me = Place(nc, nf)
    load = pltpu.make_async_copy(pair, stage, load_sem)
    load.start()
    me.barrier(line=False)

    def plane_copy(half, j):
        order = me.orders[half]
        where = (slice(None), column_half(out, half))
        dst = out.at[me.at(order[:j]) + (me.core,) + where]
        src = pair.at[where] if j == 0 else dst
        return remote(src, dst, ps.at[half, j], pr.at[half, j], ctx=me.across[order[j]])

    own_core = remote(pair, out.at[me.at() + (me.core,)], cs.at[0, 0], cr.at[0, 0], ctx=me.partner)

    def core_copy(half, j):
        order = me.orders[half]
        ref = out.at[
            me.at(order[:j], other=order[j]) + (me.core, slice(None), column_half(out, half))
        ]
        return remote(ref, ref, cs.at[half, j + 1], cr.at[half, j + 1], ctx=me.partner)

    for half in (0, 1):
        plane_copy(half, 0).start()
    own_core.start()
    load.wait()
    store = pltpu.make_async_copy(stage, out.at[me.at() + (me.core,)], store_sem)
    store.start()
    store.wait()
    for j in range(me.bits):
        for half in (0, 1):
            plane_copy(half, j).wait_recv()
        if j + 1 < me.bits:
            for half in (0, 1):
                plane_copy(half, j + 1).start()
        for half in (0, 1):
            core_copy(half, j).start()
    own_core.wait()
    for j in range(me.bits):
        for half in (0, 1):
            plane_copy(half, j).wait_send()
            core_copy(half, j).wait()


def gather_pair(nf, nc, pair):
    _, bits = plane_shape(nc)
    out = pl.pallas_call(
        functools.partial(gather_pair_kernel, nf, nc),
        out_shape=jax.ShapeDtypeStruct((2,) * (bits + 1) + pair.shape, pair.dtype),
        in_specs=[HBM_SPEC],
        out_specs=HBM_SPEC,
        scratch_shapes=[pltpu.VMEM(pair.shape, pair.dtype)]
        + [DMA((2, bits))] * 2
        + [DMA((2, bits + 1))] * 2
        + [DMA, DMA],
        compiler_params=pltpu.CompilerParams(collective_id=1, has_side_effects=True),
        name="gather_pair",
    )(pair)
    return out.reshape(nc * pair.shape[0], pair.shape[1])


def scatter_pair_kernel(nf, nc, grads, out, held, core_in, *refs):
    _, bits = plane_shape(nc)
    ins = refs[: 2 * bits]
    cs, cr, ps, pr, load_sem = refs[2 * bits :]
    me = Place(nc, nf)
    every = tuple(slice(None) for _ in range(bits))
    load = pltpu.make_async_copy(grads.at[every + (me.core,)], held, load_sem)
    load.start()
    me.barrier(line=False)
    core_copy = remote(
        grads.at[every + (1 - me.core,)], core_in, cs, cr, ctx=me.partner
    )
    core_copy.start()
    load.wait()
    core_copy.wait_recv()
    rows, width = held.shape[-2:]
    halves = [pl.ds(0, width // 2), pl.ds(width // 2, width // 2)]

    def add(index, source, source_index, cols):
        held[index + (slice(None), cols)] = (
            held[index + (slice(None), cols)].astype(jnp.float32)
            + source[source_index].astype(jnp.float32)
        ).astype(held.dtype)

    def every_chip(free):
        todo = [()]
        for j in reversed(range(bits)):
            todo = [t + (v,) for t in todo for v in ((0, 1) if j in free else (me.bit[j],))]
        return todo

    def plane_copy(half, j):
        order = me.orders[half]
        src = held.at[me.at(order[j + 1 :], other=order[j]) + (slice(None), halves[half])]
        return remote(
            src, ins[2 * j + half], ps.at[half, j], pr.at[half, j], ctx=me.across[order[j]]
        )

    for index in every_chip(range(bits)):
        add(index, core_in, index, pl.ds(0, width))
    for half in (0, 1):
        plane_copy(half, 0).start()
    for j in range(bits):
        for half in (0, 1):
            order = me.orders[half]
            plane_copy(half, j).wait_recv()
            free = order[j + 1 :]
            todo = [()]
            for b in reversed(range(bits)):
                if b in free:
                    todo = [t + (v,) for t in todo for v in (0, 1)]
            for chip, part in zip(every_chip(free), todo):
                add(chip, ins[2 * j + half], part, halves[half])
            if j + 1 < bits:
                plane_copy(half, j + 1).start()
    out[...] = held[me.at()]
    core_copy.wait_send()
    for j in range(bits):
        for half in (0, 1):
            plane_copy(half, j).wait_send()


def scatter_pair(nf, nc, grads):
    chips, bits = plane_shape(nc)
    rows, width = grads.shape[0] // nc, grads.shape[1]
    view = grads.reshape((2,) * (bits + 1) + (rows, width))
    return pl.pallas_call(
        functools.partial(scatter_pair_kernel, nf, nc),
        out_shape=jax.ShapeDtypeStruct((rows, width), grads.dtype),
        in_specs=[HBM_SPEC],
        out_specs=pl.BlockSpec(memory_space=pltpu.VMEM),
        scratch_shapes=[pltpu.VMEM((2,) * bits + (rows, width), grads.dtype)] * 2
        + [
            pltpu.VMEM((2,) * (bits - 1 - j) + (rows, width // 2), grads.dtype)
            for j in range(bits)
            for _ in (0, 1)
        ]
        + [DMA, DMA]
        + [DMA((2, bits))] * 2
        + [DMA],
        compiler_params=pltpu.CompilerParams(collective_id=2, has_side_effects=True),
        name="scatter_pair",
    )(view)


def reduce_kernel(nf, nc, count, *refs):
    _, bits = plane_shape(nc)
    parts, small = refs[:count], refs[count]
    outs, small_out = refs[count + 1 : 2 * count + 1], refs[2 * count + 1]
    rest = list(refs[2 * count + 2 :])
    held = [rest.pop(0) for _ in range(count)]
    ins = [[[rest.pop(0) for _ in (0, 1)] for _ in range(bits)] for _ in range(count)]
    line_in = [rest.pop(0) for _ in range(count)]
    final = [rest.pop(0) for _ in range(count)]
    small_sum, small_in, small_line = rest.pop(0), rest.pop(0), rest.pop(0)
    (load_sem, ps, pr, ls, lr, gs, gr, cs, cr, own_sem, ss, sr, sls, slr) = rest
    me = Place(nc, nf)
    z = me.z
    loads = [pltpu.make_async_copy(parts[i], held[i], load_sem.at[i]) for i in range(count)]
    for load in loads:
        load.start()
    me.barrier()

    def target(k):
        return (z + k) % nf

    def plane_copy(i, k, half, j):
        order = me.orders[half]
        ref = parts[i] if j == 0 else held[i]
        src = ref.at[
            (target(k),)
            + me.at(order[j + 1 :], other=order[j])
            + (slice(None), column_half(ref, half))
        ]
        return remote(
            src,
            ins[i][j][half].at[k],
            ps.at[half, i, k, j],
            pr.at[half, i, k, j],
            ctx=me.across[order[j]],
        )

    def chips_of(free):
        places, local = [()], [()]
        for b in reversed(range(bits)):
            if b in free:
                places = [t + (v,) for t in places for v in (0, 1)]
                local = [t + (v,) for t in local for v in (0, 1)]
            else:
                places = [t + (me.bit[b],) for t in places]
        return list(zip(places, local))

    def add(i, k, half, j):
        free = me.orders[half][j + 1 :]
        rows, width = held[i].shape[-2], held[i].shape[-1] // 2
        step = min(rows, 32)
        cols = pl.ds(half * width, width)
        for place, local in chips_of(free):

            def body(t, carry, place=place, local=local):
                at = pl.ds(pl.multiple_of(t * step, step), step)
                where = (target(k),) + place + (at, cols)
                total = held[i][where].astype(jnp.float32) + ins[i][j][half][
                    (k,) + local + (at,)
                ].astype(jnp.float32)
                held[i][where] = total.astype(held[i].dtype)
                return carry

            lax.fori_loop(0, rows // step, body, 0)

    def line_copy(i, k):
        return remote(
            held[i].at[(target(k),) + me.at()],
            line_in[i].at[k],
            ls.at[i, k],
            lr.at[i, k],
            fsdp=target(k),
        )

    def stage(i, k, j):
        if j > 0:
            for half in (0, 1):
                plane_copy(i, k, half, j - 1).wait_recv()
                add(i, k, half, j - 1)
        if j < bits:
            for half in (0, 1):
                plane_copy(i, k, half, j).start()
        elif k != 0:
            line_copy(i, k).start()

    def own_copy(i):
        return pltpu.make_async_copy(final[i], outs[i].at[(me.core,) + me.at()], own_sem.at[i])

    def gather_copy(i, half, j):
        order = me.orders[half]
        cols = column_half(final[i], half)
        dst = outs[i].at[(me.core,) + me.at(order[:j]) + (slice(None), cols)]
        src = final[i].at[:, cols] if j == 0 else dst
        return remote(
            src, dst, gs.at[half, i, j], gr.at[half, i, j], ctx=me.across[order[j]]
        )

    def core_copy(i):
        ref = outs[i].at[me.core]
        return remote(ref, ref, cs.at[i], cr.at[i], ctx=me.partner)

    def total(i):
        for k in range(1, nf):
            line_copy(i, k).wait_recv()
        rows = final[i].shape[0]
        step = min(rows, 32)

        def body(t, carry):
            at = pl.ds(pl.multiple_of(t * step, step), step)
            value = held[i][(z,) + me.at() + (at,)].astype(jnp.float32)
            for k in range(1, nf):
                value = value + line_in[i][k, at].astype(jnp.float32)
            final[i][at] = value.astype(final[i].dtype)
            return carry

        lax.fori_loop(0, rows // step, body, 0)
        own_copy(i).start()

    def gather_stage(i, j):
        if j == 0:
            own_copy(i).wait()
        else:
            for half in (0, 1):
                gather_copy(i, half, j - 1).wait_recv()
        if j < bits:
            for half in (0, 1):
                gather_copy(i, half, j).start()
        else:
            core_copy(i).start()

    across = [me.partner] + me.across

    def small_copy(s):
        return remote(small_sum.at[s], small_in.at[s], ss.at[s], sr.at[s], ctx=across[s])

    def small_line_copy(k):
        return remote(
            small_sum.at[bits + 1], small_line.at[z], sls.at[k], slr.at[k], fsdp=target(k)
        )

    def small_stage(s):
        if s > 0:
            small_copy(s - 1).wait_recv()
            small_sum[s] = small_sum[s - 1] + small_in[s - 1]
        if s <= bits:
            small_copy(s).start()
        else:
            for k in range(1, nf):
                small_line_copy(k).start()
            small_line[z] = small_sum[s]

    small_sum[0] = small[...]
    jobs = []
    for i in range(count):
        for k in list(range(1, nf)) + [0]:
            job = [functools.partial(stage, i, k, j) for j in range(bits + 1)]
            if k == 0:
                job += [functools.partial(total, i)]
                job += [functools.partial(gather_stage, i, j) for j in range(bits + 1)]
                job += [core_copy(i).wait_recv]
            jobs.append(job)
    small_job = [functools.partial(small_stage, s) for s in range(bits + 2)]
    for load in loads:
        load.wait()
    run_ticks([small_job] + jobs)
    for k in range(1, nf):
        small_line_copy(k).wait_recv()
    value = small_line[0]
    for k in range(1, nf):
        value = value + small_line[k]
    small_out[...] = value
    for s in range(bits + 1):
        small_copy(s).wait_send()
    for k in range(1, nf):
        small_line_copy(k).wait_send()
    for i in range(count):
        for k in range(nf):
            for half in (0, 1):
                for j in range(bits):
                    plane_copy(i, k, half, j).wait_send()
            if k:
                line_copy(i, k).wait_send()
        for half in (0, 1):
            for j in range(bits):
                gather_copy(i, half, j).wait_send()
        core_copy(i).wait_send()


def reduce_gradients(nf, nc, parts, small):
    _, bits = plane_shape(nc)
    count = len(parts)
    views = [
        p.reshape((nf,) + (2,) * bits + (p.shape[0] // (nf * 2**bits), p.shape[1])) for p in parts
    ]
    pieces = [v.shape[-2:] for v in views]
    vmem = pl.BlockSpec(memory_space=pltpu.VMEM)
    outs = pl.pallas_call(
        functools.partial(reduce_kernel, nf, nc, count),
        out_shape=[
            jax.ShapeDtypeStruct((2,) * (bits + 1) + piece, jnp.bfloat16) for piece in pieces
        ]
        + [jax.ShapeDtypeStruct(small.shape, jnp.float32)],
        in_specs=[HBM_SPEC] * count + [vmem],
        out_specs=[HBM_SPEC] * count + [vmem],
        scratch_shapes=[pltpu.VMEM(v.shape, jnp.bfloat16) for v in views]
        + [
            pltpu.VMEM((nf,) + (2,) * (bits - 1 - j) + (rows, width // 2), jnp.bfloat16)
            for rows, width in pieces
            for j in range(bits)
            for _ in (0, 1)
        ]
        + [pltpu.VMEM((nf,) + piece, jnp.bfloat16) for piece in pieces]
        + [pltpu.VMEM(piece, jnp.bfloat16) for piece in pieces]
        + [
            pltpu.VMEM((bits + 2,) + small.shape, jnp.float32),
            pltpu.VMEM((bits + 1,) + small.shape, jnp.float32),
            pltpu.VMEM((nf,) + small.shape, jnp.float32),
        ]
        + [DMA((count,))]
        + [DMA((2, count, nf, bits))] * 2
        + [DMA((count, nf))] * 2
        + [DMA((2, count, bits))] * 2
        + [DMA((count,))] * 2
        + [DMA((count,))]
        + [DMA((bits + 1,))] * 2
        + [DMA((nf,))] * 2,
        compiler_params=pltpu.CompilerParams(collective_id=3, has_side_effects=True),
        name="reduce_gradients",
    )(*views, small)
    return [
        o.reshape(p.shape[0] // nf * 2, p.shape[1]) for o, p in zip(outs, parts)
    ], outs[count]


LANES = 128
GROUP = QUERY_HEADS // KEY_VALUE_HEADS
SMEM_SPEC = pl.BlockSpec(memory_space=pltpu.SMEM)
VMEM_SPEC = pl.BlockSpec(memory_space=pltpu.VMEM)


def low_lanes(shape):
    return lax.broadcasted_iota(jnp.int32, shape, len(shape) - 1) % LANES < HEAD_SIZE


def stack_heads(ref, row, group, length, high):
    tiles = []
    for pair in range(GROUP // 2):
        cols = pl.ds((group * GROUP // 2 + pair) * LANES, LANES)
        tile = ref[pl.ds(row, length), cols].astype(jnp.float32)
        turned = pltpu.roll(tile, HEAD_SIZE, 1)
        low = low_lanes(tile.shape)
        if high:
            tiles += [jnp.where(low, 0.0, turned), jnp.where(low, 0.0, tile)]
        else:
            tiles += [jnp.where(low, tile, 0.0), jnp.where(low, turned, 0.0)]
    return jnp.concatenate(tiles, axis=0)


def unstack_heads(ref, row, group, length, value, high):
    for pair in range(GROUP // 2):
        cols = pl.ds((group * GROUP // 2 + pair) * LANES, LANES)
        first = value[2 * pair * length : (2 * pair + 1) * length]
        second = value[(2 * pair + 1) * length : (2 * pair + 2) * length]
        low = low_lanes(first.shape)
        if high:
            tile = jnp.where(low, pltpu.roll(first, HEAD_SIZE, 1), second)
        else:
            tile = jnp.where(low, first, pltpu.roll(second, HEAD_SIZE, 1))
        ref[pl.ds(row, length), cols] = tile.astype(ref.dtype)


def query_span(rank, order, starts, stored_of, which, length):
    block = order[2 * rank + which]
    first = jnp.int32(0)
    place = block * length + lax.broadcasted_iota(jnp.int32, (1, length), 1)
    begin = jnp.zeros((1, length), jnp.int32)
    for d in range(starts.shape[1]):
        first = jnp.where(starts[0, d] <= block * length, starts[0, d], first)
        begin = jnp.where(starts[0, d] <= place, starts[0, d], begin)
    place = jnp.concatenate([place] * GROUP, axis=1)
    begin = jnp.concatenate([begin] * GROUP, axis=1)
    return block, first // length, place, begin


def invert_order(order, stored_of):
    for s in range(order.shape[0]):
        stored_of[order[s]] = s


def key_rows(stored_of, block, length, blocks):
    second = stored_of[jnp.minimum(block + 1, blocks - 1)]
    return [
        pl.ds(pl.multiple_of(s * length, length), length) for s in (stored_of[block], second)
    ]


def allowed_keys(block, place, begin, length):
    key = block * length + lax.broadcasted_iota(jnp.int32, (2 * length, place.shape[1]), 0)
    return (key >= begin) & (key <= place)


def dot_last(left, right):
    return lax.dot_general(
        left, right, (((1,), (1,)), ((), ())), preferred_element_type=jnp.float32
    )


def dot_plain(left, right):
    return lax.dot_general(
        left, right, (((1,), (0,)), ((), ())), preferred_element_type=jnp.float32
    )


def attend_kernel(rank, order, starts, query, pair, attended, exact, log_sum, stored_of, acc, queries):
    length = query.shape[0] // 2
    blocks = order.shape[0]
    invert_order(order, stored_of)

    def one_block(which, carry):
        row = pl.multiple_of(which * length, length)
        block, first, place, begin = query_span(rank[0], order, starts, stored_of, which, length)
        for g in range(KEY_VALUE_HEADS):
            queries[g] = stack_heads(query, row, g, length, False).astype(jnp.bfloat16)
        acc[...] = jnp.zeros_like(acc)

        def step(t, carry):
            key_block = first + 2 * t
            rows = key_rows(stored_of, key_block, length, blocks)
            allowed = allowed_keys(key_block, place, begin, length)
            for g in range(KEY_VALUE_HEADS):
                cols = pl.ds(g * LANES, LANES)
                keys = jnp.concatenate([pair[r, cols] for r in rows], axis=0)
                scores = dot_last(keys, queries[g])
                weights = jnp.where(allowed, jnp.exp(scores), 0.0).astype(jnp.bfloat16)
                ones = jnp.where(low_lanes(keys.shape), 1.0, keys.astype(jnp.float32))
                acc[g] += dot_plain(ones.T.astype(jnp.bfloat16), weights)
            return carry

        lax.fori_loop(0, (block - first + 2) // 2, step, 0)
        for g in range(KEY_VALUE_HEADS):
            total = acc[g]
            sums = total[0:1]
            log_sum[which, g] = jnp.broadcast_to(jnp.log(sums), log_sum.shape[2:])
            value = (total / sums).T
            unstack_heads(attended, row, g, length, value, True)
            unstack_heads(exact, row, g, length, value, True)
        return carry

    lax.fori_loop(0, 2, one_block, 0)


def attend(rank, order, starts, query, pair):
    rows = query.shape[0]
    wide = GROUP * (rows // 2)
    return pl.pallas_call(
        attend_kernel,
        out_shape=[
            jax.ShapeDtypeStruct(query.shape, jnp.bfloat16),
            jax.ShapeDtypeStruct(query.shape, jnp.float32),
            jax.ShapeDtypeStruct((2, KEY_VALUE_HEADS, 8, wide), jnp.float32),
        ],
        in_specs=[SMEM_SPEC] * 3 + [VMEM_SPEC] * 2,
        out_specs=[VMEM_SPEC] * 3,
        scratch_shapes=[
            pltpu.SMEM((order.shape[0],), jnp.int32),
            pltpu.VMEM((KEY_VALUE_HEADS, LANES, wide), jnp.float32),
            pltpu.VMEM((KEY_VALUE_HEADS, wide, LANES), jnp.bfloat16),
        ],
        name="attend",
    )(rank, order, starts, query, pair)


def attend_back_kernel(
    rank, order, starts, query, pair, grad, exact, log_sum, grad_query, grad_pair,
    stored_of, total, acc, queries, grads, delta,
):
    length = query.shape[0] // 2
    blocks = order.shape[0]
    invert_order(order, stored_of)
    total[...] = jnp.zeros_like(total)

    def one_block(which, carry):
        row = pl.multiple_of(which * length, length)
        block, first, place, begin = query_span(rank[0], order, starts, stored_of, which, length)
        for g in range(KEY_VALUE_HEADS):
            queries[g] = stack_heads(query, row, g, length, False).astype(jnp.bfloat16)
            upper = stack_heads(grad, row, g, length, True)
            grads[g] = upper.astype(jnp.bfloat16)
            product = upper * stack_heads(exact, row, g, length, True)
            delta[g] = jnp.broadcast_to(
                jnp.sum(product.T, axis=0, keepdims=True), delta.shape[1:]
            )
        acc[...] = jnp.zeros_like(acc)

        def step(t, carry):
            key_block = first + 2 * t
            rows = key_rows(stored_of, key_block, length, blocks)
            allowed = allowed_keys(key_block, place, begin, length)
            for g in range(KEY_VALUE_HEADS):
                cols = pl.ds(g * LANES, LANES)
                keys = jnp.concatenate([pair[r, cols] for r in rows], axis=0)
                scores = dot_last(keys, queries[g])
                probs = jnp.where(allowed, jnp.exp(scores - log_sum[which, g, 0:1]), 0.0)
                grad_probs = dot_last(keys, grads[g])
                grad_scores = (probs * (grad_probs - delta[g, 0:1])).astype(jnp.bfloat16)
                turned = keys.astype(jnp.float32).T.astype(jnp.bfloat16)
                acc[g] += dot_plain(turned, grad_scores)
                both = dot_plain(grad_scores, queries[g]) + dot_plain(
                    probs.astype(jnp.bfloat16), grads[g]
                )
                total[rows[0], cols] += both[:length]
                total[rows[1], cols] += both[length:]
            return carry

        lax.fori_loop(0, (block - first + 2) // 2, step, 0)
        for g in range(KEY_VALUE_HEADS):
            unstack_heads(grad_query, row, g, length, acc[g].T, False)
        return carry

    lax.fori_loop(0, 2, one_block, 0)

    def finish(t, carry):
        at = pl.ds(pl.multiple_of(t * length, length), length)
        grad_pair[at, :] = total[at, :].astype(grad_pair.dtype)
        return carry

    lax.fori_loop(0, blocks, finish, 0)


def attend_back(rank, order, starts, query, pair, grad, exact, log_sum):
    rows = query.shape[0]
    wide = GROUP * (rows // 2)
    return pl.pallas_call(
        attend_back_kernel,
        out_shape=[
            jax.ShapeDtypeStruct(query.shape, jnp.float32),
            jax.ShapeDtypeStruct(pair.shape, jnp.bfloat16),
        ],
        in_specs=[SMEM_SPEC] * 3 + [VMEM_SPEC] * 5,
        out_specs=[VMEM_SPEC] * 2,
        scratch_shapes=[
            pltpu.SMEM((order.shape[0],), jnp.int32),
            pltpu.VMEM(pair.shape, jnp.float32),
            pltpu.VMEM((KEY_VALUE_HEADS, LANES, wide), jnp.float32),
            pltpu.VMEM((KEY_VALUE_HEADS, wide, LANES), jnp.bfloat16),
            pltpu.VMEM((KEY_VALUE_HEADS, wide, LANES), jnp.bfloat16),
            pltpu.VMEM((KEY_VALUE_HEADS, 8, wide), jnp.float32),
        ],
        name="attend_back",
    )(rank, order, starts, query, pair, grad, exact, log_sum)


CHUNK = 256


def head_means(values):
    shape = (LANES, LANES)
    same = (
        lax.broadcasted_iota(jnp.int32, shape, 0) // HEAD_SIZE
        == lax.broadcasted_iota(jnp.int32, shape, 1) // HEAD_SIZE
    )
    ones = jnp.where(same, 1.0, 0.0).astype(jnp.bfloat16)
    high = values.astype(jnp.bfloat16)
    low = (values - high.astype(jnp.float32)).astype(jnp.bfloat16)
    return (dot_plain(high, ones) + dot_plain(low, ones)) * (1.0 / HEAD_SIZE)


def first_quarter(shape):
    return lax.broadcasted_iota(jnp.int32, shape, len(shape) - 1) % HEAD_SIZE < HEAD_SIZE // 2


def turn(values, cosines, sines, sign):
    half = HEAD_SIZE // 2
    ahead = pltpu.roll(values, LANES - half, 1)
    behind = pltpu.roll(values, half, 1)
    other = jnp.where(first_quarter(values.shape), -ahead, behind)
    return values * cosines + sign * other * sines


def row_inverse(ref, rows):
    total = jnp.zeros((rows, 1), jnp.float32)
    width = ref.shape[1]
    for j in range(0, width, CHUNK):
        value = ref[:, j : j + CHUNK].astype(jnp.float32)
        total = total + jnp.sum(value * value, axis=1, keepdims=True)
    return lax.rsqrt(total * (1.0 / width) + EPSILON)


def project_kernel(
    rank, order, starts, tokens, weight, gain, qk_gain, frequency,
    normed, raw, query, pair, cosines, sines,
):
    rows = tokens.shape[0]
    length = rows // 2
    for which in (0, 1):
        block = order[2 * rank[0] + which]
        place = block * length + lax.broadcasted_iota(jnp.int32, (length, LANES), 0)
        begin = jnp.zeros((length, LANES), jnp.int32)
        for d in range(starts.shape[1]):
            begin = jnp.where(starts[0, d] <= place, starts[0, d], begin)
        angle = (place - begin).astype(jnp.float32) * frequency[...]
        at = pl.ds(which * length, length)
        cosines[at, :] = jnp.cos(angle)
        sines[at, :] = jnp.sin(angle)
    inverse = row_inverse(tokens, rows)
    for j in range(0, tokens.shape[1], CHUNK):
        cols = pl.ds(j, CHUNK)
        value = tokens[:, cols].astype(jnp.float32) * inverse * gain[:, cols]
        normed[:, cols] = value.astype(jnp.bfloat16)
    query_width = QUERY_HEADS * HEAD_SIZE
    key_width = KEY_VALUE_HEADS * HEAD_SIZE

    def head_turn(cols, which):
        value = raw[:, cols]
        scale = lax.rsqrt(head_means(value * value) + EPSILON)
        return turn(value * scale * qk_gain[which : which + 1, :], cosines[...], sines[...], 1.0)

    for j in range(0, weight.shape[1], CHUNK):
        raw[:, j : j + CHUNK] = dot_plain(normed[...], weight[:, j : j + CHUNK])
    for j in range(0, query_width, LANES):
        cols = pl.ds(j, LANES)
        query[:, cols] = (head_turn(cols, 0) * HEAD_SIZE**-0.5).astype(jnp.bfloat16)
    for j in range(0, key_width, LANES):
        key = head_turn(pl.ds(query_width + j, LANES), 1)
        value = raw[:, query_width + key_width + j : query_width + key_width + j + LANES]
        low = low_lanes(key.shape)
        first = jnp.where(low, key, pltpu.roll(value, HEAD_SIZE, 1))
        second = jnp.where(low, pltpu.roll(key, HEAD_SIZE, 1), value)
        pair[:, 2 * j : 2 * j + LANES] = first.astype(jnp.bfloat16)
        pair[:, 2 * j + LANES : 2 * j + 2 * LANES] = second.astype(jnp.bfloat16)


def project(rank, order, starts, tokens, weight, gain, qk_gain, frequency):
    rows, width = tokens.shape
    shape = jax.ShapeDtypeStruct
    return pl.pallas_call(
        project_kernel,
        out_shape=[
            shape((rows, width), jnp.bfloat16),
            shape((rows, weight.shape[1]), jnp.float32),
            shape((rows, QUERY_HEADS * HEAD_SIZE), jnp.bfloat16),
            shape((rows, 2 * KEY_VALUE_HEADS * HEAD_SIZE), jnp.bfloat16),
            shape((rows, LANES), jnp.float32),
            shape((rows, LANES), jnp.float32),
        ],
        in_specs=[SMEM_SPEC] * 3 + [VMEM_SPEC] * 5,
        out_specs=[VMEM_SPEC] * 6,
        name="project",
    )(rank, order, starts, tokens, weight, gain, qk_gain, frequency)


def feed_kernel(
    tokens, cotangent, attended, gain, w_out, w_gate, w_up, w_down,
    mixed, normed, hidden, grad_gate, grad_up, grad_resid, grad_branch, grad_attended, gain_grad,
    out_v, gate_v, up_v, down_v, resid, sems,
):
    rows, width = tokens.shape
    loads = [
        pltpu.make_async_copy(src, dst, sems.at[i])
        for i, (src, dst) in enumerate(
            ((w_out, out_v), (w_gate, gate_v), (w_up, up_v), (w_down, down_v))
        )
    ]
    for load in loads:
        load.start()
    loads[0].wait()
    for j in range(0, width, CHUNK):
        cols = pl.ds(j, CHUNK)
        resid[:, cols] = tokens[:, cols].astype(jnp.float32) + dot_plain(
            attended[...], out_v[:, cols]
        )
    inverse = row_inverse(resid, rows)
    for j in range(0, width, CHUNK):
        cols = pl.ds(j, CHUNK)
        normed[:, cols] = (resid[:, cols] * inverse * gain[:, cols]).astype(jnp.bfloat16)
    for load in loads[1:]:
        load.wait()
    for j in range(0, gate_v.shape[1], CHUNK):
        cols = pl.ds(j, CHUNK)
        gate = dot_plain(normed[...], gate_v[:, cols])
        up = dot_plain(normed[...], up_v[:, cols])
        sigmoid = 1.0 / (1.0 + jnp.exp(-gate))
        hidden[:, cols] = (gate * sigmoid * up).astype(jnp.bfloat16)
        grad_hidden = dot_last(cotangent[...], down_v[cols, :])
        grad_gate[:, cols] = (
            grad_hidden * up * sigmoid * (1.0 + gate * (1.0 - sigmoid))
        ).astype(jnp.bfloat16)
        grad_up[:, cols] = (grad_hidden * gate * sigmoid).astype(jnp.bfloat16)
    mean = jnp.zeros((rows, 1), jnp.float32)
    for j in range(0, width, CHUNK):
        cols = pl.ds(j, CHUNK)
        mixed[:, cols] = (resid[:, cols] + dot_plain(hidden[...], down_v[:, cols])).astype(
            jnp.bfloat16
        )
        grad = dot_last(grad_gate[...], gate_v[cols, :]) + dot_last(grad_up[...], up_v[cols, :])
        grad_resid[:, cols] = grad
        mean = mean + jnp.sum(grad * gain[:, cols] * resid[:, cols], axis=1, keepdims=True)
    mean = mean * (1.0 / width) * inverse * inverse
    for j in range(0, width, CHUNK):
        cols = pl.ds(j, CHUNK)
        grad = grad_resid[:, cols]
        value = resid[:, cols]
        gain_grad[:, cols] = jnp.sum(grad * value * inverse, axis=0, keepdims=True)
        total = cotangent[:, cols].astype(jnp.float32) + inverse * (
            grad * gain[:, cols] - value * mean
        )
        grad_resid[:, cols] = total
        grad_branch[:, cols] = total.astype(jnp.bfloat16)
    for j in range(0, attended.shape[1], CHUNK):
        cols = pl.ds(j, CHUNK)
        grad_attended[:, cols] = dot_last(grad_branch[...], out_v[cols, :]).astype(jnp.bfloat16)


def feed(tokens, cotangent, attended, gain, w_out, w_gate, w_up, w_down):
    rows, width = tokens.shape
    inner = w_gate.shape[1]
    shape = jax.ShapeDtypeStruct
    low, full = jnp.bfloat16, jnp.float32
    return pl.pallas_call(
        feed_kernel,
        out_shape=[
            shape((rows, width), low),
            shape((rows, width), low),
            shape((rows, inner), low),
            shape((rows, inner), low),
            shape((rows, inner), low),
            shape((rows, width), full),
            shape((rows, width), low),
            shape(attended.shape, low),
            shape((1, width), full),
        ],
        in_specs=[VMEM_SPEC] * 4 + [HBM_SPEC] * 4,
        out_specs=[VMEM_SPEC] * 9,
        scratch_shapes=[pltpu.VMEM(w.shape, low) for w in (w_out, w_gate, w_up, w_down)]
        + [pltpu.VMEM((rows, width), full), DMA((4,))],
        name="feed",
    )(tokens, cotangent, attended, gain, w_out, w_gate, w_up, w_down)


def project_back_kernel(
    tokens, weight, gain, qk_gain, raw, cosines, sines, grad_query, grad_pair, grad_resid,
    grad_projected, tokens_grad, gain_grad, qk_grad,
    grads,
):
    rows, width = tokens.shape
    query_width = QUERY_HEADS * HEAD_SIZE
    key_width = KEY_VALUE_HEADS * HEAD_SIZE

    def head_back(cols, which, grad):
        grad = turn(grad, cosines[...], sines[...], -1.0)
        value = raw[:, cols]
        scale = lax.rsqrt(head_means(value * value) + EPSILON)
        scaled = grad * qk_gain[which : which + 1, :]
        mean = head_means(scaled * value)
        result = scale * (scaled - value * scale * scale * mean)
        grad_projected[:, cols] = result.astype(jnp.bfloat16)
        return jnp.sum(grad * value * scale, axis=0, keepdims=True)

    sums = [jnp.zeros((1, LANES), jnp.float32)] * 2
    for j in range(0, query_width, LANES):
        cols = pl.ds(j, LANES)
        sums[0] = sums[0] + head_back(cols, 0, grad_query[:, cols] * HEAD_SIZE**-0.5)
    for j in range(0, key_width, LANES):
        first = grad_pair[:, 2 * j : 2 * j + LANES].astype(jnp.float32)
        second = grad_pair[:, 2 * j + LANES : 2 * j + 2 * LANES].astype(jnp.float32)
        low = low_lanes(first.shape)
        key = jnp.where(low, first, pltpu.roll(second, HEAD_SIZE, 1))
        value = jnp.where(low, pltpu.roll(first, HEAD_SIZE, 1), second)
        sums[1] = sums[1] + head_back(pl.ds(query_width + j, LANES), 1, key)
        at = query_width + key_width + j
        grad_projected[:, at : at + LANES] = value.astype(jnp.bfloat16)
    for which in (0, 1):
        qk_grad[which : which + 1, :] = sums[which] + pltpu.roll(sums[which], HEAD_SIZE, 1)
    inverse = row_inverse(tokens, rows)
    mean = jnp.zeros((rows, 1), jnp.float32)
    for j in range(0, width, CHUNK):
        cols = pl.ds(j, CHUNK)
        grad = dot_last(grad_projected[...], weight[cols, :])
        grads[:, cols] = grad
        value = tokens[:, cols].astype(jnp.float32)
        mean = mean + jnp.sum(grad * gain[:, cols] * value, axis=1, keepdims=True)
    mean = mean * (1.0 / width) * inverse * inverse
    for j in range(0, width, CHUNK):
        cols = pl.ds(j, CHUNK)
        grad = grads[:, cols]
        value = tokens[:, cols].astype(jnp.float32)
        gain_grad[:, cols] = jnp.sum(grad * value * inverse, axis=0, keepdims=True)
        tokens_grad[:, cols] = grad_resid[:, cols] + inverse * (
            grad * gain[:, cols] - value * mean
        )


def project_back(
    tokens, weight, gain, qk_gain, raw, cosines, sines, grad_query, grad_pair, grad_resid
):
    rows, width = tokens.shape
    shape = jax.ShapeDtypeStruct
    return pl.pallas_call(
        project_back_kernel,
        out_shape=[
            shape((rows, weight.shape[1]), jnp.bfloat16),
            shape((rows, width), jnp.float32),
            shape((1, width), jnp.float32),
            shape((2, LANES), jnp.float32),
        ],
        in_specs=[VMEM_SPEC] * 10,
        out_specs=[VMEM_SPEC] * 4,
        scratch_shapes=[pltpu.VMEM((rows, width), jnp.float32)],
        name="project_back",
    )(tokens, weight, gain, qk_gain, raw, cosines, sines, grad_query, grad_pair, grad_resid)


def transposed_times(left, right):
    return lax.dot_general(
        left, right, (((0,), (0,)), ((), ())), preferred_element_type=jnp.float32
    )


def pack_rows(arrays, multiple):
    flat = jnp.concatenate([a.astype(jnp.float32).reshape(-1) for a in arrays])
    size = multiple * 128
    return jnp.pad(flat, (0, -flat.shape[0] % size)).reshape(-1, 128)


def per_device(
    tokens,
    cotangent,
    doc_starts,
    deal_order,
    query_key_value_weight,
    w_out,
    w_gate,
    w_up,
    w_down,
    gain_attn,
    gain_ffn,
    gain_qk,
):
    ctx_count = lax.axis_size("ctx")
    fsdp_count = lax.axis_size("fsdp")
    ctx_rank = lax.axis_index("ctx")
    fsdp_rank = lax.axis_index("fsdp")
    model_shard = gain_attn.shape[0]
    qk_shard = gain_qk.shape[1]
    model = model_shard * fsdp_count
    gains = pack_rows([gain_attn, gain_ffn, gain_qk], 8)
    (qkv_full, out_full, gate_full, up_full, down_full), gains = gather_weights(
        fsdp_count, ctx_count, [query_key_value_weight, w_out, w_gate, w_up, w_down], gains
    )
    gains = gains.reshape(fsdp_count, -1)
    attn_gain = gains[:, :model_shard].reshape(1, model)
    ffn_gain = gains[:, model_shard : 2 * model_shard].reshape(1, model)
    qk_gain = gains[:, 2 * model_shard : 2 * model_shard + 2 * qk_shard]
    qk_gain = jnp.swapaxes(qk_gain.reshape(fsdp_count, 2, qk_shard), 0, 1).reshape(2, HEAD_SIZE)
    qk_gain = jnp.concatenate([qk_gain, qk_gain], axis=1)
    pack_in = tokens[0]
    grad_mixed = cotangent[0]
    token_rows = pack_in.shape[0]
    rank = ctx_rank.reshape(1).astype(jnp.int32)
    frequency = THETA ** (-jnp.arange(0, HEAD_SIZE // 2, dtype=jnp.float32) * 2.0 / HEAD_SIZE)
    frequency = jnp.concatenate([frequency] * (2 * LANES // HEAD_SIZE)).reshape(1, LANES)

    normed, raw, query, local_pair, cosines, sines = project(
        rank, deal_order, doc_starts, pack_in, qkv_full, attn_gain, qk_gain, frequency
    )
    pair = gather_pair(fsdp_count, ctx_count, local_pair)
    attended, exact, log_sum = attend(rank, deal_order, doc_starts, query, pair)
    (
        mixed_out,
        normed_ffn,
        hidden,
        grad_gate,
        grad_up,
        grad_resid,
        grad_branch,
        grad_attended,
        ffn_gain_part,
    ) = feed(pack_in, grad_mixed, attended, ffn_gain, out_full, gate_full, up_full, down_full)
    grad_query, grad_pair = attend_back(
        rank, deal_order, doc_starts, query, pair, grad_attended, exact, log_sum
    )
    grad_pair = scatter_pair(fsdp_count, ctx_count, grad_pair)
    grad_projected, tokens_grad, attn_gain_part, qk_gain_part = project_back(
        pack_in,
        qkv_full,
        attn_gain,
        qk_gain,
        raw,
        cosines,
        sines,
        grad_query,
        grad_pair,
        grad_resid,
    )
    core = ctx_rank % 2
    swap = [(i, i + 1 - 2 * (i % 2)) for i in range(ctx_count)]

    def both(values):
        return jnp.concatenate([values, lax.ppermute(values, "ctx", swap)], axis=0)

    def core_part(values, which):
        view = values.reshape(token_rows, fsdp_count, 2, -1)
        return lax.dynamic_index_in_dim(view, which, 2, keepdims=False).reshape(token_rows, -1)

    def both_part(values):
        mine = core_part(values, core)
        other = lax.ppermute(core_part(values, 1 - core), "ctx", swap)
        return jnp.concatenate([mine, other], axis=0)

    ffn_rows = both_part(normed_ffn)
    parts = [
        transposed_times(left, right).astype(jnp.bfloat16)
        for left, right in (
            (both_part(hidden), both(grad_mixed)),
            (ffn_rows, both(grad_gate)),
            (ffn_rows, both(grad_up)),
            (both_part(attended), both(grad_branch)),
            (both_part(normed), both(grad_projected)),
        )
    ]
    gain_sums = pack_rows([attn_gain_part, ffn_gain_part, qk_gain_part[:, :HEAD_SIZE]], 8)
    (down_grad, gate_grad, up_grad, out_grad, qkv_grad), gain_sums = reduce_gradients(
        fsdp_count, ctx_count, parts, gain_sums
    )
    gain_sums = gain_sums.reshape(-1)
    attn_gain_grad = lax.dynamic_slice_in_dim(gain_sums, fsdp_rank * model_shard, model_shard)
    ffn_gain_grad = lax.dynamic_slice_in_dim(
        gain_sums, model + fsdp_rank * model_shard, model_shard
    )
    qk_gain_grad = lax.dynamic_slice_in_dim(
        gain_sums[2 * model : 2 * model + 2 * HEAD_SIZE].reshape(2, HEAD_SIZE),
        fsdp_rank * qk_shard,
        qk_shard,
        axis=1,
    )
    return (
        mixed_out[None],
        tokens_grad[None],
        qkv_grad.astype(jnp.float32),
        out_grad.astype(jnp.float32),
        gate_grad.astype(jnp.float32),
        up_grad.astype(jnp.float32),
        down_grad.astype(jnp.float32),
        attn_gain_grad,
        ffn_gain_grad,
        qk_gain_grad,
    )


def solution(mesh):
    return jax.shard_map(
        per_device,
        mesh=mesh,
        in_specs=(
            P("fsdp", "ctx", None),
            P("fsdp", "ctx", None),
            P("fsdp", None),
            P(),
            P("fsdp", None),
            P("fsdp", None),
            P("fsdp", None),
            P("fsdp", None),
            P("fsdp", None),
            P("fsdp"),
            P("fsdp"),
            P(None, "fsdp"),
        ),
        out_specs=(
            P("fsdp", "ctx", None),
            P("fsdp", "ctx", None),
            P("fsdp", None),
            P("fsdp", None),
            P("fsdp", None),
            P("fsdp", None),
            P("fsdp", None),
            P("fsdp"),
            P("fsdp"),
            P(None, "fsdp"),
        ),
        check_vma=False,
    )
```

```python
import functools

import jax
import jax.numpy as jnp
from jax import lax
from jax.experimental import pallas as pl
from jax.experimental.pallas import tpu as pltpu
from jax.sharding import PartitionSpec as P

QUERY_HEADS = 16
KEY_VALUE_HEADS = 4
HEAD_SIZE = 64


EPSILON = 1e-06
THETA = 10000.0

MESH = pl.DeviceIdType.MESH
DMA = pltpu.SemaphoreType.DMA
HBM_SPEC = pl.BlockSpec(memory_space=pl.ANY)
VMEM_SPEC = pl.BlockSpec(memory_space=pltpu.VMEM)
SPACING = 2
VMEM_LIMIT = 67043328


def plane_shape(ctx_count):
    chips = ctx_count // 2
    bits = chips.bit_length() - 1
    assert 2**bits == chips and ctx_count == 2 * chips
    return chips, bits


class Place:
    def __init__(self, ctx_count, fsdp_count):
        self.chips, self.bits = plane_shape(ctx_count)
        self.fsdp_count = fsdp_count
        self.ctx = lax.axis_index("ctx")
        self.z = lax.axis_index("fsdp")
        self.core = self.ctx % 2
        chip = self.ctx // 2
        self.bit = [(chip // 2**j) % 2 for j in range(self.bits)]
        self.across = [self.ctx + (1 - 2 * self.bit[j]) * 2 * 2**j for j in range(self.bits)]
        self.partner = self.ctx + 1 - 2 * self.core
        self.orders = (list(range(self.bits)), list(reversed(range(self.bits))))

    def at(self, free=(), other=None):
        return tuple(
            slice(None) if j in free else (1 - self.bit[j] if j == other else self.bit[j])
            for j in reversed(range(self.bits))
        )

    def barrier(self, plane=True, line=True, near=False):
        sem = pltpu.get_barrier_semaphore()
        count = 0
        if plane:
            for p in self.across + [self.partner]:
                pl.semaphore_signal(sem, inc=1, device_id={"ctx": p}, device_id_type=MESH)
                count += 1
        if line:
            for k in range(1, self.fsdp_count):
                pl.semaphore_signal(
                    sem,
                    inc=1,
                    device_id={"fsdp": (self.z + k) % self.fsdp_count},
                    device_id_type=MESH,
                )
                count += 1
        pl.semaphore_wait(sem, count)


def remote(src, dst, send, recv, **where):
    return pltpu.make_async_remote_copy(
        src, dst, send, recv, device_id=where, device_id_type=MESH
    )


def run_ticks(jobs, spacing=SPACING):
    depth = max(len(job) for job in jobs)
    for tick in range(len(jobs) + spacing * (depth - 1)):
        for j in reversed(range(depth)):
            t = tick - spacing * j
            if 0 <= t < len(jobs) and j < len(jobs[t]):
                jobs[t][j]()


def column_half(ref, half):
    n = ref.shape[-1] // 2
    return pl.ds(half * n, n)


def gather_kernel(nf, nc, count, *refs):
    shards, small = refs[:count], refs[count]
    outs, small_out = refs[count + 1 : 2 * count + 1], refs[2 * count + 1]
    stages = refs[2 * count + 2 : 3 * count + 3]
    up_s, up_r, down_s, down_r, ps, pr, cs, cr, ss, sr, load_sem, store_sem = refs[3 * count + 3 :]
    me = Place(nc, nf)
    z = me.z
    loads = [
        pltpu.make_async_copy(src, dst, load_sem.at[i])
        for i, (src, dst) in enumerate(zip(list(shards) + [small], stages))
    ]
    stores = [
        pltpu.make_async_copy(stages[i], dst.at[z], store_sem.at[i])
        for i, dst in enumerate(list(outs) + [small_out])
    ]
    for load in loads:
        load.start()
    me.barrier()

    def source(k):
        pairs = jnp.minimum(z, nf - 1 - z)
        near = (k + 1) // 2
        near_source = z - near if k % 2 == 1 else z + near
        far = k - pairs
        far_source = jnp.where(2 * z < nf - 1, z + far, z - far)
        return jnp.where(k <= 2 * pairs, near_source, far_source)

    sources = [None] + [source(k) for k in range(1, nf)]

    def line_copy(i, src_z, src, up):
        to = z + 1 if up else z - 1
        sems = (up_s, up_r) if up else (down_s, down_r)
        return remote(
            src,
            outs[i].at[(src_z, me.core) + me.at()],
            sems[0].at[i, src_z],
            sems[1].at[i, src_z],
            fsdp=to,
        )

    def line_start(i, src_z, src, up, condition):
        @pl.when(condition)
        def _():
            line_copy(i, src_z, src, up).start()

    def small_copy(k):
        return remote(small, small_out.at[z], ss.at[k], sr.at[k], fsdp=(z + k) % nf)

    for k in range(1, nf):
        small_copy(k).start()
    for i in range(count):
        mine = shards[i].at[(me.core,) + me.at()]
        line_start(i, z, mine, True, z + 1 < nf)
        line_start(i, z, mine, False, z > 0)

    def line_stage(i, k):
        src_z = sources[k]
        here = outs[i].at[(src_z, me.core) + me.at()]
        below = src_z < z

        @pl.when(below)
        def _():
            line_copy(i, src_z, here, True).wait_recv()

        @pl.when(jnp.logical_not(below))
        def _():
            line_copy(i, src_z, here, False).wait_recv()

        line_start(i, src_z, here, True, jnp.logical_and(below, z + 1 < nf))
        line_start(i, src_z, here, False, jnp.logical_and(src_z > z, z > 0))

    def plane_copy(i, k, half, j):
        order = me.orders[half]
        ref = outs[i].at[
            (sources[k], me.core) + me.at(order[:j]) + (slice(None), column_half(outs[i], half))
        ]
        return remote(
            ref, ref, ps.at[half, i, k, j], pr.at[half, i, k, j], ctx=me.across[order[j]]
        )

    def core_copy(i, k):
        ref = outs[i].at[sources[k], me.core]
        return remote(ref, ref, cs.at[i, k], cr.at[i, k], ctx=me.partner)

    def plane_stage(i, k, j):
        if j == 0:
            line_stage(i, k)
        else:
            for half in (0, 1):
                plane_copy(i, k, half, j - 1).wait_recv()
        if j < me.bits:
            for half in (0, 1):
                plane_copy(i, k, half, j).start()
        else:
            core_copy(i, k).start()

    order = [(i, k) for i in range(count) for k in range(1, nf)]
    jobs = [
        [functools.partial(plane_stage, i, k, j) for j in range(me.bits + 1)]
        + [core_copy(i, k).wait_recv]
        for i, k in order
    ]
    for load, store in zip(loads, stores):
        load.wait()
        store.start()
    run_ticks(jobs)
    for k in range(1, nf):
        small_copy(k).wait_recv()
        small_copy(k).wait_send()
    for i in range(count):
        @pl.when(z + 1 < nf)
        def _():
            line_copy(i, z, shards[i].at[(me.core,) + me.at()], True).wait_send()

        @pl.when(z > 0)
        def _():
            line_copy(i, z, shards[i].at[(me.core,) + me.at()], False).wait_send()

    for i, k in order:
        src_z = sources[k]
        here = outs[i].at[(src_z, me.core) + me.at()]

        @pl.when(jnp.logical_and(src_z < z, z + 1 < nf))
        def _():
            line_copy(i, src_z, here, True).wait_send()

        @pl.when(jnp.logical_and(src_z > z, z > 0))
        def _():
            line_copy(i, src_z, here, False).wait_send()

        for half in (0, 1):
            for j in range(me.bits):
                plane_copy(i, k, half, j).wait_send()
        core_copy(i, k).wait_send()
    for store in stores:
        store.wait()


def gather_weights(nf, nc, shards, small):
    _, bits = plane_shape(nc)
    count = len(shards)
    views = [w.reshape((2,) * (1 + bits) + (w.shape[0] // nc, w.shape[1])) for w in shards]
    arrays = views + [small]
    outs = pl.pallas_call(
        functools.partial(gather_kernel, nf, nc, count),
        out_shape=[jax.ShapeDtypeStruct((nf,) + v.shape, v.dtype) for v in arrays],
        in_specs=[HBM_SPEC] * (count + 1),
        out_specs=[HBM_SPEC] * (count + 1),
        scratch_shapes=[pltpu.VMEM(v.shape, v.dtype) for v in arrays]
        + [DMA((count, nf))] * 4
        + [DMA((2, count, nf, bits))] * 2
        + [DMA((count, nf))] * 2
        + [DMA((nf,))] * 2
        + [DMA((count + 1,))] * 2,
        compiler_params=pltpu.CompilerParams(collective_id=0, has_side_effects=True),
        name="gather_weights",
    )(*arrays)
    return [o.reshape(nf * w.shape[0], w.shape[1]) for o, w in zip(outs, shards)], outs[count]


def gather_pair_kernel(nf, nc, pair, out, stage, ps, pr, cs, cr, load_sem, store_sem):
    me = Place(nc, nf)
    load = pltpu.make_async_copy(pair, stage, load_sem)
    load.start()
    me.barrier(line=False)

    def plane_copy(half, j):
        order = me.orders[half]
        where = (slice(None), column_half(out, half))
        dst = out.at[me.at(order[:j]) + (me.core,) + where]
        src = pair.at[where] if j == 0 else dst
        return remote(src, dst, ps.at[half, j], pr.at[half, j], ctx=me.across[order[j]])

    own_core = remote(pair, out.at[me.at() + (me.core,)], cs.at[0, 0], cr.at[0, 0], ctx=me.partner)

    def core_copy(half, j):
        order = me.orders[half]
        ref = out.at[
            me.at(order[:j], other=order[j]) + (me.core, slice(None), column_half(out, half))
        ]
        return remote(ref, ref, cs.at[half, j + 1], cr.at[half, j + 1], ctx=me.partner)

    for half in (0, 1):
        plane_copy(half, 0).start()
    own_core.start()
    load.wait()
    store = pltpu.make_async_copy(stage, out.at[me.at() + (me.core,)], store_sem)
    store.start()
    store.wait()
    for j in range(me.bits):
        for half in (0, 1):
            plane_copy(half, j).wait_recv()
        if j + 1 < me.bits:
            for half in (0, 1):
                plane_copy(half, j + 1).start()
        for half in (0, 1):
            core_copy(half, j).start()
    own_core.wait()
    for j in range(me.bits):
        for half in (0, 1):
            plane_copy(half, j).wait_send()
            core_copy(half, j).wait()


def gather_pair(nf, nc, pair):
    _, bits = plane_shape(nc)
    out = pl.pallas_call(
        functools.partial(gather_pair_kernel, nf, nc),
        out_shape=jax.ShapeDtypeStruct((2,) * (bits + 1) + pair.shape, pair.dtype),
        in_specs=[HBM_SPEC],
        out_specs=HBM_SPEC,
        scratch_shapes=[pltpu.VMEM(pair.shape, pair.dtype)]
        + [DMA((2, bits))] * 2
        + [DMA((2, bits + 1))] * 2
        + [DMA, DMA],
        compiler_params=pltpu.CompilerParams(collective_id=1, has_side_effects=True),
        name="gather_pair",
    )(pair)
    return out.reshape(nc * pair.shape[0], pair.shape[1])


def reduce_kernel(nf, nc, pairs, lefts_count, rights_count, *refs):
    _, bits = plane_shape(nc)
    count = len(pairs)
    rest = list(refs)

    def take(n):
        return [rest.pop(0) for _ in range(n)]

    lefts, rights = take(lefts_count), take(rights_count)
    grad_pair, back_in = take(1)[0], take(BACK_LOADS)
    gain, qk_gain, cosines, sines, ffn_gain_part = take(5)
    outs, (tokens_grad, small_out) = take(count), take(2)
    left_v, right_v, held = take(lefts_count), take(rights_count + 1), take(count)
    ins = [[take(2) for _ in range(bits)] for _ in range(count)]
    line_in, final = take(count), take(count)
    small_sum, small_in, small_line = take(3)
    pair_held, pair_core, *pair_in = take(2 + 2 * bits)
    back_v, grads = take(BACK_LOADS), take(1)[0]
    back_sem, grad_sem, pl_sem, pcs, pcr, pps, ppr = take(7)
    (ll, lls, llr, rl, rls, rlr, ps, pr, ls, lr, gs, gr, cs, cr, own_sem, ss, sr, sls, slr) = rest
    me = Place(nc, nf)
    z = me.z
    rows = rights[0].shape[0]
    projected_v = right_v[rights_count]
    back_loads = [
        pltpu.make_async_copy(src, dst, back_sem.at[n])
        for n, (src, dst) in enumerate(zip(back_in, back_v))
    ]
    every = tuple(slice(None) for _ in range(bits))
    pair_load = pltpu.make_async_copy(grad_pair.at[every + (me.core,)], pair_held, pl_sem)
    pair_core_copy = remote(
        grad_pair.at[every + (1 - me.core,)], pair_core, pcs, pcr, ctx=me.partner
    )

    def left_load(a):
        return pltpu.make_async_copy(
            lefts[a].at[:, me.core], left_v[a].at[:, :, pl.ds(0, rows)], ll.at[a]
        )

    def right_load(b):
        return pltpu.make_async_copy(rights[b], right_v[b].at[pl.ds(0, rows)], rl.at[b])

    def left_copy(a):
        return remote(
            lefts[a].at[:, 1 - me.core],
            left_v[a].at[:, :, pl.ds(rows, rows)],
            lls.at[a],
            llr.at[a],
            ctx=me.partner,
        )

    def right_copy(b):
        src = rights[b] if b < rights_count else projected_v.at[pl.ds(0, rows)]
        return remote(
            src, right_v[b].at[pl.ds(rows, rows)], rls.at[b], rlr.at[b], ctx=me.partner
        )

    order, seen = [], set()
    for a, b in pairs:
        for key in (("left", a), ("right", b)):
            if key not in seen and key != ("right", rights_count):
                seen.add(key)
                order.append(key)
    for at, (side, n) in enumerate(order):
        (left_load if side == "left" else right_load)(n).start()
        if at == 1:
            pair_load.start()
    for load in back_loads:
        load.start()
    me.barrier()
    for at, (side, n) in enumerate(order):
        (left_copy if side == "left" else right_copy)(n).start()
        if at == 1:
            pair_core_copy.start()
    arrived = set()

    def arrive(side, n):
        if (side, n) not in arrived:
            arrived.add((side, n))
            if (side, n) in order:
                (left_load if side == "left" else right_load)(n).wait()
            (left_copy if side == "left" else right_copy)(n).wait_recv()

    def target(k):
        return (z + k) % nf

    def form(i, k):
        a, b = pairs[i]
        arrive("left", a)
        arrive("right", b)
        width = held[i].shape[-1]
        chunk = min(width, CHUNK)

        def body(t, carry):
            cols = pl.ds(pl.multiple_of(t * chunk, chunk), chunk)
            value = dot_plain(left_v[a][target(k)], right_v[b][:, cols]).astype(jnp.bfloat16)
            held[i][target(k), ..., cols] = value.reshape(held[i].shape[1:-1] + (chunk,))
            return carry

        lax.fori_loop(0, width // chunk, body, 0)

    def plane_copy(i, k, half, j):
        order = me.orders[half]
        src = held[i].at[
            (target(k),)
            + me.at(order[j + 1 :], other=order[j])
            + (slice(None), column_half(held[i], half))
        ]
        return remote(
            src,
            ins[i][j][half].at[k],
            ps.at[half, i, k, j],
            pr.at[half, i, k, j],
            ctx=me.across[order[j]],
        )

    def pair_copy(half, j):
        order = me.orders[half]
        src = pair_held.at[
            me.at(order[j + 1 :], other=order[j]) + (slice(None), column_half(pair_held, half))
        ]
        return remote(
            src, pair_in[2 * j + half], pps.at[half, j], ppr.at[half, j], ctx=me.across[order[j]]
        )

    def pair_add(place, source, local, cols):
        where = place + (slice(None), cols)
        total = pair_held[where].astype(jnp.float32) + source[local].astype(jnp.float32)
        pair_held[where] = total.astype(pair_held.dtype)

    def pair_stage(j):
        if j == 0:
            pair_load.wait()
            pair_core_copy.wait_recv()
            for place, local in chips_of(range(bits)):
                pair_add(place, pair_core, local, slice(None))
        else:
            for half in (0, 1):
                pair_copy(half, j - 1).wait_recv()
                for place, local in chips_of(me.orders[half][j:]):
                    pair_add(place, pair_in[2 * (j - 1) + half], local, column_half(pair_held, half))
        if j < bits:
            for half in (0, 1):
                pair_copy(half, j).start()

    tokens, weight, raw, grad_query, grad_resid = back_v
    query_width = QUERY_HEADS * HEAD_SIZE
    key_width = KEY_VALUE_HEADS * HEAD_SIZE
    own = pl.ds(0, rows)

    def head_back(cols, which, grad):
        grad = turn(grad, cosines[...], sines[...], -1.0)
        value = raw[:, cols]
        scale = lax.rsqrt(head_means(value * value) + EPSILON)
        scaled = grad * qk_gain[which : which + 1, :]
        mean = head_means(scaled * value)
        result = scale * (scaled - value * scale * scale * mean)
        projected_v[own, cols] = result.astype(jnp.bfloat16)
        return jnp.sum(grad * value * scale, axis=0, keepdims=True)

    def heads_stage():
        for load in back_loads:
            load.wait()
        sums = [jnp.zeros((1, LANES), jnp.float32)] * 2
        for j in range(0, query_width, LANES):
            cols = pl.ds(j, LANES)
            sums[0] = sums[0] + head_back(cols, 0, grad_query[:, cols] * HEAD_SIZE**-0.5)
        here = me.at()
        for j in range(0, key_width, LANES):
            first = pair_held[here + (slice(None), pl.ds(2 * j, LANES))].astype(jnp.float32)
            second = pair_held[here + (slice(None), pl.ds(2 * j + LANES, LANES))].astype(
                jnp.float32
            )
            low = low_lanes(first.shape)
            key = jnp.where(low, first, pltpu.roll(second, HEAD_SIZE, 1))
            value = jnp.where(low, pltpu.roll(first, HEAD_SIZE, 1), second)
            sums[1] = sums[1] + head_back(pl.ds(query_width + j, LANES), 1, key)
            projected_v[own, pl.ds(query_width + key_width + j, LANES)] = value.astype(jnp.bfloat16)
        both = [total + pltpu.roll(total, HEAD_SIZE, 1) for total in sums]
        small_sum[0, pl.ds(2 * gain_rows, 1), :] = jnp.where(
            low_lanes(both[0].shape), both[0], both[1]
        )
        right_copy(rights_count).start()

    gain_rows = gain.shape[1] // LANES
    width = gain.shape[1]
    inverse_mean = []

    def matmul_stage():
        inverse = row_inverse(tokens, rows)
        mean = jnp.zeros((rows, 1), jnp.float32)
        for j in range(0, width, CHUNK):
            cols = pl.ds(j, CHUNK)
            grad = dot_last(projected_v[own, :], weight[cols, :])
            grads[:, cols] = grad
            value = tokens[:, cols].astype(jnp.float32)
            mean = mean + jnp.sum(grad * gain[:, cols] * value, axis=1, keepdims=True)
        inverse_mean.extend([inverse, mean * (1.0 / width) * inverse * inverse])

    def norm_stage():
        inverse, mean = inverse_mean
        for j in range(0, width, CHUNK):
            cols = pl.ds(j, CHUNK)
            grad = grads[:, cols]
            value = tokens[:, cols].astype(jnp.float32)
            part = jnp.sum(grad * value * inverse, axis=0, keepdims=True)
            for c in range(0, CHUNK, LANES):
                small_sum[0, pl.ds((j + c) // LANES, 1), :] = part[:, c : c + LANES]
            grad_resid[:, cols] = grad_resid[:, cols] + inverse * (
                grad * gain[:, cols] - value * mean
            )
        tokens_grad_store.start()

    tokens_grad_store = pltpu.make_async_copy(grad_resid, tokens_grad, grad_sem)

    def chips_of(free):
        places, local = [()], [()]
        for b in reversed(range(bits)):
            if b in free:
                places = [t + (v,) for t in places for v in (0, 1)]
                local = [t + (v,) for t in local for v in (0, 1)]
            else:
                places = [t + (me.bit[b],) for t in places]
        return list(zip(places, local))

    def add(i, k, half, j):
        free = me.orders[half][j + 1 :]
        rows, width = held[i].shape[-2], held[i].shape[-1] // 2
        step = min(rows, 32)
        cols = pl.ds(half * width, width)
        for place, local in chips_of(free):

            def body(t, carry, place=place, local=local):
                at = pl.ds(pl.multiple_of(t * step, step), step)
                where = (target(k),) + place + (at, cols)
                total = held[i][where].astype(jnp.float32) + ins[i][j][half][
                    (k,) + local + (at,)
                ].astype(jnp.float32)
                held[i][where] = total.astype(held[i].dtype)
                return carry

            lax.fori_loop(0, rows // step, body, 0)

    def line_copy(i, k):
        return remote(
            held[i].at[(target(k),) + me.at()],
            line_in[i].at[k],
            ls.at[i, k],
            lr.at[i, k],
            fsdp=target(k),
        )

    def stage(i, k, j):
        if j == 0:
            form(i, k)
        else:
            send(i, k, j - 1)

    def send(i, k, j):
        if j > 0:
            for half in (0, 1):
                plane_copy(i, k, half, j - 1).wait_recv()
                add(i, k, half, j - 1)
        if j < bits:
            for half in (0, 1):
                plane_copy(i, k, half, j).start()
        elif k != 0:
            line_copy(i, k).start()

    def own_copy(i):
        return pltpu.make_async_copy(final[i], outs[i].at[(me.core,) + me.at()], own_sem.at[i])

    def gather_copy(i, half, j):
        order = me.orders[half]
        cols = column_half(final[i], half)
        dst = outs[i].at[(me.core,) + me.at(order[:j]) + (slice(None), cols)]
        src = final[i].at[:, cols] if j == 0 else dst
        return remote(
            src, dst, gs.at[half, i, j], gr.at[half, i, j], ctx=me.across[order[j]]
        )

    def core_copy(i):
        ref = outs[i].at[me.core]
        return remote(ref, ref, cs.at[i], cr.at[i], ctx=me.partner)

    def total(i):
        for k in range(1, nf):
            line_copy(i, k).wait_recv()
        rows = final[i].shape[0]
        step = min(rows, 32)

        def body(t, carry):
            at = pl.ds(pl.multiple_of(t * step, step), step)
            value = held[i][(z,) + me.at() + (at,)].astype(jnp.float32)
            for k in range(1, nf):
                value = value + line_in[i][k, at].astype(jnp.float32)
            final[i][at] = value.astype(final[i].dtype)
            return carry

        lax.fori_loop(0, rows // step, body, 0)
        own_copy(i).start()

    def gather_stage(i, j):
        if j == 0:
            own_copy(i).wait()
        else:
            for half in (0, 1):
                gather_copy(i, half, j - 1).wait_recv()
        if j < bits:
            for half in (0, 1):
                gather_copy(i, half, j).start()
        else:
            core_copy(i).start()

    across = [me.partner] + me.across

    def small_copy(s):
        return remote(small_sum.at[s], small_in.at[s], ss.at[s], sr.at[s], ctx=across[s])

    def small_line_copy(k):
        return remote(
            small_sum.at[bits + 1], small_line.at[z], sls.at[k], slr.at[k], fsdp=target(k)
        )

    def small_stage(s):
        if s > 0:
            small_copy(s - 1).wait_recv()
            small_sum[s] = small_sum[s - 1] + small_in[s - 1]
        if s <= bits:
            small_copy(s).start()
        else:
            for k in range(1, nf):
                small_line_copy(k).start()
            small_line[z] = small_sum[s]

    small_sum[0] = jnp.zeros(small_sum.shape[1:], jnp.float32)
    for r in range(gain_rows):
        small_sum[0, pl.ds(gain_rows + r, 1), :] = ffn_gain_part[:, r * LANES : (r + 1) * LANES]
    jobs = []
    for i in range(count):
        for k in list(range(1, nf)) + [0]:
            job = [functools.partial(stage, i, k, j) for j in range(bits + 2)]
            if k == 0:
                job += [functools.partial(total, i)]
                job += [functools.partial(gather_stage, i, j) for j in range(bits + 1)]
                job += [core_copy(i).wait_recv]
            jobs.append(job)
    back_job = [functools.partial(pair_stage, j) for j in range(bits + 1)]
    back_job += [heads_stage, matmul_stage, norm_stage]
    back_job += [functools.partial(small_stage, s) for s in range(bits + 2)]
    run_ticks(jobs[:1] + [back_job] + jobs[1:])
    for k in range(1, nf):
        small_line_copy(k).wait_recv()
    value = small_line[0]
    for k in range(1, nf):
        value = value + small_line[k]
    small_out[...] = value
    for s in range(bits + 1):
        small_copy(s).wait_send()
    for k in range(1, nf):
        small_line_copy(k).wait_send()
    for i in range(count):
        for k in range(nf):
            for half in (0, 1):
                for j in range(bits):
                    plane_copy(i, k, half, j).wait_send()
            if k:
                line_copy(i, k).wait_send()
        for half in (0, 1):
            for j in range(bits):
                gather_copy(i, half, j).wait_send()
        core_copy(i).wait_send()
    for side, n in order + [("right", rights_count)]:
        (left_copy if side == "left" else right_copy)(n).wait_send()
    pair_core_copy.wait_send()
    for half in (0, 1):
        for j in range(bits):
            pair_copy(half, j).wait_send()
    tokens_grad_store.wait()


BACK_LOADS = 5


def reduce_gradients(nf, nc, pairs, lefts, rights, grad_pair, back, ffn_gain_part):
    _, bits = plane_shape(nc)
    rows = rights[0].shape[0]
    count = len(pairs)
    views = [a.reshape(nf, 2, a.shape[0] // (2 * nf), rows) for a in lefts]
    widths = [b.shape[1] for b in rights] + [back[1].shape[1]]
    pieces = [(lefts[a].shape[0] // (nf * nc), widths[b]) for a, b in pairs]
    pair_rows, pair_width = grad_pair.shape[0] // nc, grad_pair.shape[1]
    pair_view = grad_pair.reshape((2,) * (bits + 1) + (pair_rows, pair_width))
    gain_rows = 2 * ffn_gain_part.shape[1] // LANES + 1
    small = jax.ShapeDtypeStruct((gain_rows + -gain_rows % 8, LANES), jnp.float32)
    outs = pl.pallas_call(
        functools.partial(reduce_kernel, nf, nc, pairs, len(lefts), len(rights)),
        out_shape=[
            jax.ShapeDtypeStruct((2,) * (bits + 1) + piece, jnp.bfloat16) for piece in pieces
        ]
        + [jax.ShapeDtypeStruct(back[4].shape, jnp.float32), small],
        in_specs=[HBM_SPEC] * (len(lefts) + len(rights) + 1 + BACK_LOADS) + [VMEM_SPEC] * 5,
        out_specs=[HBM_SPEC] * (count + 1) + [VMEM_SPEC],
        scratch_shapes=[
            pltpu.VMEM((nf, v.shape[2], 2 * rows), jnp.bfloat16) for v in views
        ]
        + [pltpu.VMEM((2 * rows, n), jnp.bfloat16) for n in widths]
        + [pltpu.VMEM((nf,) + (2,) * bits + piece, jnp.bfloat16) for piece in pieces]
        + [
            pltpu.VMEM((nf,) + (2,) * (bits - 1 - j) + (r, width // 2), jnp.bfloat16)
            for r, width in pieces
            for j in range(bits)
            for _ in (0, 1)
        ]
        + [pltpu.VMEM((nf,) + piece, jnp.bfloat16) for piece in pieces]
        + [pltpu.VMEM(piece, jnp.bfloat16) for piece in pieces]
        + [
            pltpu.VMEM((bits + 2,) + small.shape, jnp.float32),
            pltpu.VMEM((bits + 1,) + small.shape, jnp.float32),
            pltpu.VMEM((nf,) + small.shape, jnp.float32),
        ]
        + [pltpu.VMEM((2,) * bits + (pair_rows, pair_width), jnp.bfloat16)] * 2
        + [
            pltpu.VMEM((2,) * (bits - 1 - j) + (pair_rows, pair_width // 2), jnp.bfloat16)
            for j in range(bits)
            for _ in (0, 1)
        ]
        + [pltpu.VMEM(v.shape, v.dtype) for v in back[:BACK_LOADS]]
        + [pltpu.VMEM(back[4].shape, jnp.float32)]
        + [DMA((BACK_LOADS,)), DMA, DMA, DMA, DMA, DMA((2, bits)), DMA((2, bits))]
        + [DMA((len(lefts),))] * 3
        + [DMA((len(widths),))] * 3
        + [DMA((2, count, nf, bits))] * 2
        + [DMA((count, nf))] * 2
        + [DMA((2, count, bits))] * 2
        + [DMA((count,))] * 2
        + [DMA((count,))]
        + [DMA((bits + 1,))] * 2
        + [DMA((nf,))] * 2,
        compiler_params=pltpu.CompilerParams(
            collective_id=2, has_side_effects=True, vmem_limit_bytes=VMEM_LIMIT
        ),
        name="reduce_gradients",
    )(*views, *rights, pair_view, *back, ffn_gain_part)
    return [
        o.reshape(r * nc, width) for o, (r, width) in zip(outs, pieces)
    ], outs[count], outs[count + 1]


LANES = 128
GROUP = QUERY_HEADS // KEY_VALUE_HEADS
SMEM_SPEC = pl.BlockSpec(memory_space=pltpu.SMEM)


def low_lanes(shape):
    return lax.broadcasted_iota(jnp.int32, shape, len(shape) - 1) % LANES < HEAD_SIZE


def stack_heads(ref, row, group, length, high):
    tiles = []
    for pair in range(GROUP // 2):
        cols = pl.ds((group * GROUP // 2 + pair) * LANES, LANES)
        tile = ref[pl.ds(row, length), cols].astype(jnp.float32)
        turned = pltpu.roll(tile, HEAD_SIZE, 1)
        low = low_lanes(tile.shape)
        if high:
            tiles += [jnp.where(low, 0.0, turned), jnp.where(low, 0.0, tile)]
        else:
            tiles += [jnp.where(low, tile, 0.0), jnp.where(low, turned, 0.0)]
    return jnp.concatenate(tiles, axis=0)


def unstack_heads(ref, row, group, length, value, high):
    for pair in range(GROUP // 2):
        cols = pl.ds((group * GROUP // 2 + pair) * LANES, LANES)
        first = value[2 * pair * length : (2 * pair + 1) * length]
        second = value[(2 * pair + 1) * length : (2 * pair + 2) * length]
        low = low_lanes(first.shape)
        if high:
            tile = jnp.where(low, pltpu.roll(first, HEAD_SIZE, 1), second)
        else:
            tile = jnp.where(low, first, pltpu.roll(second, HEAD_SIZE, 1))
        ref[pl.ds(row, length), cols] = tile.astype(ref.dtype)


def query_span(rank, order, starts, stored_of, which, length):
    block = order[2 * rank + which]
    first = jnp.int32(0)
    place = block * length + lax.broadcasted_iota(jnp.int32, (1, length), 1)
    begin = jnp.zeros((1, length), jnp.int32)
    for d in range(starts.shape[1]):
        first = jnp.where(starts[0, d] <= block * length, starts[0, d], first)
        begin = jnp.where(starts[0, d] <= place, starts[0, d], begin)
    place = jnp.concatenate([place] * GROUP, axis=1)
    begin = jnp.concatenate([begin] * GROUP, axis=1)
    return block, first // length, place, begin


def invert_order(order, stored_of):
    for s in range(order.shape[0]):
        stored_of[order[s]] = s


def key_rows(stored_of, block, length, blocks):
    second = stored_of[jnp.minimum(block + 1, blocks - 1)]
    return [
        pl.ds(pl.multiple_of(s * length, length), length) for s in (stored_of[block], second)
    ]


def allowed_keys(block, place, begin, length):
    key = block * length + lax.broadcasted_iota(jnp.int32, (2 * length, place.shape[1]), 0)
    return (key >= begin) & (key <= place)


def dot_last(left, right):
    return lax.dot_general(
        left, right, (((1,), (1,)), ((), ())), preferred_element_type=jnp.float32
    )


def dot_plain(left, right):
    return lax.dot_general(
        left, right, (((1,), (0,)), ((), ())), preferred_element_type=jnp.float32
    )


def attend_kernel(rank, order, starts, query, pair, attended, exact, log_sum, stored_of, acc, queries):
    length = query.shape[0] // 2
    blocks = order.shape[0]
    invert_order(order, stored_of)

    def one_block(which, carry):
        row = pl.multiple_of(which * length, length)
        block, first, place, begin = query_span(rank[0], order, starts, stored_of, which, length)
        for g in range(KEY_VALUE_HEADS):
            queries[g] = stack_heads(query, row, g, length, False).astype(jnp.bfloat16)
        acc[...] = jnp.zeros_like(acc)

        def step(t, carry):
            key_block = first + 2 * t
            rows = key_rows(stored_of, key_block, length, blocks)
            allowed = allowed_keys(key_block, place, begin, length)
            for g in range(KEY_VALUE_HEADS):
                cols = pl.ds(g * LANES, LANES)
                keys = jnp.concatenate([pair[r, cols] for r in rows], axis=0)
                scores = dot_last(keys, queries[g])
                weights = jnp.where(allowed, jnp.exp(scores), 0.0).astype(jnp.bfloat16)
                ones = jnp.where(low_lanes(keys.shape), 1.0, keys.astype(jnp.float32))
                acc[g] += dot_plain(ones.T.astype(jnp.bfloat16), weights)
            return carry

        lax.fori_loop(0, (block - first + 2) // 2, step, 0)
        for g in range(KEY_VALUE_HEADS):
            total = acc[g]
            sums = total[0:1]
            log_sum[which, g] = jnp.broadcast_to(jnp.log(sums), log_sum.shape[2:])
            value = (total / sums).T
            unstack_heads(attended, row, g, length, value, True)
            unstack_heads(exact, row, g, length, value, True)
        return carry

    lax.fori_loop(0, 2, one_block, 0)


def attend(rank, order, starts, query, pair):
    rows = query.shape[0]
    wide = GROUP * (rows // 2)
    return pl.pallas_call(
        attend_kernel,
        out_shape=[
            jax.ShapeDtypeStruct(query.shape, jnp.bfloat16),
            jax.ShapeDtypeStruct(query.shape, jnp.float32),
            jax.ShapeDtypeStruct((2, KEY_VALUE_HEADS, 8, wide), jnp.float32),
        ],
        in_specs=[SMEM_SPEC] * 3 + [VMEM_SPEC] * 2,
        out_specs=[VMEM_SPEC] * 3,
        scratch_shapes=[
            pltpu.SMEM((order.shape[0],), jnp.int32),
            pltpu.VMEM((KEY_VALUE_HEADS, LANES, wide), jnp.float32),
            pltpu.VMEM((KEY_VALUE_HEADS, wide, LANES), jnp.bfloat16),
        ],
        name="attend",
    )(rank, order, starts, query, pair)


def attend_back_kernel(
    rank, order, starts, query, pair, grad, exact, log_sum, grad_query, grad_pair,
    stored_of, total, acc, queries, grads, delta,
):
    length = query.shape[0] // 2
    blocks = order.shape[0]
    invert_order(order, stored_of)
    total[...] = jnp.zeros_like(total)

    def one_block(which, carry):
        row = pl.multiple_of(which * length, length)
        block, first, place, begin = query_span(rank[0], order, starts, stored_of, which, length)
        for g in range(KEY_VALUE_HEADS):
            queries[g] = stack_heads(query, row, g, length, False).astype(jnp.bfloat16)
            upper = stack_heads(grad, row, g, length, True)
            grads[g] = upper.astype(jnp.bfloat16)
            product = upper * stack_heads(exact, row, g, length, True)
            delta[g] = jnp.broadcast_to(
                jnp.sum(product.T, axis=0, keepdims=True), delta.shape[1:]
            )
        acc[...] = jnp.zeros_like(acc)

        def step(t, carry):
            key_block = first + 2 * t
            rows = key_rows(stored_of, key_block, length, blocks)
            allowed = allowed_keys(key_block, place, begin, length)
            for g in range(KEY_VALUE_HEADS):
                cols = pl.ds(g * LANES, LANES)
                keys = jnp.concatenate([pair[r, cols] for r in rows], axis=0)
                scores = dot_last(keys, queries[g])
                probs = jnp.where(allowed, jnp.exp(scores - log_sum[which, g, 0:1]), 0.0)
                grad_probs = dot_last(keys, grads[g])
                grad_scores = (probs * (grad_probs - delta[g, 0:1])).astype(jnp.bfloat16)
                turned = keys.astype(jnp.float32).T.astype(jnp.bfloat16)
                acc[g] += dot_plain(turned, grad_scores)
                both = dot_plain(grad_scores, queries[g]) + dot_plain(
                    probs.astype(jnp.bfloat16), grads[g]
                )
                total[rows[0], cols] += both[:length]
                total[rows[1], cols] += both[length:]
            return carry

        lax.fori_loop(0, (block - first + 2) // 2, step, 0)
        for g in range(KEY_VALUE_HEADS):
            unstack_heads(grad_query, row, g, length, acc[g].T, False)
        return carry

    lax.fori_loop(0, 2, one_block, 0)

    def finish(t, carry):
        at = pl.ds(pl.multiple_of(t * length, length), length)
        grad_pair[at, :] = total[at, :].astype(grad_pair.dtype)
        return carry

    lax.fori_loop(0, blocks, finish, 0)


def attend_back(rank, order, starts, query, pair, grad, exact, log_sum):
    rows = query.shape[0]
    wide = GROUP * (rows // 2)
    return pl.pallas_call(
        attend_back_kernel,
        out_shape=[
            jax.ShapeDtypeStruct(query.shape, jnp.float32),
            jax.ShapeDtypeStruct(pair.shape, jnp.bfloat16),
        ],
        in_specs=[SMEM_SPEC] * 3 + [VMEM_SPEC] * 5,
        out_specs=[VMEM_SPEC] * 2,
        scratch_shapes=[
            pltpu.SMEM((order.shape[0],), jnp.int32),
            pltpu.VMEM(pair.shape, jnp.float32),
            pltpu.VMEM((KEY_VALUE_HEADS, LANES, wide), jnp.float32),
            pltpu.VMEM((KEY_VALUE_HEADS, wide, LANES), jnp.bfloat16),
            pltpu.VMEM((KEY_VALUE_HEADS, wide, LANES), jnp.bfloat16),
            pltpu.VMEM((KEY_VALUE_HEADS, 8, wide), jnp.float32),
        ],
        name="attend_back",
    )(rank, order, starts, query, pair, grad, exact, log_sum)


CHUNK = 256


def head_means(values):
    shape = (LANES, LANES)
    same = (
        lax.broadcasted_iota(jnp.int32, shape, 0) // HEAD_SIZE
        == lax.broadcasted_iota(jnp.int32, shape, 1) // HEAD_SIZE
    )
    ones = jnp.where(same, 1.0, 0.0).astype(jnp.bfloat16)
    high = values.astype(jnp.bfloat16)
    low = (values - high.astype(jnp.float32)).astype(jnp.bfloat16)
    return (dot_plain(high, ones) + dot_plain(low, ones)) * (1.0 / HEAD_SIZE)


def first_quarter(shape):
    return lax.broadcasted_iota(jnp.int32, shape, len(shape) - 1) % HEAD_SIZE < HEAD_SIZE // 2


def turn(values, cosines, sines, sign):
    half = HEAD_SIZE // 2
    ahead = pltpu.roll(values, LANES - half, 1)
    behind = pltpu.roll(values, half, 1)
    other = jnp.where(first_quarter(values.shape), -ahead, behind)
    return values * cosines + sign * other * sines


def row_inverse(ref, rows):
    total = jnp.zeros((rows, 1), jnp.float32)
    width = ref.shape[1]
    for j in range(0, width, CHUNK):
        value = ref[:, j : j + CHUNK].astype(jnp.float32)
        total = total + jnp.sum(value * value, axis=1, keepdims=True)
    return lax.rsqrt(total * (1.0 / width) + EPSILON)


def project_kernel(
    rank, order, starts, tokens, weight, gain, qk_gain, frequency,
    normed_turned, raw, query, pair, cosines, sines,
    normed,
):
    rows = tokens.shape[0]
    length = rows // 2
    for which in (0, 1):
        block = order[2 * rank[0] + which]
        place = block * length + lax.broadcasted_iota(jnp.int32, (length, LANES), 0)
        begin = jnp.zeros((length, LANES), jnp.int32)
        for d in range(starts.shape[1]):
            begin = jnp.where(starts[0, d] <= place, starts[0, d], begin)
        angle = (place - begin).astype(jnp.float32) * frequency[...]
        at = pl.ds(which * length, length)
        cosines[at, :] = jnp.cos(angle)
        sines[at, :] = jnp.sin(angle)
    inverse = row_inverse(tokens, rows)
    for j in range(0, tokens.shape[1], CHUNK):
        cols = pl.ds(j, CHUNK)
        value = tokens[:, cols].astype(jnp.float32) * inverse * gain[:, cols]
        normed[:, cols] = value.astype(jnp.bfloat16)
        normed_turned[cols, :] = value.T.astype(jnp.bfloat16)
    query_width = QUERY_HEADS * HEAD_SIZE
    key_width = KEY_VALUE_HEADS * HEAD_SIZE

    def head_turn(cols, which):
        value = raw[:, cols]
        scale = lax.rsqrt(head_means(value * value) + EPSILON)
        return turn(value * scale * qk_gain[which : which + 1, :], cosines[...], sines[...], 1.0)

    for j in range(0, weight.shape[1], CHUNK):
        raw[:, j : j + CHUNK] = dot_plain(normed[...], weight[:, j : j + CHUNK])
    for j in range(0, query_width, LANES):
        cols = pl.ds(j, LANES)
        query[:, cols] = (head_turn(cols, 0) * HEAD_SIZE**-0.5).astype(jnp.bfloat16)
    for j in range(0, key_width, LANES):
        key = head_turn(pl.ds(query_width + j, LANES), 1)
        value = raw[:, query_width + key_width + j : query_width + key_width + j + LANES]
        low = low_lanes(key.shape)
        first = jnp.where(low, key, pltpu.roll(value, HEAD_SIZE, 1))
        second = jnp.where(low, pltpu.roll(key, HEAD_SIZE, 1), value)
        pair[:, 2 * j : 2 * j + LANES] = first.astype(jnp.bfloat16)
        pair[:, 2 * j + LANES : 2 * j + 2 * LANES] = second.astype(jnp.bfloat16)


def project(rank, order, starts, tokens, weight, gain, qk_gain, frequency):
    rows, width = tokens.shape
    shape = jax.ShapeDtypeStruct
    return pl.pallas_call(
        project_kernel,
        out_shape=[
            shape((width, rows), jnp.bfloat16),
            shape((rows, weight.shape[1]), jnp.float32),
            shape((rows, QUERY_HEADS * HEAD_SIZE), jnp.bfloat16),
            shape((rows, 2 * KEY_VALUE_HEADS * HEAD_SIZE), jnp.bfloat16),
            shape((rows, LANES), jnp.float32),
            shape((rows, LANES), jnp.float32),
        ],
        in_specs=[SMEM_SPEC] * 3 + [VMEM_SPEC] * 5,
        out_specs=[VMEM_SPEC] * 6,
        scratch_shapes=[pltpu.VMEM((rows, width), jnp.bfloat16)],
        name="project",
    )(rank, order, starts, tokens, weight, gain, qk_gain, frequency)


def feed_kernel(
    tokens, cotangent, attended, gain, w_out, w_gate, w_up, w_down,
    mixed, normed_turned, hidden_turned, attended_turned, grad_gate, grad_up, grad_resid, grad_branch,
    grad_attended, gain_grad,
    out_v, gate_v, up_v, down_v, resid, normed, hidden, sems,
):
    rows, width = tokens.shape
    loads = [
        pltpu.make_async_copy(src, dst, sems.at[i])
        for i, (src, dst) in enumerate(
            ((w_out, out_v), (w_gate, gate_v), (w_up, up_v), (w_down, down_v))
        )
    ]
    for load in loads:
        load.start()
    loads[0].wait()
    for j in range(0, width, CHUNK):
        cols = pl.ds(j, CHUNK)
        resid[:, cols] = tokens[:, cols].astype(jnp.float32) + dot_plain(
            attended[...], out_v[:, cols]
        )
    inverse = row_inverse(resid, rows)
    for j in range(0, width, CHUNK):
        cols = pl.ds(j, CHUNK)
        value = resid[:, cols] * inverse * gain[:, cols]
        normed[:, cols] = value.astype(jnp.bfloat16)
        normed_turned[cols, :] = value.T.astype(jnp.bfloat16)
    for load in loads[1:]:
        load.wait()
    for j in range(0, gate_v.shape[1], CHUNK):
        cols = pl.ds(j, CHUNK)
        gate = dot_plain(normed[...], gate_v[:, cols])
        up = dot_plain(normed[...], up_v[:, cols])
        sigmoid = 1.0 / (1.0 + jnp.exp(-gate))
        inner = gate * sigmoid * up
        hidden[:, cols] = inner.astype(jnp.bfloat16)
        hidden_turned[cols, :] = inner.T.astype(jnp.bfloat16)
        grad_hidden = dot_last(cotangent[...], down_v[cols, :])
        grad_gate[:, cols] = (
            grad_hidden * up * sigmoid * (1.0 + gate * (1.0 - sigmoid))
        ).astype(jnp.bfloat16)
        grad_up[:, cols] = (grad_hidden * gate * sigmoid).astype(jnp.bfloat16)
    mean = jnp.zeros((rows, 1), jnp.float32)
    for j in range(0, width, CHUNK):
        cols = pl.ds(j, CHUNK)
        mixed[:, cols] = (resid[:, cols] + dot_plain(hidden[...], down_v[:, cols])).astype(
            jnp.bfloat16
        )
        grad = dot_last(grad_gate[...], gate_v[cols, :]) + dot_last(grad_up[...], up_v[cols, :])
        grad_resid[:, cols] = grad
        mean = mean + jnp.sum(grad * gain[:, cols] * resid[:, cols], axis=1, keepdims=True)
    mean = mean * (1.0 / width) * inverse * inverse
    for j in range(0, width, CHUNK):
        cols = pl.ds(j, CHUNK)
        grad = grad_resid[:, cols]
        value = resid[:, cols]
        gain_grad[:, cols] = jnp.sum(grad * value * inverse, axis=0, keepdims=True)
        total = cotangent[:, cols].astype(jnp.float32) + inverse * (
            grad * gain[:, cols] - value * mean
        )
        grad_resid[:, cols] = total
        grad_branch[:, cols] = total.astype(jnp.bfloat16)
    for j in range(0, attended.shape[1], CHUNK):
        cols = pl.ds(j, CHUNK)
        attended_turned[cols, :] = attended[:, cols].astype(jnp.float32).T.astype(jnp.bfloat16)
        grad_attended[:, cols] = dot_last(grad_branch[...], out_v[cols, :]).astype(jnp.bfloat16)


def feed(tokens, cotangent, attended, gain, w_out, w_gate, w_up, w_down):
    rows, width = tokens.shape
    inner = w_gate.shape[1]
    shape = jax.ShapeDtypeStruct
    low, full = jnp.bfloat16, jnp.float32
    return pl.pallas_call(
        feed_kernel,
        out_shape=[
            shape((rows, width), low),
            shape((width, rows), low),
            shape((inner, rows), low),
            shape((attended.shape[1], rows), low),
            shape((rows, inner), low),
            shape((rows, inner), low),
            shape((rows, width), full),
            shape((rows, width), low),
            shape(attended.shape, low),
            shape((1, width), full),
        ],
        in_specs=[VMEM_SPEC] * 4 + [HBM_SPEC] * 4,
        out_specs=[VMEM_SPEC] * 10,
        scratch_shapes=[pltpu.VMEM(w.shape, low) for w in (w_out, w_gate, w_up, w_down)]
        + [
            pltpu.VMEM((rows, width), full),
            pltpu.VMEM((rows, width), low),
            pltpu.VMEM((rows, inner), low),
            DMA((4,)),
        ],
        name="feed",
    )(tokens, cotangent, attended, gain, w_out, w_gate, w_up, w_down)


def pack_rows(arrays, multiple):
    flat = jnp.concatenate([a.astype(jnp.float32).reshape(-1) for a in arrays])
    size = multiple * 128
    return jnp.pad(flat, (0, -flat.shape[0] % size)).reshape(-1, 128)


def per_device(
    tokens,
    cotangent,
    doc_starts,
    deal_order,
    query_key_value_weight,
    w_out,
    w_gate,
    w_up,
    w_down,
    gain_attn,
    gain_ffn,
    gain_qk,
):
    ctx_count = lax.axis_size("ctx")
    fsdp_count = lax.axis_size("fsdp")
    ctx_rank = lax.axis_index("ctx")
    fsdp_rank = lax.axis_index("fsdp")
    model_shard = gain_attn.shape[0]
    qk_shard = gain_qk.shape[1]
    model = model_shard * fsdp_count
    gains = pack_rows([gain_attn, gain_ffn, gain_qk], 8)
    (qkv_full, out_full, gate_full, up_full, down_full), gains = gather_weights(
        fsdp_count, ctx_count, [query_key_value_weight, w_out, w_gate, w_up, w_down], gains
    )
    gains = gains.reshape(fsdp_count, -1)
    attn_gain = gains[:, :model_shard].reshape(1, model)
    ffn_gain = gains[:, model_shard : 2 * model_shard].reshape(1, model)
    qk_gain = gains[:, 2 * model_shard : 2 * model_shard + 2 * qk_shard]
    qk_gain = jnp.swapaxes(qk_gain.reshape(fsdp_count, 2, qk_shard), 0, 1).reshape(2, HEAD_SIZE)
    qk_gain = jnp.concatenate([qk_gain, qk_gain], axis=1)
    pack_in = tokens[0]
    grad_mixed = cotangent[0]
    token_rows = pack_in.shape[0]
    rank = ctx_rank.reshape(1).astype(jnp.int32)
    frequency = THETA ** (-jnp.arange(0, HEAD_SIZE // 2, dtype=jnp.float32) * 2.0 / HEAD_SIZE)
    frequency = jnp.concatenate([frequency] * (2 * LANES // HEAD_SIZE)).reshape(1, LANES)

    normed, raw, query, local_pair, cosines, sines = project(
        rank, deal_order, doc_starts, pack_in, qkv_full, attn_gain, qk_gain, frequency
    )
    pair = gather_pair(fsdp_count, ctx_count, local_pair)
    attended, exact, log_sum = attend(rank, deal_order, doc_starts, query, pair)
    (
        mixed_out,
        normed_ffn,
        hidden,
        attended_turned,
        grad_gate,
        grad_up,
        grad_resid,
        grad_branch,
        grad_attended,
        ffn_gain_part,
    ) = feed(pack_in, grad_mixed, attended, ffn_gain, out_full, gate_full, up_full, down_full)
    grad_query, grad_pair = attend_back(
        rank, deal_order, doc_starts, query, pair, grad_attended, exact, log_sum
    )
    (down_grad, gate_grad, up_grad, out_grad, qkv_grad), tokens_grad, gain_sums = reduce_gradients(
        fsdp_count,
        ctx_count,
        ((0, 0), (1, 1), (1, 2), (2, 3), (3, 4)),
        [hidden, normed_ffn, attended_turned, normed],
        [grad_mixed, grad_gate, grad_up, grad_branch],
        grad_pair,
        [
            pack_in,
            qkv_full,
            raw,
            grad_query,
            grad_resid,
            attn_gain,
            qk_gain,
            cosines,
            sines,
        ],
        ffn_gain_part,
    )
    gain_sums = gain_sums.reshape(-1)
    attn_gain_grad = lax.dynamic_slice_in_dim(gain_sums, fsdp_rank * model_shard, model_shard)
    ffn_gain_grad = lax.dynamic_slice_in_dim(
        gain_sums, model + fsdp_rank * model_shard, model_shard
    )
    qk_gain_grad = lax.dynamic_slice_in_dim(
        gain_sums[2 * model : 2 * model + 2 * HEAD_SIZE].reshape(2, HEAD_SIZE),
        fsdp_rank * qk_shard,
        qk_shard,
        axis=1,
    )
    return (
        mixed_out[None],
        tokens_grad[None],
        qkv_grad.astype(jnp.float32),
        out_grad.astype(jnp.float32),
        gate_grad.astype(jnp.float32),
        up_grad.astype(jnp.float32),
        down_grad.astype(jnp.float32),
        attn_gain_grad,
        ffn_gain_grad,
        qk_gain_grad,
    )


def solution(mesh):
    return jax.shard_map(
        per_device,
        mesh=mesh,
        in_specs=(
            P("fsdp", "ctx", None),
            P("fsdp", "ctx", None),
            P("fsdp", None),
            P(),
            P("fsdp", None),
            P("fsdp", None),
            P("fsdp", None),
            P("fsdp", None),
            P("fsdp", None),
            P("fsdp"),
            P("fsdp"),
            P(None, "fsdp"),
        ),
        out_specs=(
            P("fsdp", "ctx", None),
            P("fsdp", "ctx", None),
            P("fsdp", None),
            P("fsdp", None),
            P("fsdp", None),
            P("fsdp", None),
            P("fsdp", None),
            P("fsdp"),
            P("fsdp"),
            P(None, "fsdp"),
        ),
        check_vma=False,
    )
```

```python
import functools

import jax
import jax.numpy as jnp
from jax import lax
from jax.experimental import pallas as pl
from jax.experimental.pallas import tpu as pltpu
from jax.sharding import PartitionSpec as P

QUERY_HEADS = 16
KEY_VALUE_HEADS = 4
HEAD_SIZE = 64


EPSILON = 1e-06
THETA = 10000.0

MESH = pl.DeviceIdType.MESH
DMA = pltpu.SemaphoreType.DMA
HBM_SPEC = pl.BlockSpec(memory_space=pl.ANY)
VMEM_SPEC = pl.BlockSpec(memory_space=pltpu.VMEM)
SPACING = 2
VMEM_LIMIT = 67043328


def plane_shape(ctx_count):
    chips = ctx_count // 2
    bits = chips.bit_length() - 1
    assert 2**bits == chips and ctx_count == 2 * chips
    return chips, bits


class Place:
    def __init__(self, ctx_count, fsdp_count):
        self.chips, self.bits = plane_shape(ctx_count)
        self.fsdp_count = fsdp_count
        self.ctx = lax.axis_index("ctx")
        self.z = lax.axis_index("fsdp")
        self.core = self.ctx % 2
        chip = self.ctx // 2
        self.bit = [(chip // 2**j) % 2 for j in range(self.bits)]
        self.across = [self.ctx + (1 - 2 * self.bit[j]) * 2 * 2**j for j in range(self.bits)]
        self.partner = self.ctx + 1 - 2 * self.core
        self.orders = (list(range(self.bits)), list(reversed(range(self.bits))))

    def at(self, free=(), other=None):
        return tuple(
            slice(None) if j in free else (1 - self.bit[j] if j == other else self.bit[j])
            for j in reversed(range(self.bits))
        )

    def barrier(self, plane=True, line=True, near=False):
        sem = pltpu.get_barrier_semaphore()
        count = 0
        if plane:
            for p in self.across + [self.partner]:
                pl.semaphore_signal(sem, inc=1, device_id={"ctx": p}, device_id_type=MESH)
                count += 1
        if line:
            for k in range(1, self.fsdp_count):
                pl.semaphore_signal(
                    sem,
                    inc=1,
                    device_id={"fsdp": (self.z + k) % self.fsdp_count},
                    device_id_type=MESH,
                )
                count += 1
        pl.semaphore_wait(sem, count)


def remote(src, dst, send, recv, **where):
    return pltpu.make_async_remote_copy(
        src, dst, send, recv, device_id=where, device_id_type=MESH
    )


def run_ticks(jobs, spacing=SPACING):
    depth = max(len(job) for job in jobs)
    for tick in range(len(jobs) + spacing * (depth - 1)):
        for j in reversed(range(depth)):
            t = tick - spacing * j
            if 0 <= t < len(jobs) and j < len(jobs[t]):
                jobs[t][j]()


def column_half(ref, half):
    n = ref.shape[-1] // 2
    return pl.ds(half * n, n)


def gather_kernel(nf, nc, count, *refs):
    rest = list(refs)

    def take(n):
        return [rest.pop(0) for _ in range(n)]

    shards, (small, tokens, order_of, starts, frequency) = take(count), take(5)
    outs, (attn_gain, ffn_gain, qk_gain) = take(count), take(3)
    normed_turned, raw, query, cosines, sines, pair = take(6)
    weight, small_v, normed, pair_v, *stages = take(count + 3)
    up_s, up_r, down_s, down_r, ps, pr, cs, cr, ss, sr, load_sem, store_sem = take(12)
    pps, ppr, pcs, pcr, pair_sem = rest
    first_out = outs[0]
    outs = [weight] + list(outs[1:])
    me = Place(nc, nf)
    z = me.z
    loads = [
        pltpu.make_async_copy(
            shards[i], weight.at[z] if i == 0 else stages[i - 1], load_sem.at[i]
        )
        for i in range(count)
    ]
    stores = [
        pltpu.make_async_copy(stages[i - 1], outs[i].at[z], store_sem.at[i])
        for i in range(1, count)
    ]
    weight_store = pltpu.make_async_copy(weight, first_out, store_sem.at[0])
    for load in loads:
        load.start()
    me.barrier()

    def source(k):
        pairs = jnp.minimum(z, nf - 1 - z)
        near = (k + 1) // 2
        near_source = z - near if k % 2 == 1 else z + near
        far = k - pairs
        far_source = jnp.where(2 * z < nf - 1, z + far, z - far)
        return jnp.where(k <= 2 * pairs, near_source, far_source)

    sources = [None] + [source(k) for k in range(1, nf)]

    def line_copy(i, src_z, src, up):
        to = z + 1 if up else z - 1
        sems = (up_s, up_r) if up else (down_s, down_r)
        return remote(
            src,
            outs[i].at[(src_z, me.core) + me.at()],
            sems[0].at[i, src_z],
            sems[1].at[i, src_z],
            fsdp=to,
        )

    def line_start(i, src_z, src, up, condition):
        @pl.when(condition)
        def _():
            line_copy(i, src_z, src, up).start()

    def small_copy(k):
        return remote(small, small_v.at[z], ss.at[k], sr.at[k], fsdp=(z + k) % nf)

    def own_start(i):
        mine = shards[i].at[(me.core,) + me.at()]
        line_start(i, z, mine, True, z + 1 < nf)
        line_start(i, z, mine, False, z > 0)

    for k in range(1, nf):
        small_copy(k).start()
    for i in range(min(AHEAD, count)):
        own_start(i)
    small_v[z] = small[...]

    def line_stage(i, k):
        src_z = sources[k]
        here = outs[i].at[(src_z, me.core) + me.at()]
        below = src_z < z

        @pl.when(below)
        def _():
            line_copy(i, src_z, here, True).wait_recv()

        @pl.when(jnp.logical_not(below))
        def _():
            line_copy(i, src_z, here, False).wait_recv()

        line_start(i, src_z, here, True, jnp.logical_and(below, z + 1 < nf))
        line_start(i, src_z, here, False, jnp.logical_and(src_z > z, z > 0))
        if k == nf - 1 and i + AHEAD < count:
            own_start(i + AHEAD)

    def plane_copy(i, k, half, j):
        order = me.orders[half]
        ref = outs[i].at[
            (sources[k], me.core) + me.at(order[:j]) + (slice(None), column_half(outs[i], half))
        ]
        return remote(
            ref, ref, ps.at[half, i, k, j], pr.at[half, i, k, j], ctx=me.across[order[j]]
        )

    def core_copy(i, k):
        ref = outs[i].at[sources[k], me.core]
        return remote(ref, ref, cs.at[i, k], cr.at[i, k], ctx=me.partner)

    def plane_stage(i, k, j):
        if j == 0:
            line_stage(i, k)
        else:
            for half in (0, 1):
                plane_copy(i, k, half, j - 1).wait_recv()
        if j < me.bits:
            for half in (0, 1):
                plane_copy(i, k, half, j).start()
        else:
            core_copy(i, k).start()

    order = [(i, k) for i in range(count) for k in range(1, nf)]
    jobs = [
        [functools.partial(plane_stage, i, k, j) for j in range(me.bits + 1)]
        + [core_copy(i, k).wait_recv]
        for i, k in order
    ]
    rows = tokens.shape[0]
    length = rows // 2
    width = tokens.shape[1]
    query_width = QUERY_HEADS * HEAD_SIZE
    key_width = KEY_VALUE_HEADS * HEAD_SIZE

    def angle_stage():
        for which in (0, 1):
            block = order_of[2 * me.ctx + which]
            place = block * length + lax.broadcasted_iota(jnp.int32, (length, LANES), 0)
            begin = jnp.zeros((length, LANES), jnp.int32)
            for d in range(starts.shape[1]):
                begin = jnp.where(starts[0, d] <= place, starts[0, d], begin)
            angle = (place - begin).astype(jnp.float32) * frequency[...]
            at = pl.ds(which * length, length)
            cosines[at, :] = jnp.cos(angle)
            sines[at, :] = jnp.sin(angle)

    def norm_stage():
        for k in range(1, nf):
            small_copy(k).wait_recv()
        per = width // nf // LANES
        for c in range(width // LANES):
            cols = pl.ds(c * LANES, LANES)
            attn_gain[:, cols] = small_v[c // per, pl.ds(c % per, 1), :]
            ffn_gain[:, cols] = small_v[c // per, pl.ds(per + c % per, 1), :]
        value = small_v[0, pl.ds(2 * per, 2), :]
        for k in range(1, nf):
            value = value + small_v[k, pl.ds(2 * per, 2), :]
        qk_gain[...] = value
        inverse = row_inverse(tokens, rows)
        for j in range(0, width, CHUNK):
            cols = pl.ds(j, CHUNK)
            value = tokens[:, cols].astype(jnp.float32) * inverse * attn_gain[:, cols]
            normed[:, cols] = value.astype(jnp.bfloat16)
            normed_turned[cols, :] = value.T.astype(jnp.bfloat16)

    def matmul_stage():
        weight_store.start()
        for j in range(0, raw.shape[1], CHUNK):
            cols = weight[..., pl.ds(j, CHUNK)].reshape(width, CHUNK)
            raw[:, j : j + CHUNK] = dot_plain(normed[...], cols)

    def head_turn(cols, which):
        value = raw[:, cols]
        scale = lax.rsqrt(head_means(value * value) + EPSILON)
        return turn(value * scale * qk_gain[which : which + 1, :], cosines[...], sines[...], 1.0)

    def key_stage():
        for j in range(0, key_width, LANES):
            key = head_turn(pl.ds(query_width + j, LANES), 1)
            value = raw[:, query_width + key_width + j : query_width + key_width + j + LANES]
            low = low_lanes(key.shape)
            first = jnp.where(low, key, pltpu.roll(value, HEAD_SIZE, 1))
            second = jnp.where(low, pltpu.roll(key, HEAD_SIZE, 1), value)
            pair_v[:, 2 * j : 2 * j + LANES] = first.astype(jnp.bfloat16)
            pair_v[:, 2 * j + LANES : 2 * j + 2 * LANES] = second.astype(jnp.bfloat16)
        for half in (0, 1):
            pair_copy(half, 0).start()
        pair_own_core.start()
        pair_store.start()

    def query_stage():
        for j in range(0, query_width, LANES):
            cols = pl.ds(j, LANES)
            query[:, cols] = (head_turn(cols, 0) * HEAD_SIZE**-0.5).astype(jnp.bfloat16)

    def pair_copy(half, j):
        order = me.orders[half]
        where = (slice(None), column_half(pair, half))
        dst = pair.at[me.at(order[:j]) + (me.core,) + where]
        src = pair_v.at[where] if j == 0 else dst
        return remote(src, dst, pps.at[half, j], ppr.at[half, j], ctx=me.across[order[j]])

    pair_own_core = remote(
        pair_v, pair.at[me.at() + (me.core,)], pcs.at[0, 0], pcr.at[0, 0], ctx=me.partner
    )
    pair_store = pltpu.make_async_copy(pair_v, pair.at[me.at() + (me.core,)], pair_sem)

    def pair_core_copy(half, j):
        order = me.orders[half]
        where = me.at(order[:j], other=order[j])
        ref = pair.at[where + (me.core, slice(None), column_half(pair, half))]
        return remote(ref, ref, pcs.at[half, j + 1], pcr.at[half, j + 1], ctx=me.partner)

    def pair_stage(j):
        if j == 0:
            pair_store.wait()
        for half in (0, 1):
            pair_copy(half, j).wait_recv()
        if j + 1 < me.bits:
            for half in (0, 1):
                pair_copy(half, j + 1).start()
        for half in (0, 1):
            pair_core_copy(half, j).start()

    def pause():
        pass

    project_job = [norm_stage] + [pause] * me.bits
    project_job += [matmul_stage, key_stage]
    project_job += [functools.partial(pair_stage, j) for j in range(me.bits)]
    angle_stage()
    for load in loads:
        load.wait()
    for store in stores:
        store.start()
    run_ticks(jobs[: nf - 1] + [project_job] + jobs[nf - 1 :])
    query_stage()
    for k in range(1, nf):
        small_copy(k).wait_send()
    pair_own_core.wait()
    for j in range(me.bits):
        for half in (0, 1):
            pair_copy(half, j).wait_send()
            pair_core_copy(half, j).wait()
    weight_store.wait()
    for i in range(count):
        @pl.when(z + 1 < nf)
        def _():
            line_copy(i, z, shards[i].at[(me.core,) + me.at()], True).wait_send()

        @pl.when(z > 0)
        def _():
            line_copy(i, z, shards[i].at[(me.core,) + me.at()], False).wait_send()

    for i, k in order:
        src_z = sources[k]
        here = outs[i].at[(src_z, me.core) + me.at()]

        @pl.when(jnp.logical_and(src_z < z, z + 1 < nf))
        def _():
            line_copy(i, src_z, here, True).wait_send()

        @pl.when(jnp.logical_and(src_z > z, z > 0))
        def _():
            line_copy(i, src_z, here, False).wait_send()

        for half in (0, 1):
            for j in range(me.bits):
                plane_copy(i, k, half, j).wait_send()
        core_copy(i, k).wait_send()
    for store in stores:
        store.wait()


AHEAD = 2


def gather_weights(nf, nc, shards, small, tokens, order, starts, frequency):
    _, bits = plane_shape(nc)
    count = len(shards)
    rows, width = tokens.shape
    shape = jax.ShapeDtypeStruct
    low, full = jnp.bfloat16, jnp.float32
    query_width = QUERY_HEADS * HEAD_SIZE
    pair_width = 2 * KEY_VALUE_HEADS * HEAD_SIZE
    views = [w.reshape((2,) * (1 + bits) + (w.shape[0] // nc, w.shape[1])) for w in shards]
    outs = pl.pallas_call(
        functools.partial(gather_kernel, nf, nc, count),
        out_shape=[shape((nf,) + v.shape, v.dtype) for v in views]
        + [
            shape((1, width), full),
            shape((1, width), full),
            shape((2, LANES), full),
            shape((width, rows), low),
            shape((rows, shards[0].shape[1]), full),
            shape((rows, query_width), low),
            shape((rows, LANES), full),
            shape((rows, LANES), full),
            shape((2,) * (bits + 1) + (rows, pair_width), low),
        ],
        in_specs=[HBM_SPEC] * count + [VMEM_SPEC] * 2 + [SMEM_SPEC] * 2 + [VMEM_SPEC],
        out_specs=[HBM_SPEC] * count + [VMEM_SPEC] * 8 + [HBM_SPEC],
        scratch_shapes=[
            pltpu.VMEM((nf,) + views[0].shape, low),
            pltpu.VMEM((nf,) + small.shape, full),
            pltpu.VMEM((rows, width), low),
            pltpu.VMEM((rows, pair_width), low),
        ]
        + [pltpu.VMEM(v.shape, v.dtype) for v in views[1:]]
        + [DMA((count, nf))] * 4
        + [DMA((2, count, nf, bits))] * 2
        + [DMA((count, nf))] * 2
        + [DMA((nf,))] * 2
        + [DMA((count,))] * 2
        + [DMA((2, bits))] * 2
        + [DMA((2, bits + 1))] * 2
        + [DMA],
        compiler_params=pltpu.CompilerParams(
            collective_id=0, has_side_effects=True, vmem_limit_bytes=VMEM_LIMIT
        ),
        name="gather_weights",
    )(*views, small, tokens, order, starts, frequency)
    full_weights = [o.reshape(nf * w.shape[0], w.shape[1]) for o, w in zip(outs, shards)]
    return full_weights, outs[count:-1], outs[-1].reshape(nc * rows, pair_width)


def reduce_kernel(nf, nc, pairs, lefts_count, rights_count, *refs):
    _, bits = plane_shape(nc)
    count = len(pairs)
    rest = list(refs)

    def take(n):
        return [rest.pop(0) for _ in range(n)]

    lefts, rights = take(lefts_count), take(rights_count)
    grad_pair, back_in = take(1)[0], take(BACK_LOADS)
    gain, qk_gain, cosines, sines, ffn_gain_part = take(5)
    outs, (tokens_grad, small_out) = take(count), take(2)
    left_v, right_v, held = take(lefts_count), take(rights_count + 1), take(count)
    ins = [[take(2) for _ in range(bits)] for _ in range(count)]
    line_in, final = take(count), take(count)
    small_sum, small_in, small_line = take(3)
    pair_held, pair_core, *pair_in = take(2 + 2 * bits)
    back_v, grads = take(BACK_LOADS), take(1)[0]
    back_sem, grad_sem, pl_sem, pcs, pcr, pps, ppr = take(7)
    (ll, lls, llr, rl, rls, rlr, ps, pr, ls, lr, gs, gr, cs, cr, own_sem, ss, sr, sls, slr) = rest
    me = Place(nc, nf)
    z = me.z
    rows = rights[0].shape[0]
    projected_v = right_v[rights_count]
    back_loads = [
        pltpu.make_async_copy(src, dst, back_sem.at[n])
        for n, (src, dst) in enumerate(zip(back_in, back_v))
    ]
    every = tuple(slice(None) for _ in range(bits))
    pair_load = pltpu.make_async_copy(grad_pair.at[every + (me.core,)], pair_held, pl_sem)
    pair_core_copy = remote(
        grad_pair.at[every + (1 - me.core,)], pair_core, pcs, pcr, ctx=me.partner
    )

    def left_load(a):
        return pltpu.make_async_copy(
            lefts[a].at[:, me.core], left_v[a].at[:, :, pl.ds(0, rows)], ll.at[a]
        )

    def right_load(b):
        return pltpu.make_async_copy(rights[b], right_v[b].at[pl.ds(0, rows)], rl.at[b])

    def left_copy(a):
        return remote(
            lefts[a].at[:, 1 - me.core],
            left_v[a].at[:, :, pl.ds(rows, rows)],
            lls.at[a],
            llr.at[a],
            ctx=me.partner,
        )

    def right_copy(b):
        src = rights[b] if b < rights_count else projected_v.at[pl.ds(0, rows)]
        return remote(
            src, right_v[b].at[pl.ds(rows, rows)], rls.at[b], rlr.at[b], ctx=me.partner
        )

    order, seen = [], set()
    for a, b in pairs:
        for key in (("left", a), ("right", b)):
            if key not in seen and key != ("right", rights_count):
                seen.add(key)
                order.append(key)
    for at, (side, n) in enumerate(order):
        (left_load if side == "left" else right_load)(n).start()
        if at == 1:
            pair_load.start()
    for load in back_loads:
        load.start()
    me.barrier()
    for at, (side, n) in enumerate(order):
        (left_copy if side == "left" else right_copy)(n).start()
        if at == 1:
            pair_core_copy.start()
    arrived = set()

    def arrive(side, n):
        if (side, n) not in arrived:
            arrived.add((side, n))
            if (side, n) in order:
                (left_load if side == "left" else right_load)(n).wait()
            (left_copy if side == "left" else right_copy)(n).wait_recv()

    def target(k):
        return (z + k) % nf

    def form(i, k):
        a, b = pairs[i]
        arrive("left", a)
        arrive("right", b)
        width = held[i].shape[-1]
        chunk = min(width, CHUNK)

        def body(t, carry):
            cols = pl.ds(pl.multiple_of(t * chunk, chunk), chunk)
            value = dot_plain(left_v[a][target(k)], right_v[b][:, cols]).astype(jnp.bfloat16)
            held[i][target(k), ..., cols] = value.reshape(held[i].shape[1:-1] + (chunk,))
            return carry

        lax.fori_loop(0, width // chunk, body, 0)

    def plane_copy(i, k, half, j):
        order = me.orders[half]
        src = held[i].at[
            (target(k),)
            + me.at(order[j + 1 :], other=order[j])
            + (slice(None), column_half(held[i], half))
        ]
        return remote(
            src,
            ins[i][j][half].at[k],
            ps.at[half, i, k, j],
            pr.at[half, i, k, j],
            ctx=me.across[order[j]],
        )

    def pair_copy(half, j):
        order = me.orders[half]
        src = pair_held.at[
            me.at(order[j + 1 :], other=order[j]) + (slice(None), column_half(pair_held, half))
        ]
        return remote(
            src, pair_in[2 * j + half], pps.at[half, j], ppr.at[half, j], ctx=me.across[order[j]]
        )

    def pair_add(place, source, local, cols):
        where = place + (slice(None), cols)
        total = pair_held[where].astype(jnp.float32) + source[local].astype(jnp.float32)
        pair_held[where] = total.astype(pair_held.dtype)

    def pair_stage(j):
        if j == 0:
            pair_load.wait()
            pair_core_copy.wait_recv()
            for place, local in chips_of(range(bits)):
                pair_add(place, pair_core, local, slice(None))
        else:
            for half in (0, 1):
                pair_copy(half, j - 1).wait_recv()
                for place, local in chips_of(me.orders[half][j:]):
                    pair_add(place, pair_in[2 * (j - 1) + half], local, column_half(pair_held, half))
        if j < bits:
            for half in (0, 1):
                pair_copy(half, j).start()

    tokens, weight, raw, grad_query, grad_resid = back_v
    query_width = QUERY_HEADS * HEAD_SIZE
    key_width = KEY_VALUE_HEADS * HEAD_SIZE
    own = pl.ds(0, rows)

    def head_back(cols, which, grad):
        grad = turn(grad, cosines[...], sines[...], -1.0)
        value = raw[:, cols]
        scale = lax.rsqrt(head_means(value * value) + EPSILON)
        scaled = grad * qk_gain[which : which + 1, :]
        mean = head_means(scaled * value)
        result = scale * (scaled - value * scale * scale * mean)
        projected_v[own, cols] = result.astype(jnp.bfloat16)
        return jnp.sum(grad * value * scale, axis=0, keepdims=True)

    def heads_stage():
        for load in back_loads:
            load.wait()
        sums = [jnp.zeros((1, LANES), jnp.float32)] * 2
        for j in range(0, query_width, LANES):
            cols = pl.ds(j, LANES)
            sums[0] = sums[0] + head_back(cols, 0, grad_query[:, cols] * HEAD_SIZE**-0.5)
        here = me.at()
        for j in range(0, key_width, LANES):
            first = pair_held[here + (slice(None), pl.ds(2 * j, LANES))].astype(jnp.float32)
            second = pair_held[here + (slice(None), pl.ds(2 * j + LANES, LANES))].astype(
                jnp.float32
            )
            low = low_lanes(first.shape)
            key = jnp.where(low, first, pltpu.roll(second, HEAD_SIZE, 1))
            value = jnp.where(low, pltpu.roll(first, HEAD_SIZE, 1), second)
            sums[1] = sums[1] + head_back(pl.ds(query_width + j, LANES), 1, key)
            projected_v[own, pl.ds(query_width + key_width + j, LANES)] = value.astype(jnp.bfloat16)
        both = [total + pltpu.roll(total, HEAD_SIZE, 1) for total in sums]
        small_sum[0, pl.ds(2 * gain_rows, 1), :] = jnp.where(
            low_lanes(both[0].shape), both[0], both[1]
        )
        right_copy(rights_count).start()

    gain_rows = gain.shape[1] // LANES
    width = gain.shape[1]
    inverse_mean = []

    def matmul_stage():
        inverse = row_inverse(tokens, rows)
        mean = jnp.zeros((rows, 1), jnp.float32)
        for j in range(0, width, CHUNK):
            cols = pl.ds(j, CHUNK)
            grad = dot_last(projected_v[own, :], weight[cols, :])
            grads[:, cols] = grad
            value = tokens[:, cols].astype(jnp.float32)
            mean = mean + jnp.sum(grad * gain[:, cols] * value, axis=1, keepdims=True)
        inverse_mean.extend([inverse, mean * (1.0 / width) * inverse * inverse])

    def norm_stage():
        inverse, mean = inverse_mean
        for j in range(0, width, CHUNK):
            cols = pl.ds(j, CHUNK)
            grad = grads[:, cols]
            value = tokens[:, cols].astype(jnp.float32)
            part = jnp.sum(grad * value * inverse, axis=0, keepdims=True)
            for c in range(0, CHUNK, LANES):
                small_sum[0, pl.ds((j + c) // LANES, 1), :] = part[:, c : c + LANES]
            grad_resid[:, cols] = grad_resid[:, cols] + inverse * (
                grad * gain[:, cols] - value * mean
            )
        tokens_grad_store.start()

    tokens_grad_store = pltpu.make_async_copy(grad_resid, tokens_grad, grad_sem)

    def chips_of(free):
        places, local = [()], [()]
        for b in reversed(range(bits)):
            if b in free:
                places = [t + (v,) for t in places for v in (0, 1)]
                local = [t + (v,) for t in local for v in (0, 1)]
            else:
                places = [t + (me.bit[b],) for t in places]
        return list(zip(places, local))

    def add(i, k, half, j):
        free = me.orders[half][j + 1 :]
        rows, width = held[i].shape[-2], held[i].shape[-1] // 2
        step = min(rows, 32)
        cols = pl.ds(half * width, width)
        for place, local in chips_of(free):

            def body(t, carry, place=place, local=local):
                at = pl.ds(pl.multiple_of(t * step, step), step)
                where = (target(k),) + place + (at, cols)
                total = held[i][where].astype(jnp.float32) + ins[i][j][half][
                    (k,) + local + (at,)
                ].astype(jnp.float32)
                held[i][where] = total.astype(held[i].dtype)
                return carry

            lax.fori_loop(0, rows // step, body, 0)

    def line_copy(i, k):
        return remote(
            held[i].at[(target(k),) + me.at()],
            line_in[i].at[k],
            ls.at[i, k],
            lr.at[i, k],
            fsdp=target(k),
        )

    def stage(i, k, j):
        if j == 0:
            form(i, k)
        else:
            send(i, k, j - 1)

    def send(i, k, j):
        if j > 0:
            for half in (0, 1):
                plane_copy(i, k, half, j - 1).wait_recv()
                add(i, k, half, j - 1)
        if j < bits:
            for half in (0, 1):
                plane_copy(i, k, half, j).start()
        elif k != 0:
            line_copy(i, k).start()

    def own_copy(i):
        return pltpu.make_async_copy(final[i], outs[i].at[(me.core,) + me.at()], own_sem.at[i])

    def gather_copy(i, half, j):
        order = me.orders[half]
        cols = column_half(final[i], half)
        dst = outs[i].at[(me.core,) + me.at(order[:j]) + (slice(None), cols)]
        src = final[i].at[:, cols] if j == 0 else dst
        return remote(
            src, dst, gs.at[half, i, j], gr.at[half, i, j], ctx=me.across[order[j]]
        )

    def core_copy(i):
        ref = outs[i].at[me.core]
        return remote(ref, ref, cs.at[i], cr.at[i], ctx=me.partner)

    def total(i):
        for k in range(1, nf):
            line_copy(i, k).wait_recv()
        rows = final[i].shape[0]
        step = min(rows, 32)

        def body(t, carry):
            at = pl.ds(pl.multiple_of(t * step, step), step)
            value = held[i][(z,) + me.at() + (at,)].astype(jnp.float32)
            for k in range(1, nf):
                value = value + line_in[i][k, at].astype(jnp.float32)
            final[i][at] = value.astype(final[i].dtype)
            return carry

        lax.fori_loop(0, rows // step, body, 0)
        own_copy(i).start()

    def gather_stage(i, j):
        if j == 0:
            own_copy(i).wait()
        else:
            for half in (0, 1):
                gather_copy(i, half, j - 1).wait_recv()
        if j < bits:
            for half in (0, 1):
                gather_copy(i, half, j).start()
        else:
            core_copy(i).start()

    across = [me.partner] + me.across

    def small_copy(s):
        return remote(small_sum.at[s], small_in.at[s], ss.at[s], sr.at[s], ctx=across[s])

    def small_line_copy(k):
        return remote(
            small_sum.at[bits + 1], small_line.at[z], sls.at[k], slr.at[k], fsdp=target(k)
        )

    def small_stage(s):
        if s > 0:
            small_copy(s - 1).wait_recv()
            small_sum[s] = small_sum[s - 1] + small_in[s - 1]
        if s <= bits:
            small_copy(s).start()
        else:
            for k in range(1, nf):
                small_line_copy(k).start()
            small_line[z] = small_sum[s]

    small_sum[0] = jnp.zeros(small_sum.shape[1:], jnp.float32)
    for r in range(gain_rows):
        small_sum[0, pl.ds(gain_rows + r, 1), :] = ffn_gain_part[:, r * LANES : (r + 1) * LANES]
    jobs = []
    for i in range(count):
        for k in list(range(1, nf)) + [0]:
            job = [functools.partial(stage, i, k, j) for j in range(bits + 2)]
            if k == 0:
                job += [functools.partial(total, i)]
                job += [functools.partial(gather_stage, i, j) for j in range(bits + 1)]
                job += [core_copy(i).wait_recv]
            jobs.append(job)
    back_job = [functools.partial(pair_stage, j) for j in range(bits + 1)]
    back_job += [heads_stage, matmul_stage, norm_stage]
    back_job += [functools.partial(small_stage, s) for s in range(bits + 2)]
    run_ticks(jobs[:1] + [back_job] + jobs[1:])
    for k in range(1, nf):
        small_line_copy(k).wait_recv()
    value = small_line[0]
    for k in range(1, nf):
        value = value + small_line[k]
    small_out[...] = value
    for s in range(bits + 1):
        small_copy(s).wait_send()
    for k in range(1, nf):
        small_line_copy(k).wait_send()
    for i in range(count):
        for k in range(nf):
            for half in (0, 1):
                for j in range(bits):
                    plane_copy(i, k, half, j).wait_send()
            if k:
                line_copy(i, k).wait_send()
        for half in (0, 1):
            for j in range(bits):
                gather_copy(i, half, j).wait_send()
        core_copy(i).wait_send()
    for side, n in order + [("right", rights_count)]:
        (left_copy if side == "left" else right_copy)(n).wait_send()
    pair_core_copy.wait_send()
    for half in (0, 1):
        for j in range(bits):
            pair_copy(half, j).wait_send()
    tokens_grad_store.wait()


BACK_LOADS = 5


def reduce_gradients(nf, nc, pairs, lefts, rights, grad_pair, back, ffn_gain_part):
    _, bits = plane_shape(nc)
    rows = rights[0].shape[0]
    count = len(pairs)
    views = [a.reshape(nf, 2, a.shape[0] // (2 * nf), rows) for a in lefts]
    widths = [b.shape[1] for b in rights] + [back[1].shape[1]]
    pieces = [(lefts[a].shape[0] // (nf * nc), widths[b]) for a, b in pairs]
    pair_rows, pair_width = grad_pair.shape[0] // nc, grad_pair.shape[1]
    pair_view = grad_pair.reshape((2,) * (bits + 1) + (pair_rows, pair_width))
    gain_rows = 2 * ffn_gain_part.shape[1] // LANES + 1
    small = jax.ShapeDtypeStruct((gain_rows + -gain_rows % 8, LANES), jnp.float32)
    outs = pl.pallas_call(
        functools.partial(reduce_kernel, nf, nc, pairs, len(lefts), len(rights)),
        out_shape=[
            jax.ShapeDtypeStruct((2,) * (bits + 1) + piece, jnp.bfloat16) for piece in pieces
        ]
        + [jax.ShapeDtypeStruct(back[4].shape, jnp.float32), small],
        in_specs=[HBM_SPEC] * (len(lefts) + len(rights) + 1 + BACK_LOADS) + [VMEM_SPEC] * 5,
        out_specs=[HBM_SPEC] * (count + 1) + [VMEM_SPEC],
        scratch_shapes=[
            pltpu.VMEM((nf, v.shape[2], 2 * rows), jnp.bfloat16) for v in views
        ]
        + [pltpu.VMEM((2 * rows, n), jnp.bfloat16) for n in widths]
        + [pltpu.VMEM((nf,) + (2,) * bits + piece, jnp.bfloat16) for piece in pieces]
        + [
            pltpu.VMEM((nf,) + (2,) * (bits - 1 - j) + (r, width // 2), jnp.bfloat16)
            for r, width in pieces
            for j in range(bits)
            for _ in (0, 1)
        ]
        + [pltpu.VMEM((nf,) + piece, jnp.bfloat16) for piece in pieces]
        + [pltpu.VMEM(piece, jnp.bfloat16) for piece in pieces]
        + [
            pltpu.VMEM((bits + 2,) + small.shape, jnp.float32),
            pltpu.VMEM((bits + 1,) + small.shape, jnp.float32),
            pltpu.VMEM((nf,) + small.shape, jnp.float32),
        ]
        + [pltpu.VMEM((2,) * bits + (pair_rows, pair_width), jnp.bfloat16)] * 2
        + [
            pltpu.VMEM((2,) * (bits - 1 - j) + (pair_rows, pair_width // 2), jnp.bfloat16)
            for j in range(bits)
            for _ in (0, 1)
        ]
        + [pltpu.VMEM(v.shape, v.dtype) for v in back[:BACK_LOADS]]
        + [pltpu.VMEM(back[4].shape, jnp.float32)]
        + [DMA((BACK_LOADS,)), DMA, DMA, DMA, DMA, DMA((2, bits)), DMA((2, bits))]
        + [DMA((len(lefts),))] * 3
        + [DMA((len(widths),))] * 3
        + [DMA((2, count, nf, bits))] * 2
        + [DMA((count, nf))] * 2
        + [DMA((2, count, bits))] * 2
        + [DMA((count,))] * 2
        + [DMA((count,))]
        + [DMA((bits + 1,))] * 2
        + [DMA((nf,))] * 2,
        compiler_params=pltpu.CompilerParams(
            collective_id=2, has_side_effects=True, vmem_limit_bytes=VMEM_LIMIT
        ),
        name="reduce_gradients",
    )(*views, *rights, pair_view, *back, ffn_gain_part)
    return [
        o.reshape(r * nc, width) for o, (r, width) in zip(outs, pieces)
    ], outs[count], outs[count + 1]


LANES = 128
GROUP = QUERY_HEADS // KEY_VALUE_HEADS
SMEM_SPEC = pl.BlockSpec(memory_space=pltpu.SMEM)


def low_lanes(shape):
    return lax.broadcasted_iota(jnp.int32, shape, len(shape) - 1) % LANES < HEAD_SIZE


def stack_heads(ref, row, group, length, high):
    tiles = []
    for pair in range(GROUP // 2):
        cols = pl.ds((group * GROUP // 2 + pair) * LANES, LANES)
        tile = ref[pl.ds(row, length), cols].astype(jnp.float32)
        turned = pltpu.roll(tile, HEAD_SIZE, 1)
        low = low_lanes(tile.shape)
        if high:
            tiles += [jnp.where(low, 0.0, turned), jnp.where(low, 0.0, tile)]
        else:
            tiles += [jnp.where(low, tile, 0.0), jnp.where(low, turned, 0.0)]
    return jnp.concatenate(tiles, axis=0)


def unstack_heads(ref, row, group, length, value, high):
    for pair in range(GROUP // 2):
        cols = pl.ds((group * GROUP // 2 + pair) * LANES, LANES)
        first = value[2 * pair * length : (2 * pair + 1) * length]
        second = value[(2 * pair + 1) * length : (2 * pair + 2) * length]
        low = low_lanes(first.shape)
        if high:
            tile = jnp.where(low, pltpu.roll(first, HEAD_SIZE, 1), second)
        else:
            tile = jnp.where(low, first, pltpu.roll(second, HEAD_SIZE, 1))
        ref[pl.ds(row, length), cols] = tile.astype(ref.dtype)


def query_span(rank, order, starts, stored_of, which, length):
    block = order[2 * rank + which]
    first = jnp.int32(0)
    place = block * length + lax.broadcasted_iota(jnp.int32, (1, length), 1)
    begin = jnp.zeros((1, length), jnp.int32)
    for d in range(starts.shape[1]):
        first = jnp.where(starts[0, d] <= block * length, starts[0, d], first)
        begin = jnp.where(starts[0, d] <= place, starts[0, d], begin)
    place = jnp.concatenate([place] * GROUP, axis=1)
    begin = jnp.concatenate([begin] * GROUP, axis=1)
    return block, first // length, place, begin


def invert_order(order, stored_of):
    for s in range(order.shape[0]):
        stored_of[order[s]] = s


def key_rows(stored_of, block, length, blocks):
    second = stored_of[jnp.minimum(block + 1, blocks - 1)]
    return [
        pl.ds(pl.multiple_of(s * length, length), length) for s in (stored_of[block], second)
    ]


def allowed_keys(block, place, begin, length):
    key = block * length + lax.broadcasted_iota(jnp.int32, (2 * length, place.shape[1]), 0)
    return (key >= begin) & (key <= place)


def dot_last(left, right):
    return lax.dot_general(
        left, right, (((1,), (1,)), ((), ())), preferred_element_type=jnp.float32
    )


def dot_plain(left, right):
    return lax.dot_general(
        left, right, (((1,), (0,)), ((), ())), preferred_element_type=jnp.float32
    )


def attend_kernel(rank, order, starts, query, pair, attended, exact, log_sum, stored_of, acc, queries):
    length = query.shape[0] // 2
    blocks = order.shape[0]
    invert_order(order, stored_of)

    def one_block(which, carry):
        row = pl.multiple_of(which * length, length)
        block, first, place, begin = query_span(rank[0], order, starts, stored_of, which, length)
        for g in range(KEY_VALUE_HEADS):
            queries[g] = stack_heads(query, row, g, length, False).astype(jnp.bfloat16)
        acc[...] = jnp.zeros_like(acc)

        def step(t, carry):
            key_block = first + 2 * t
            rows = key_rows(stored_of, key_block, length, blocks)
            allowed = allowed_keys(key_block, place, begin, length)
            for g in range(KEY_VALUE_HEADS):
                cols = pl.ds(g * LANES, LANES)
                keys = jnp.concatenate([pair[r, cols] for r in rows], axis=0)
                scores = dot_last(keys, queries[g])
                weights = jnp.where(allowed, jnp.exp(scores), 0.0).astype(jnp.bfloat16)
                ones = jnp.where(low_lanes(keys.shape), 1.0, keys.astype(jnp.float32))
                acc[g] += dot_plain(ones.T.astype(jnp.bfloat16), weights)
            return carry

        lax.fori_loop(0, (block - first + 2) // 2, step, 0)
        for g in range(KEY_VALUE_HEADS):
            total = acc[g]
            sums = total[0:1]
            log_sum[which, g] = jnp.broadcast_to(jnp.log(sums), log_sum.shape[2:])
            value = (total / sums).T
            unstack_heads(attended, row, g, length, value, True)
            unstack_heads(exact, row, g, length, value, True)
        return carry

    lax.fori_loop(0, 2, one_block, 0)


def attend(rank, order, starts, query, pair):
    rows = query.shape[0]
    wide = GROUP * (rows // 2)
    return pl.pallas_call(
        attend_kernel,
        out_shape=[
            jax.ShapeDtypeStruct(query.shape, jnp.bfloat16),
            jax.ShapeDtypeStruct(query.shape, jnp.float32),
            jax.ShapeDtypeStruct((2, KEY_VALUE_HEADS, 8, wide), jnp.float32),
        ],
        in_specs=[SMEM_SPEC] * 3 + [VMEM_SPEC] * 2,
        out_specs=[VMEM_SPEC] * 3,
        scratch_shapes=[
            pltpu.SMEM((order.shape[0],), jnp.int32),
            pltpu.VMEM((KEY_VALUE_HEADS, LANES, wide), jnp.float32),
            pltpu.VMEM((KEY_VALUE_HEADS, wide, LANES), jnp.bfloat16),
        ],
        name="attend",
    )(rank, order, starts, query, pair)


def attend_back_kernel(
    rank, order, starts, query, pair, grad, exact, log_sum, grad_query, grad_pair,
    stored_of, total, acc, queries, grads, delta,
):
    length = query.shape[0] // 2
    blocks = order.shape[0]
    invert_order(order, stored_of)
    total[...] = jnp.zeros_like(total)

    def one_block(which, carry):
        row = pl.multiple_of(which * length, length)
        block, first, place, begin = query_span(rank[0], order, starts, stored_of, which, length)
        for g in range(KEY_VALUE_HEADS):
            queries[g] = stack_heads(query, row, g, length, False).astype(jnp.bfloat16)
            upper = stack_heads(grad, row, g, length, True)
            grads[g] = upper.astype(jnp.bfloat16)
            product = upper * stack_heads(exact, row, g, length, True)
            delta[g] = jnp.broadcast_to(
                jnp.sum(product.T, axis=0, keepdims=True), delta.shape[1:]
            )
        acc[...] = jnp.zeros_like(acc)

        def step(t, carry):
            key_block = first + 2 * t
            rows = key_rows(stored_of, key_block, length, blocks)
            allowed = allowed_keys(key_block, place, begin, length)
            for g in range(KEY_VALUE_HEADS):
                cols = pl.ds(g * LANES, LANES)
                keys = jnp.concatenate([pair[r, cols] for r in rows], axis=0)
                scores = dot_last(keys, queries[g])
                probs = jnp.where(allowed, jnp.exp(scores - log_sum[which, g, 0:1]), 0.0)
                grad_probs = dot_last(keys, grads[g])
                grad_scores = (probs * (grad_probs - delta[g, 0:1])).astype(jnp.bfloat16)
                turned = keys.astype(jnp.float32).T.astype(jnp.bfloat16)
                acc[g] += dot_plain(turned, grad_scores)
                both = dot_plain(grad_scores, queries[g]) + dot_plain(
                    probs.astype(jnp.bfloat16), grads[g]
                )
                total[rows[0], cols] += both[:length]
                total[rows[1], cols] += both[length:]
            return carry

        lax.fori_loop(0, (block - first + 2) // 2, step, 0)
        for g in range(KEY_VALUE_HEADS):
            unstack_heads(grad_query, row, g, length, acc[g].T, False)
        return carry

    lax.fori_loop(0, 2, one_block, 0)

    def finish(t, carry):
        at = pl.ds(pl.multiple_of(t * length, length), length)
        grad_pair[at, :] = total[at, :].astype(grad_pair.dtype)
        return carry

    lax.fori_loop(0, blocks, finish, 0)


def attend_back(rank, order, starts, query, pair, grad, exact, log_sum):
    rows = query.shape[0]
    wide = GROUP * (rows // 2)
    return pl.pallas_call(
        attend_back_kernel,
        out_shape=[
            jax.ShapeDtypeStruct(query.shape, jnp.float32),
            jax.ShapeDtypeStruct(pair.shape, jnp.bfloat16),
        ],
        in_specs=[SMEM_SPEC] * 3 + [VMEM_SPEC] * 5,
        out_specs=[VMEM_SPEC] * 2,
        scratch_shapes=[
            pltpu.SMEM((order.shape[0],), jnp.int32),
            pltpu.VMEM(pair.shape, jnp.float32),
            pltpu.VMEM((KEY_VALUE_HEADS, LANES, wide), jnp.float32),
            pltpu.VMEM((KEY_VALUE_HEADS, wide, LANES), jnp.bfloat16),
            pltpu.VMEM((KEY_VALUE_HEADS, wide, LANES), jnp.bfloat16),
            pltpu.VMEM((KEY_VALUE_HEADS, 8, wide), jnp.float32),
        ],
        name="attend_back",
    )(rank, order, starts, query, pair, grad, exact, log_sum)


CHUNK = 256


def head_means(values):
    shape = (LANES, LANES)
    same = (
        lax.broadcasted_iota(jnp.int32, shape, 0) // HEAD_SIZE
        == lax.broadcasted_iota(jnp.int32, shape, 1) // HEAD_SIZE
    )
    ones = jnp.where(same, 1.0, 0.0).astype(jnp.bfloat16)
    high = values.astype(jnp.bfloat16)
    low = (values - high.astype(jnp.float32)).astype(jnp.bfloat16)
    return (dot_plain(high, ones) + dot_plain(low, ones)) * (1.0 / HEAD_SIZE)


def first_quarter(shape):
    return lax.broadcasted_iota(jnp.int32, shape, len(shape) - 1) % HEAD_SIZE < HEAD_SIZE // 2


def turn(values, cosines, sines, sign):
    half = HEAD_SIZE // 2
    ahead = pltpu.roll(values, LANES - half, 1)
    behind = pltpu.roll(values, half, 1)
    other = jnp.where(first_quarter(values.shape), -ahead, behind)
    return values * cosines + sign * other * sines


def row_inverse(ref, rows):
    total = jnp.zeros((rows, 1), jnp.float32)
    width = ref.shape[1]
    for j in range(0, width, CHUNK):
        value = ref[:, j : j + CHUNK].astype(jnp.float32)
        total = total + jnp.sum(value * value, axis=1, keepdims=True)
    return lax.rsqrt(total * (1.0 / width) + EPSILON)


def feed_kernel(
    tokens, cotangent, attended, gain, w_out, w_gate, w_up, w_down,
    mixed, normed_turned, hidden_turned, attended_turned, grad_gate, grad_up, grad_resid, grad_branch,
    grad_attended, gain_grad,
    out_v, gate_v, up_v, down_v, resid, normed, hidden, sems,
):
    rows, width = tokens.shape
    loads = [
        pltpu.make_async_copy(src, dst, sems.at[i])
        for i, (src, dst) in enumerate(
            ((w_out, out_v), (w_gate, gate_v), (w_up, up_v), (w_down, down_v))
        )
    ]
    for load in loads:
        load.start()
    loads[0].wait()
    for j in range(0, width, CHUNK):
        cols = pl.ds(j, CHUNK)
        resid[:, cols] = tokens[:, cols].astype(jnp.float32) + dot_plain(
            attended[...], out_v[:, cols]
        )
    inverse = row_inverse(resid, rows)
    for j in range(0, width, CHUNK):
        cols = pl.ds(j, CHUNK)
        value = resid[:, cols] * inverse * gain[:, cols]
        normed[:, cols] = value.astype(jnp.bfloat16)
        normed_turned[cols, :] = value.T.astype(jnp.bfloat16)
    for load in loads[1:]:
        load.wait()
    for j in range(0, gate_v.shape[1], CHUNK):
        cols = pl.ds(j, CHUNK)
        gate = dot_plain(normed[...], gate_v[:, cols])
        up = dot_plain(normed[...], up_v[:, cols])
        sigmoid = 1.0 / (1.0 + jnp.exp(-gate))
        inner = gate * sigmoid * up
        hidden[:, cols] = inner.astype(jnp.bfloat16)
        hidden_turned[cols, :] = inner.T.astype(jnp.bfloat16)
        grad_hidden = dot_last(cotangent[...], down_v[cols, :])
        grad_gate[:, cols] = (
            grad_hidden * up * sigmoid * (1.0 + gate * (1.0 - sigmoid))
        ).astype(jnp.bfloat16)
        grad_up[:, cols] = (grad_hidden * gate * sigmoid).astype(jnp.bfloat16)
    mean = jnp.zeros((rows, 1), jnp.float32)
    for j in range(0, width, CHUNK):
        cols = pl.ds(j, CHUNK)
        mixed[:, cols] = (resid[:, cols] + dot_plain(hidden[...], down_v[:, cols])).astype(
            jnp.bfloat16
        )
        grad = dot_last(grad_gate[...], gate_v[cols, :]) + dot_last(grad_up[...], up_v[cols, :])
        grad_resid[:, cols] = grad
        mean = mean + jnp.sum(grad * gain[:, cols] * resid[:, cols], axis=1, keepdims=True)
    mean = mean * (1.0 / width) * inverse * inverse
    for j in range(0, width, CHUNK):
        cols = pl.ds(j, CHUNK)
        grad = grad_resid[:, cols]
        value = resid[:, cols]
        gain_grad[:, cols] = jnp.sum(grad * value * inverse, axis=0, keepdims=True)
        total = cotangent[:, cols].astype(jnp.float32) + inverse * (
            grad * gain[:, cols] - value * mean
        )
        grad_resid[:, cols] = total
        grad_branch[:, cols] = total.astype(jnp.bfloat16)
    for j in range(0, attended.shape[1], CHUNK):
        cols = pl.ds(j, CHUNK)
        attended_turned[cols, :] = attended[:, cols].astype(jnp.float32).T.astype(jnp.bfloat16)
        grad_attended[:, cols] = dot_last(grad_branch[...], out_v[cols, :]).astype(jnp.bfloat16)


def feed(tokens, cotangent, attended, gain, w_out, w_gate, w_up, w_down):
    rows, width = tokens.shape
    inner = w_gate.shape[1]
    shape = jax.ShapeDtypeStruct
    low, full = jnp.bfloat16, jnp.float32
    return pl.pallas_call(
        feed_kernel,
        out_shape=[
            shape((rows, width), low),
            shape((width, rows), low),
            shape((inner, rows), low),
            shape((attended.shape[1], rows), low),
            shape((rows, inner), low),
            shape((rows, inner), low),
            shape((rows, width), full),
            shape((rows, width), low),
            shape(attended.shape, low),
            shape((1, width), full),
        ],
        in_specs=[VMEM_SPEC] * 4 + [HBM_SPEC] * 4,
        out_specs=[VMEM_SPEC] * 10,
        scratch_shapes=[pltpu.VMEM(w.shape, low) for w in (w_out, w_gate, w_up, w_down)]
        + [
            pltpu.VMEM((rows, width), full),
            pltpu.VMEM((rows, width), low),
            pltpu.VMEM((rows, inner), low),
            DMA((4,)),
        ],
        name="feed",
    )(tokens, cotangent, attended, gain, w_out, w_gate, w_up, w_down)


def pack_rows(arrays, multiple):
    flat = jnp.concatenate([a.astype(jnp.float32).reshape(-1) for a in arrays])
    size = multiple * 128
    return jnp.pad(flat, (0, -flat.shape[0] % size)).reshape(-1, 128)


def per_device(
    tokens,
    cotangent,
    doc_starts,
    deal_order,
    query_key_value_weight,
    w_out,
    w_gate,
    w_up,
    w_down,
    gain_attn,
    gain_ffn,
    gain_qk,
):
    ctx_count = lax.axis_size("ctx")
    fsdp_count = lax.axis_size("fsdp")
    ctx_rank = lax.axis_index("ctx")
    fsdp_rank = lax.axis_index("fsdp")
    model_shard = gain_attn.shape[0]
    qk_shard = gain_qk.shape[1]
    model = model_shard * fsdp_count
    pack_in = tokens[0]
    grad_mixed = cotangent[0]
    rank = ctx_rank.reshape(1).astype(jnp.int32)
    frequency = THETA ** (-jnp.arange(0, HEAD_SIZE // 2, dtype=jnp.float32) * 2.0 / HEAD_SIZE)
    frequency = jnp.concatenate([frequency] * (2 * LANES // HEAD_SIZE)).reshape(1, LANES)
    lane = jnp.arange(LANES) % HEAD_SIZE - fsdp_rank * qk_shard
    own_lanes = (lane >= 0) & (lane < qk_shard)
    qk_rows = jnp.where(own_lanes, jnp.tile(gain_qk, (1, LANES // qk_shard)), 0)
    gains = pack_rows([gain_attn, gain_ffn, qk_rows], 8)
    weights, (attn_gain, ffn_gain, qk_gain, normed, raw, query, cosines, sines), pair = (
        gather_weights(
            fsdp_count,
            ctx_count,
            [query_key_value_weight, w_out, w_gate, w_up, w_down],
            gains,
            pack_in,
            deal_order,
            doc_starts,
            frequency,
        )
    )
    qkv_full, out_full, gate_full, up_full, down_full = weights
    attended, exact, log_sum = attend(rank, deal_order, doc_starts, query, pair)
    (
        mixed_out,
        normed_ffn,
        hidden,
        attended_turned,
        grad_gate,
        grad_up,
        grad_resid,
        grad_branch,
        grad_attended,
        ffn_gain_part,
    ) = feed(pack_in, grad_mixed, attended, ffn_gain, out_full, gate_full, up_full, down_full)
    grad_query, grad_pair = attend_back(
        rank, deal_order, doc_starts, query, pair, grad_attended, exact, log_sum
    )
    (down_grad, gate_grad, up_grad, out_grad, qkv_grad), tokens_grad, gain_sums = reduce_gradients(
        fsdp_count,
        ctx_count,
        ((0, 0), (1, 1), (1, 2), (2, 3), (3, 4)),
        [hidden, normed_ffn, attended_turned, normed],
        [grad_mixed, grad_gate, grad_up, grad_branch],
        grad_pair,
        [
            pack_in,
            qkv_full,
            raw,
            grad_query,
            grad_resid,
            attn_gain,
            qk_gain,
            cosines,
            sines,
        ],
        ffn_gain_part,
    )
    gain_sums = gain_sums.reshape(-1)
    attn_gain_grad = lax.dynamic_slice_in_dim(gain_sums, fsdp_rank * model_shard, model_shard)
    ffn_gain_grad = lax.dynamic_slice_in_dim(
        gain_sums, model + fsdp_rank * model_shard, model_shard
    )
    qk_gain_grad = lax.dynamic_slice_in_dim(
        gain_sums[2 * model : 2 * model + 2 * HEAD_SIZE].reshape(2, HEAD_SIZE),
        fsdp_rank * qk_shard,
        qk_shard,
        axis=1,
    )
    return (
        mixed_out[None],
        tokens_grad[None],
        qkv_grad.astype(jnp.float32),
        out_grad.astype(jnp.float32),
        gate_grad.astype(jnp.float32),
        up_grad.astype(jnp.float32),
        down_grad.astype(jnp.float32),
        attn_gain_grad,
        ffn_gain_grad,
        qk_gain_grad,
    )


def solution(mesh):
    return jax.shard_map(
        per_device,
        mesh=mesh,
        in_specs=(
            P("fsdp", "ctx", None),
            P("fsdp", "ctx", None),
            P("fsdp", None),
            P(),
            P("fsdp", None),
            P("fsdp", None),
            P("fsdp", None),
            P("fsdp", None),
            P("fsdp", None),
            P("fsdp"),
            P("fsdp"),
            P(None, "fsdp"),
        ),
        out_specs=(
            P("fsdp", "ctx", None),
            P("fsdp", "ctx", None),
            P("fsdp", None),
            P("fsdp", None),
            P("fsdp", None),
            P("fsdp", None),
            P("fsdp", None),
            P("fsdp"),
            P("fsdp"),
            P(None, "fsdp"),
        ),
        check_vma=False,
    )
```

```python
import functools

import jax
import jax.numpy as jnp
from jax import lax
from jax.experimental import pallas as pl
from jax.experimental.pallas import tpu as pltpu
from jax.sharding import PartitionSpec as P

QUERY_HEADS = 16
KEY_VALUE_HEADS = 4
HEAD_SIZE = 64


EPSILON = 1e-06
THETA = 10000.0

MESH = pl.DeviceIdType.MESH
DMA = pltpu.SemaphoreType.DMA
HBM_SPEC = pl.BlockSpec(memory_space=pl.ANY)
VMEM_SPEC = pl.BlockSpec(memory_space=pltpu.VMEM)
SPACING = 2
VMEM_LIMIT = 67043328


def plane_shape(ctx_count):
    chips = ctx_count // 2
    bits = chips.bit_length() - 1
    assert 2**bits == chips and ctx_count == 2 * chips
    return chips, bits


class Place:
    def __init__(self, ctx_count, fsdp_count):
        self.chips, self.bits = plane_shape(ctx_count)
        self.fsdp_count = fsdp_count
        self.ctx = lax.axis_index("ctx")
        self.z = lax.axis_index("fsdp")
        self.core = self.ctx % 2
        chip = self.ctx // 2
        self.bit = [(chip // 2**j) % 2 for j in range(self.bits)]
        self.across = [self.ctx + (1 - 2 * self.bit[j]) * 2 * 2**j for j in range(self.bits)]
        self.partner = self.ctx + 1 - 2 * self.core
        self.orders = (list(range(self.bits)), list(reversed(range(self.bits))))

    def at(self, free=(), other=None):
        return tuple(
            slice(None) if j in free else (1 - self.bit[j] if j == other else self.bit[j])
            for j in reversed(range(self.bits))
        )

    def barrier(self, plane=True, line=True, near=False):
        sem = pltpu.get_barrier_semaphore()
        count = 0
        if plane:
            for p in self.across + [self.partner]:
                pl.semaphore_signal(sem, inc=1, device_id={"ctx": p}, device_id_type=MESH)
                count += 1
        if line:
            for k in range(1, self.fsdp_count):
                pl.semaphore_signal(
                    sem,
                    inc=1,
                    device_id={"fsdp": (self.z + k) % self.fsdp_count},
                    device_id_type=MESH,
                )
                count += 1
        pl.semaphore_wait(sem, count)


def remote(src, dst, send, recv, **where):
    return pltpu.make_async_remote_copy(
        src, dst, send, recv, device_id=where, device_id_type=MESH
    )


def run_ticks(jobs, spacing=SPACING):
    depth = max(len(job) for job in jobs)
    for tick in range(len(jobs) + spacing * (depth - 1)):
        for j in reversed(range(depth)):
            t = tick - spacing * j
            if 0 <= t < len(jobs) and j < len(jobs[t]):
                jobs[t][j]()


def column_half(ref, half):
    n = ref.shape[-1] // 2
    return pl.ds(half * n, n)


def gather_kernel(nf, nc, count, *refs):
    rest = list(refs)

    def take(n):
        return [rest.pop(0) for _ in range(n)]

    shards, (small, tokens, order_of, starts, frequency) = take(count), take(5)
    outs, (attn_gain, ffn_gain, qk_gain) = take(count), take(3)
    normed_turned, raw, query, cosines, sines, pair = take(6)
    weight, small_v, normed, pair_v, *stages = take(count + 3)
    up_s, up_r, down_s, down_r, ps, pr, cs, cr, ss, sr, load_sem, store_sem = take(12)
    pps, ppr, pcs, pcr, pair_sem = rest
    first_out = outs[0]
    outs = [weight] + list(outs[1:])
    me = Place(nc, nf)
    z = me.z
    loads = [
        pltpu.make_async_copy(
            shards[i], weight.at[z] if i == 0 else stages[i - 1], load_sem.at[i]
        )
        for i in range(count)
    ]
    stores = [
        pltpu.make_async_copy(stages[i - 1], outs[i].at[z], store_sem.at[i])
        for i in range(1, count)
    ]
    weight_store = pltpu.make_async_copy(weight, first_out, store_sem.at[0])
    for load in loads:
        load.start()
    me.barrier()

    def source(k):
        pairs = jnp.minimum(z, nf - 1 - z)
        near = (k + 1) // 2
        near_source = z - near if k % 2 == 1 else z + near
        far = k - pairs
        far_source = jnp.where(2 * z < nf - 1, z + far, z - far)
        return jnp.where(k <= 2 * pairs, near_source, far_source)

    sources = [None] + [source(k) for k in range(1, nf)]

    def line_copy(i, src_z, src, up):
        to = z + 1 if up else z - 1
        sems = (up_s, up_r) if up else (down_s, down_r)
        return remote(
            src,
            outs[i].at[(src_z, me.core) + me.at()],
            sems[0].at[i, src_z],
            sems[1].at[i, src_z],
            fsdp=to,
        )

    def line_start(i, src_z, src, up, condition):
        @pl.when(condition)
        def _():
            line_copy(i, src_z, src, up).start()

    def small_copy(k):
        return remote(small, small_v.at[z], ss.at[k], sr.at[k], fsdp=(z + k) % nf)

    def own_start(i):
        mine = shards[i].at[(me.core,) + me.at()]
        line_start(i, z, mine, True, z + 1 < nf)
        line_start(i, z, mine, False, z > 0)

    for k in range(1, nf):
        small_copy(k).start()
    for i in range(min(AHEAD, count)):
        own_start(i)
    small_v[z] = small[...]

    def line_stage(i, k):
        src_z = sources[k]
        here = outs[i].at[(src_z, me.core) + me.at()]
        below = src_z < z

        @pl.when(below)
        def _():
            line_copy(i, src_z, here, True).wait_recv()

        @pl.when(jnp.logical_not(below))
        def _():
            line_copy(i, src_z, here, False).wait_recv()

        line_start(i, src_z, here, True, jnp.logical_and(below, z + 1 < nf))
        line_start(i, src_z, here, False, jnp.logical_and(src_z > z, z > 0))
        if k == nf - 1 and i + AHEAD < count:
            own_start(i + AHEAD)

    def plane_copy(i, k, half, j):
        order = me.orders[half]
        ref = outs[i].at[
            (sources[k], me.core) + me.at(order[:j]) + (slice(None), column_half(outs[i], half))
        ]
        return remote(
            ref, ref, ps.at[half, i, k, j], pr.at[half, i, k, j], ctx=me.across[order[j]]
        )

    def core_copy(i, k):
        ref = outs[i].at[sources[k], me.core]
        return remote(ref, ref, cs.at[i, k], cr.at[i, k], ctx=me.partner)

    def plane_stage(i, k, j):
        if j == 0:
            line_stage(i, k)
        else:
            for half in (0, 1):
                plane_copy(i, k, half, j - 1).wait_recv()
        if j < me.bits:
            for half in (0, 1):
                plane_copy(i, k, half, j).start()
        else:
            core_copy(i, k).start()

    order = [(i, k) for i in range(count) for k in range(1, nf)]
    jobs = [
        [functools.partial(plane_stage, i, k, j) for j in range(me.bits + 1)]
        + [core_copy(i, k).wait_recv]
        for i, k in order
    ]
    rows = tokens.shape[0]
    length = rows // 2
    width = tokens.shape[1]
    query_width = QUERY_HEADS * HEAD_SIZE
    key_width = KEY_VALUE_HEADS * HEAD_SIZE

    def angle_stage():
        for which in (0, 1):
            block = order_of[2 * me.ctx + which]
            place = block * length + lax.broadcasted_iota(jnp.int32, (length, LANES), 0)
            begin = jnp.zeros((length, LANES), jnp.int32)
            for d in range(starts.shape[1]):
                begin = jnp.where(starts[0, d] <= place, starts[0, d], begin)
            angle = (place - begin).astype(jnp.float32) * frequency[...]
            at = pl.ds(which * length, length)
            cosines[at, :] = jnp.cos(angle)
            sines[at, :] = jnp.sin(angle)

    def norm_stage():
        for k in range(1, nf):
            small_copy(k).wait_recv()
        per = width // nf // LANES
        for c in range(width // LANES):
            cols = pl.ds(c * LANES, LANES)
            attn_gain[:, cols] = small_v[c // per, pl.ds(c % per, 1), :]
            ffn_gain[:, cols] = small_v[c // per, pl.ds(per + c % per, 1), :]
        value = small_v[0, pl.ds(2 * per, 2), :]
        for k in range(1, nf):
            value = value + small_v[k, pl.ds(2 * per, 2), :]
        qk_gain[...] = value
        inverse = row_inverse(tokens, rows)
        for j in range(0, width, CHUNK):
            cols = pl.ds(j, CHUNK)
            value = tokens[:, cols].astype(jnp.float32) * inverse * attn_gain[:, cols]
            normed[:, cols] = value.astype(jnp.bfloat16)
            normed_turned[cols, :] = value.T.astype(jnp.bfloat16)

    def matmul_stage():
        weight_store.start()
        for j in range(0, raw.shape[1], CHUNK):
            cols = weight[..., pl.ds(j, CHUNK)].reshape(width, CHUNK)
            raw[:, j : j + CHUNK] = dot_plain(normed[...], cols)

    def head_turn(cols, which):
        value = raw[:, cols]
        scale = lax.rsqrt(head_means(value * value) + EPSILON)
        return turn(value * scale * qk_gain[which : which + 1, :], cosines[...], sines[...], 1.0)

    def key_stage():
        for j in range(0, key_width, LANES):
            key = head_turn(pl.ds(query_width + j, LANES), 1)
            value = raw[:, query_width + key_width + j : query_width + key_width + j + LANES]
            low = low_lanes(key.shape)
            first = jnp.where(low, key, pltpu.roll(value, HEAD_SIZE, 1))
            second = jnp.where(low, pltpu.roll(key, HEAD_SIZE, 1), value)
            pair_v[:, 2 * j : 2 * j + LANES] = first.astype(jnp.bfloat16)
            pair_v[:, 2 * j + LANES : 2 * j + 2 * LANES] = second.astype(jnp.bfloat16)
        for half in (0, 1):
            pair_copy(half, 0).start()
        pair_own_core.start()
        pair_store.start()

    def query_stage():
        for j in range(0, query_width, LANES):
            cols = pl.ds(j, LANES)
            query[:, cols] = (head_turn(cols, 0) * HEAD_SIZE**-0.5).astype(jnp.bfloat16)

    def pair_copy(half, j):
        order = me.orders[half]
        where = (slice(None), column_half(pair, half))
        dst = pair.at[me.at(order[:j]) + (me.core,) + where]
        src = pair_v.at[where] if j == 0 else dst
        return remote(src, dst, pps.at[half, j], ppr.at[half, j], ctx=me.across[order[j]])

    pair_own_core = remote(
        pair_v, pair.at[me.at() + (me.core,)], pcs.at[0, 0], pcr.at[0, 0], ctx=me.partner
    )
    pair_store = pltpu.make_async_copy(pair_v, pair.at[me.at() + (me.core,)], pair_sem)

    def pair_core_copy(half, j):
        order = me.orders[half]
        where = me.at(order[:j], other=order[j])
        ref = pair.at[where + (me.core, slice(None), column_half(pair, half))]
        return remote(ref, ref, pcs.at[half, j + 1], pcr.at[half, j + 1], ctx=me.partner)

    def pair_stage(j):
        if j == 0:
            pair_store.wait()
        for half in (0, 1):
            pair_copy(half, j).wait_recv()
        if j + 1 < me.bits:
            for half in (0, 1):
                pair_copy(half, j + 1).start()
        for half in (0, 1):
            pair_core_copy(half, j).start()

    def pause():
        pass

    project_job = [norm_stage] + [pause] * me.bits
    project_job += [matmul_stage, key_stage]
    project_job += [functools.partial(pair_stage, j) for j in range(me.bits)]
    angle_stage()
    for load in loads:
        load.wait()
    for store in stores:
        store.start()
    run_ticks(jobs[: nf - 1] + [project_job] + jobs[nf - 1 :])
    query_stage()
    for k in range(1, nf):
        small_copy(k).wait_send()
    pair_own_core.wait()
    for j in range(me.bits):
        for half in (0, 1):
            pair_copy(half, j).wait_send()
            pair_core_copy(half, j).wait()
    weight_store.wait()
    for i in range(count):
        @pl.when(z + 1 < nf)
        def _():
            line_copy(i, z, shards[i].at[(me.core,) + me.at()], True).wait_send()

        @pl.when(z > 0)
        def _():
            line_copy(i, z, shards[i].at[(me.core,) + me.at()], False).wait_send()

    for i, k in order:
        src_z = sources[k]
        here = outs[i].at[(src_z, me.core) + me.at()]

        @pl.when(jnp.logical_and(src_z < z, z + 1 < nf))
        def _():
            line_copy(i, src_z, here, True).wait_send()

        @pl.when(jnp.logical_and(src_z > z, z > 0))
        def _():
            line_copy(i, src_z, here, False).wait_send()

        for half in (0, 1):
            for j in range(me.bits):
                plane_copy(i, k, half, j).wait_send()
        core_copy(i, k).wait_send()
    for store in stores:
        store.wait()


AHEAD = 1


def gather_weights(nf, nc, shards, small, tokens, order, starts, frequency):
    _, bits = plane_shape(nc)
    count = len(shards)
    rows, width = tokens.shape
    shape = jax.ShapeDtypeStruct
    low, full = jnp.bfloat16, jnp.float32
    query_width = QUERY_HEADS * HEAD_SIZE
    pair_width = 2 * KEY_VALUE_HEADS * HEAD_SIZE
    views = [w.reshape((2,) * (1 + bits) + (w.shape[0] // nc, w.shape[1])) for w in shards]
    outs = pl.pallas_call(
        functools.partial(gather_kernel, nf, nc, count),
        out_shape=[shape((nf,) + v.shape, v.dtype) for v in views]
        + [
            shape((1, width), full),
            shape((1, width), full),
            shape((2, LANES), full),
            shape((width, rows), low),
            shape((rows, shards[0].shape[1]), full),
            shape((rows, query_width), low),
            shape((rows, LANES), full),
            shape((rows, LANES), full),
            shape((2,) * (bits + 1) + (rows, pair_width), low),
        ],
        in_specs=[HBM_SPEC] * count + [VMEM_SPEC] * 2 + [SMEM_SPEC] * 2 + [VMEM_SPEC],
        out_specs=[HBM_SPEC] * count + [VMEM_SPEC] * 8 + [HBM_SPEC],
        scratch_shapes=[
            pltpu.VMEM((nf,) + views[0].shape, low),
            pltpu.VMEM((nf,) + small.shape, full),
            pltpu.VMEM((rows, width), low),
            pltpu.VMEM((rows, pair_width), low),
        ]
        + [pltpu.VMEM(v.shape, v.dtype) for v in views[1:]]
        + [DMA((count, nf))] * 4
        + [DMA((2, count, nf, bits))] * 2
        + [DMA((count, nf))] * 2
        + [DMA((nf,))] * 2
        + [DMA((count,))] * 2
        + [DMA((2, bits))] * 2
        + [DMA((2, bits + 1))] * 2
        + [DMA],
        compiler_params=pltpu.CompilerParams(
            collective_id=0, has_side_effects=True, vmem_limit_bytes=VMEM_LIMIT
        ),
        name="gather_weights",
    )(*views, small, tokens, order, starts, frequency)
    full_weights = [o.reshape(nf * w.shape[0], w.shape[1]) for o, w in zip(outs, shards)]
    return full_weights, outs[count:-1], outs[-1].reshape(nc * rows, pair_width)


def reduce_kernel(nf, nc, pairs, lefts_count, rights_count, *refs):
    _, bits = plane_shape(nc)
    count = len(pairs)
    rest = list(refs)

    def take(n):
        return [rest.pop(0) for _ in range(n)]

    lefts, rights = take(lefts_count), take(rights_count)
    grad_pair, back_in = take(1)[0], take(BACK_LOADS)
    gain, qk_gain, cosines, sines, ffn_gain_part = take(5)
    outs, (tokens_grad, small_out) = take(count), take(2)
    left_v, right_v, held = take(lefts_count), take(rights_count + 1), take(count)
    ins = [[take(2) for _ in range(bits)] for _ in range(count)]
    line_in, final = take(count), take(count)
    small_sum, small_in, small_line = take(3)
    pair_held, pair_core, *pair_in = take(2 + 2 * bits)
    back_v, grads = take(BACK_LOADS), take(1)[0]
    back_sem, grad_sem, pl_sem, pcs, pcr, pps, ppr = take(7)
    (ll, lls, llr, rl, rls, rlr, ps, pr, ls, lr, gs, gr, cs, cr, own_sem, ss, sr, sls, slr) = rest
    me = Place(nc, nf)
    z = me.z
    rows = rights[0].shape[0]
    projected_v = right_v[rights_count]
    back_loads = [
        pltpu.make_async_copy(src, dst, back_sem.at[n])
        for n, (src, dst) in enumerate(zip(back_in, back_v))
    ]
    every = tuple(slice(None) for _ in range(bits))
    pair_load = pltpu.make_async_copy(grad_pair.at[every + (me.core,)], pair_held, pl_sem)
    pair_core_copy = remote(
        grad_pair.at[every + (1 - me.core,)], pair_core, pcs, pcr, ctx=me.partner
    )

    def left_load(a):
        return pltpu.make_async_copy(
            lefts[a].at[:, me.core], left_v[a].at[:, :, pl.ds(0, rows)], ll.at[a]
        )

    def right_load(b):
        return pltpu.make_async_copy(rights[b], right_v[b].at[pl.ds(0, rows)], rl.at[b])

    def left_copy(a):
        return remote(
            lefts[a].at[:, 1 - me.core],
            left_v[a].at[:, :, pl.ds(rows, rows)],
            lls.at[a],
            llr.at[a],
            ctx=me.partner,
        )

    def right_copy(b):
        src = rights[b] if b < rights_count else projected_v.at[pl.ds(0, rows)]
        return remote(
            src, right_v[b].at[pl.ds(rows, rows)], rls.at[b], rlr.at[b], ctx=me.partner
        )

    order, seen = [], set()
    for a, b in pairs:
        for key in (("left", a), ("right", b)):
            if key not in seen and key != ("right", rights_count):
                seen.add(key)
                order.append(key)
    for at, (side, n) in enumerate(order):
        (left_load if side == "left" else right_load)(n).start()
        if at == 1:
            pair_load.start()
    for load in back_loads:
        load.start()
    me.barrier()
    for at, (side, n) in enumerate(order):
        (left_copy if side == "left" else right_copy)(n).start()
        if at == 1:
            pair_core_copy.start()
    arrived = set()

    def arrive(side, n):
        if (side, n) not in arrived:
            arrived.add((side, n))
            if (side, n) in order:
                (left_load if side == "left" else right_load)(n).wait()
            (left_copy if side == "left" else right_copy)(n).wait_recv()

    def target(k):
        return (z + k) % nf

    def form(i, k):
        a, b = pairs[i]
        arrive("left", a)
        arrive("right", b)
        width = held[i].shape[-1]
        chunk = min(width, CHUNK)

        def body(t, carry):
            cols = pl.ds(pl.multiple_of(t * chunk, chunk), chunk)
            value = dot_plain(left_v[a][target(k)], right_v[b][:, cols]).astype(jnp.bfloat16)
            held[i][target(k), ..., cols] = value.reshape(held[i].shape[1:-1] + (chunk,))
            return carry

        lax.fori_loop(0, width // chunk, body, 0)

    def plane_copy(i, k, half, j):
        order = me.orders[half]
        src = held[i].at[
            (target(k),)
            + me.at(order[j + 1 :], other=order[j])
            + (slice(None), column_half(held[i], half))
        ]
        return remote(
            src,
            ins[i][j][half].at[k],
            ps.at[half, i, k, j],
            pr.at[half, i, k, j],
            ctx=me.across[order[j]],
        )

    def pair_copy(half, j):
        order = me.orders[half]
        src = pair_held.at[
            me.at(order[j + 1 :], other=order[j]) + (slice(None), column_half(pair_held, half))
        ]
        return remote(
            src, pair_in[2 * j + half], pps.at[half, j], ppr.at[half, j], ctx=me.across[order[j]]
        )

    def pair_add(place, source, local, cols):
        where = place + (slice(None), cols)
        total = pair_held[where].astype(jnp.float32) + source[local].astype(jnp.float32)
        pair_held[where] = total.astype(pair_held.dtype)

    def pair_stage(j):
        if j == 0:
            pair_load.wait()
            pair_core_copy.wait_recv()
            for place, local in chips_of(range(bits)):
                pair_add(place, pair_core, local, slice(None))
        else:
            for half in (0, 1):
                pair_copy(half, j - 1).wait_recv()
                for place, local in chips_of(me.orders[half][j:]):
                    pair_add(place, pair_in[2 * (j - 1) + half], local, column_half(pair_held, half))
        if j < bits:
            for half in (0, 1):
                pair_copy(half, j).start()

    tokens, weight, raw, grad_query, grad_resid = back_v
    query_width = QUERY_HEADS * HEAD_SIZE
    key_width = KEY_VALUE_HEADS * HEAD_SIZE
    own = pl.ds(0, rows)

    def head_back(cols, which, grad):
        grad = turn(grad, cosines[...], sines[...], -1.0)
        value = raw[:, cols]
        scale = lax.rsqrt(head_means(value * value) + EPSILON)
        scaled = grad * qk_gain[which : which + 1, :]
        mean = head_means(scaled * value)
        result = scale * (scaled - value * scale * scale * mean)
        projected_v[own, cols] = result.astype(jnp.bfloat16)
        return jnp.sum(grad * value * scale, axis=0, keepdims=True)

    def heads_stage():
        for load in back_loads:
            load.wait()
        sums = [jnp.zeros((1, LANES), jnp.float32)] * 2
        for j in range(0, query_width, LANES):
            cols = pl.ds(j, LANES)
            sums[0] = sums[0] + head_back(cols, 0, grad_query[:, cols] * HEAD_SIZE**-0.5)
        here = me.at()
        for j in range(0, key_width, LANES):
            first = pair_held[here + (slice(None), pl.ds(2 * j, LANES))].astype(jnp.float32)
            second = pair_held[here + (slice(None), pl.ds(2 * j + LANES, LANES))].astype(
                jnp.float32
            )
            low = low_lanes(first.shape)
            key = jnp.where(low, first, pltpu.roll(second, HEAD_SIZE, 1))
            value = jnp.where(low, pltpu.roll(first, HEAD_SIZE, 1), second)
            sums[1] = sums[1] + head_back(pl.ds(query_width + j, LANES), 1, key)
            projected_v[own, pl.ds(query_width + key_width + j, LANES)] = value.astype(jnp.bfloat16)
        both = [total + pltpu.roll(total, HEAD_SIZE, 1) for total in sums]
        small_sum[0, pl.ds(2 * gain_rows, 1), :] = jnp.where(
            low_lanes(both[0].shape), both[0], both[1]
        )
        right_copy(rights_count).start()

    gain_rows = gain.shape[1] // LANES
    width = gain.shape[1]
    inverse_mean = []

    def matmul_stage():
        inverse = row_inverse(tokens, rows)
        mean = jnp.zeros((rows, 1), jnp.float32)
        for j in range(0, width, CHUNK):
            cols = pl.ds(j, CHUNK)
            grad = dot_last(projected_v[own, :], weight[cols, :])
            grads[:, cols] = grad
            value = tokens[:, cols].astype(jnp.float32)
            mean = mean + jnp.sum(grad * gain[:, cols] * value, axis=1, keepdims=True)
        inverse_mean.extend([inverse, mean * (1.0 / width) * inverse * inverse])

    def norm_stage():
        inverse, mean = inverse_mean
        for j in range(0, width, CHUNK):
            cols = pl.ds(j, CHUNK)
            grad = grads[:, cols]
            value = tokens[:, cols].astype(jnp.float32)
            part = jnp.sum(grad * value * inverse, axis=0, keepdims=True)
            for c in range(0, CHUNK, LANES):
                small_sum[0, pl.ds((j + c) // LANES, 1), :] = part[:, c : c + LANES]
            grad_resid[:, cols] = grad_resid[:, cols] + inverse * (
                grad * gain[:, cols] - value * mean
            )
        tokens_grad_store.start()

    tokens_grad_store = pltpu.make_async_copy(grad_resid, tokens_grad, grad_sem)

    def chips_of(free):
        places, local = [()], [()]
        for b in reversed(range(bits)):
            if b in free:
                places = [t + (v,) for t in places for v in (0, 1)]
                local = [t + (v,) for t in local for v in (0, 1)]
            else:
                places = [t + (me.bit[b],) for t in places]
        return list(zip(places, local))

    def add(i, k, half, j):
        free = me.orders[half][j + 1 :]
        rows, width = held[i].shape[-2], held[i].shape[-1] // 2
        step = min(rows, 32)
        cols = pl.ds(half * width, width)
        for place, local in chips_of(free):

            def body(t, carry, place=place, local=local):
                at = pl.ds(pl.multiple_of(t * step, step), step)
                where = (target(k),) + place + (at, cols)
                total = held[i][where].astype(jnp.float32) + ins[i][j][half][
                    (k,) + local + (at,)
                ].astype(jnp.float32)
                held[i][where] = total.astype(held[i].dtype)
                return carry

            lax.fori_loop(0, rows // step, body, 0)

    def line_copy(i, k):
        return remote(
            held[i].at[(target(k),) + me.at()],
            line_in[i].at[k],
            ls.at[i, k],
            lr.at[i, k],
            fsdp=target(k),
        )

    def stage(i, k, j):
        if j == 0:
            form(i, k)
        else:
            send(i, k, j - 1)

    def send(i, k, j):
        if j > 0:
            for half in (0, 1):
                plane_copy(i, k, half, j - 1).wait_recv()
                add(i, k, half, j - 1)
        if j < bits:
            for half in (0, 1):
                plane_copy(i, k, half, j).start()
        elif k != 0:
            line_copy(i, k).start()

    def own_copy(i):
        return pltpu.make_async_copy(final[i], outs[i].at[(me.core,) + me.at()], own_sem.at[i])

    def gather_copy(i, half, j):
        order = me.orders[half]
        cols = column_half(final[i], half)
        dst = outs[i].at[(me.core,) + me.at(order[:j]) + (slice(None), cols)]
        src = final[i].at[:, cols] if j == 0 else dst
        return remote(
            src, dst, gs.at[half, i, j], gr.at[half, i, j], ctx=me.across[order[j]]
        )

    def core_copy(i):
        ref = outs[i].at[me.core]
        return remote(ref, ref, cs.at[i], cr.at[i], ctx=me.partner)

    def total(i):
        for k in range(1, nf):
            line_copy(i, k).wait_recv()
        rows = final[i].shape[0]
        step = min(rows, 32)

        def body(t, carry):
            at = pl.ds(pl.multiple_of(t * step, step), step)
            value = held[i][(z,) + me.at() + (at,)].astype(jnp.float32)
            for k in range(1, nf):
                value = value + line_in[i][k, at].astype(jnp.float32)
            final[i][at] = value.astype(final[i].dtype)
            return carry

        lax.fori_loop(0, rows // step, body, 0)
        own_copy(i).start()

    def gather_stage(i, j):
        if j == 0:
            own_copy(i).wait()
        else:
            for half in (0, 1):
                gather_copy(i, half, j - 1).wait_recv()
        if j < bits:
            for half in (0, 1):
                gather_copy(i, half, j).start()
        else:
            core_copy(i).start()

    across = [me.partner] + me.across

    def small_copy(s):
        return remote(small_sum.at[s], small_in.at[s], ss.at[s], sr.at[s], ctx=across[s])

    def small_line_copy(k):
        return remote(
            small_sum.at[bits + 1], small_line.at[z], sls.at[k], slr.at[k], fsdp=target(k)
        )

    def small_stage(s):
        if s > 0:
            small_copy(s - 1).wait_recv()
            small_sum[s] = small_sum[s - 1] + small_in[s - 1]
        if s <= bits:
            small_copy(s).start()
        else:
            for k in range(1, nf):
                small_line_copy(k).start()
            small_line[z] = small_sum[s]

    small_sum[0] = jnp.zeros(small_sum.shape[1:], jnp.float32)
    for r in range(gain_rows):
        small_sum[0, pl.ds(gain_rows + r, 1), :] = ffn_gain_part[:, r * LANES : (r + 1) * LANES]
    jobs = []
    for i in range(count):
        for k in list(range(1, nf)) + [0]:
            job = [functools.partial(stage, i, k, j) for j in range(bits + 2)]
            if k == 0:
                job += [functools.partial(total, i)]
                job += [functools.partial(gather_stage, i, j) for j in range(bits + 1)]
                job += [core_copy(i).wait_recv]
            jobs.append(job)
    back_job = [functools.partial(pair_stage, j) for j in range(bits + 1)]
    back_job += [heads_stage, matmul_stage, norm_stage]
    back_job += [functools.partial(small_stage, s) for s in range(bits + 2)]
    run_ticks(jobs[:1] + [back_job] + jobs[1:])
    for k in range(1, nf):
        small_line_copy(k).wait_recv()
    value = small_line[0]
    for k in range(1, nf):
        value = value + small_line[k]
    small_out[...] = value
    for s in range(bits + 1):
        small_copy(s).wait_send()
    for k in range(1, nf):
        small_line_copy(k).wait_send()
    for i in range(count):
        for k in range(nf):
            for half in (0, 1):
                for j in range(bits):
                    plane_copy(i, k, half, j).wait_send()
            if k:
                line_copy(i, k).wait_send()
        for half in (0, 1):
            for j in range(bits):
                gather_copy(i, half, j).wait_send()
        core_copy(i).wait_send()
    for side, n in order + [("right", rights_count)]:
        (left_copy if side == "left" else right_copy)(n).wait_send()
    pair_core_copy.wait_send()
    for half in (0, 1):
        for j in range(bits):
            pair_copy(half, j).wait_send()
    tokens_grad_store.wait()


BACK_LOADS = 5


def reduce_gradients(nf, nc, pairs, lefts, rights, grad_pair, back, ffn_gain_part):
    _, bits = plane_shape(nc)
    rows = rights[0].shape[0]
    count = len(pairs)
    views = [a.reshape(nf, 2, a.shape[0] // (2 * nf), rows) for a in lefts]
    widths = [b.shape[1] for b in rights] + [back[1].shape[1]]
    pieces = [(lefts[a].shape[0] // (nf * nc), widths[b]) for a, b in pairs]
    pair_rows, pair_width = grad_pair.shape[0] // nc, grad_pair.shape[1]
    pair_view = grad_pair.reshape((2,) * (bits + 1) + (pair_rows, pair_width))
    gain_rows = 2 * ffn_gain_part.shape[1] // LANES + 1
    small = jax.ShapeDtypeStruct((gain_rows + -gain_rows % 8, LANES), jnp.float32)
    outs = pl.pallas_call(
        functools.partial(reduce_kernel, nf, nc, pairs, len(lefts), len(rights)),
        out_shape=[
            jax.ShapeDtypeStruct((2,) * (bits + 1) + piece, jnp.bfloat16) for piece in pieces
        ]
        + [jax.ShapeDtypeStruct(back[4].shape, jnp.float32), small],
        in_specs=[HBM_SPEC] * (len(lefts) + len(rights) + 1 + BACK_LOADS) + [VMEM_SPEC] * 5,
        out_specs=[HBM_SPEC] * (count + 1) + [VMEM_SPEC],
        scratch_shapes=[
            pltpu.VMEM((nf, v.shape[2], 2 * rows), jnp.bfloat16) for v in views
        ]
        + [pltpu.VMEM((2 * rows, n), jnp.bfloat16) for n in widths]
        + [pltpu.VMEM((nf,) + (2,) * bits + piece, jnp.bfloat16) for piece in pieces]
        + [
            pltpu.VMEM((nf,) + (2,) * (bits - 1 - j) + (r, width // 2), jnp.bfloat16)
            for r, width in pieces
            for j in range(bits)
            for _ in (0, 1)
        ]
        + [pltpu.VMEM((nf,) + piece, jnp.bfloat16) for piece in pieces]
        + [pltpu.VMEM(piece, jnp.bfloat16) for piece in pieces]
        + [
            pltpu.VMEM((bits + 2,) + small.shape, jnp.float32),
            pltpu.VMEM((bits + 1,) + small.shape, jnp.float32),
            pltpu.VMEM((nf,) + small.shape, jnp.float32),
        ]
        + [pltpu.VMEM((2,) * bits + (pair_rows, pair_width), jnp.bfloat16)] * 2
        + [
            pltpu.VMEM((2,) * (bits - 1 - j) + (pair_rows, pair_width // 2), jnp.bfloat16)
            for j in range(bits)
            for _ in (0, 1)
        ]
        + [pltpu.VMEM(v.shape, v.dtype) for v in back[:BACK_LOADS]]
        + [pltpu.VMEM(back[4].shape, jnp.float32)]
        + [DMA((BACK_LOADS,)), DMA, DMA, DMA, DMA, DMA((2, bits)), DMA((2, bits))]
        + [DMA((len(lefts),))] * 3
        + [DMA((len(widths),))] * 3
        + [DMA((2, count, nf, bits))] * 2
        + [DMA((count, nf))] * 2
        + [DMA((2, count, bits))] * 2
        + [DMA((count,))] * 2
        + [DMA((count,))]
        + [DMA((bits + 1,))] * 2
        + [DMA((nf,))] * 2,
        compiler_params=pltpu.CompilerParams(
            collective_id=2, has_side_effects=True, vmem_limit_bytes=VMEM_LIMIT
        ),
        name="reduce_gradients",
    )(*views, *rights, pair_view, *back, ffn_gain_part)
    return [
        o.reshape(r * nc, width) for o, (r, width) in zip(outs, pieces)
    ], outs[count], outs[count + 1]


WIDEN_STEPS = 4


def widen_kernel(*refs):
    count = len(refs) // 2
    for source, target in zip(refs[:count], refs[count:]):
        target[...] = source[...].astype(jnp.float32)


def widen(arrays):
    specs = [
        pl.BlockSpec((a.shape[0] // WIDEN_STEPS, a.shape[1]), lambda t: (t, 0)) for a in arrays
    ]
    return pl.pallas_call(
        widen_kernel,
        grid=(WIDEN_STEPS,),
        out_shape=[jax.ShapeDtypeStruct(a.shape, jnp.float32) for a in arrays],
        in_specs=specs,
        out_specs=specs,
        compiler_params=pltpu.CompilerParams(vmem_limit_bytes=VMEM_LIMIT),
        name="widen",
    )(*arrays)


LANES = 128
GROUP = QUERY_HEADS // KEY_VALUE_HEADS
SMEM_SPEC = pl.BlockSpec(memory_space=pltpu.SMEM)


def low_lanes(shape):
    return lax.broadcasted_iota(jnp.int32, shape, len(shape) - 1) % LANES < HEAD_SIZE


def stack_heads(ref, row, group, length, high):
    tiles = []
    for pair in range(GROUP // 2):
        cols = pl.ds((group * GROUP // 2 + pair) * LANES, LANES)
        tile = ref[pl.ds(row, length), cols].astype(jnp.float32)
        turned = pltpu.roll(tile, HEAD_SIZE, 1)
        low = low_lanes(tile.shape)
        if high:
            tiles += [jnp.where(low, 0.0, turned), jnp.where(low, 0.0, tile)]
        else:
            tiles += [jnp.where(low, tile, 0.0), jnp.where(low, turned, 0.0)]
    return jnp.concatenate(tiles, axis=0)


def unstack_heads(ref, row, group, length, value, high):
    for pair in range(GROUP // 2):
        cols = pl.ds((group * GROUP // 2 + pair) * LANES, LANES)
        first = value[2 * pair * length : (2 * pair + 1) * length]
        second = value[(2 * pair + 1) * length : (2 * pair + 2) * length]
        low = low_lanes(first.shape)
        if high:
            tile = jnp.where(low, pltpu.roll(first, HEAD_SIZE, 1), second)
        else:
            tile = jnp.where(low, first, pltpu.roll(second, HEAD_SIZE, 1))
        ref[pl.ds(row, length), cols] = tile.astype(ref.dtype)


def query_span(rank, order, starts, stored_of, which, length):
    block = order[2 * rank + which]
    first = jnp.int32(0)
    place = block * length + lax.broadcasted_iota(jnp.int32, (1, length), 1)
    begin = jnp.zeros((1, length), jnp.int32)
    for d in range(starts.shape[1]):
        first = jnp.where(starts[0, d] <= block * length, starts[0, d], first)
        begin = jnp.where(starts[0, d] <= place, starts[0, d], begin)
    place = jnp.concatenate([place] * GROUP, axis=1)
    begin = jnp.concatenate([begin] * GROUP, axis=1)
    return block, first // length, place, begin


def invert_order(order, stored_of):
    for s in range(order.shape[0]):
        stored_of[order[s]] = s


def key_rows(stored_of, block, length, blocks):
    second = stored_of[jnp.minimum(block + 1, blocks - 1)]
    return [
        pl.ds(pl.multiple_of(s * length, length), length) for s in (stored_of[block], second)
    ]


def allowed_keys(block, place, begin, length):
    key = block * length + lax.broadcasted_iota(jnp.int32, (2 * length, place.shape[1]), 0)
    return (key >= begin) & (key <= place)


def dot_last(left, right):
    return lax.dot_general(
        left, right, (((1,), (1,)), ((), ())), preferred_element_type=jnp.float32
    )


def dot_plain(left, right):
    return lax.dot_general(
        left, right, (((1,), (0,)), ((), ())), preferred_element_type=jnp.float32
    )


def attend_kernel(rank, order, starts, query, pair, attended, exact, log_sum, stored_of, acc, queries):
    length = query.shape[0] // 2
    blocks = order.shape[0]
    invert_order(order, stored_of)

    def one_block(which, carry):
        row = pl.multiple_of(which * length, length)
        block, first, place, begin = query_span(rank[0], order, starts, stored_of, which, length)
        for g in range(KEY_VALUE_HEADS):
            queries[g] = stack_heads(query, row, g, length, False).astype(jnp.bfloat16)
        acc[...] = jnp.zeros_like(acc)

        def step(t, carry):
            key_block = first + 2 * t
            rows = key_rows(stored_of, key_block, length, blocks)
            allowed = allowed_keys(key_block, place, begin, length)
            for g in range(KEY_VALUE_HEADS):
                cols = pl.ds(g * LANES, LANES)
                keys = jnp.concatenate([pair[r, cols] for r in rows], axis=0)
                scores = dot_last(keys, queries[g])
                weights = jnp.where(allowed, jnp.exp(scores), 0.0).astype(jnp.bfloat16)
                ones = jnp.where(low_lanes(keys.shape), 1.0, keys.astype(jnp.float32))
                acc[g] += dot_plain(ones.T.astype(jnp.bfloat16), weights)
            return carry

        lax.fori_loop(0, (block - first + 2) // 2, step, 0)
        for g in range(KEY_VALUE_HEADS):
            total = acc[g]
            sums = total[0:1]
            log_sum[which, g] = jnp.broadcast_to(jnp.log(sums), log_sum.shape[2:])
            value = (total / sums).T
            unstack_heads(attended, row, g, length, value, True)
            unstack_heads(exact, row, g, length, value, True)
        return carry

    lax.fori_loop(0, 2, one_block, 0)


def attend(rank, order, starts, query, pair):
    rows = query.shape[0]
    wide = GROUP * (rows // 2)
    return pl.pallas_call(
        attend_kernel,
        out_shape=[
            jax.ShapeDtypeStruct(query.shape, jnp.bfloat16),
            jax.ShapeDtypeStruct(query.shape, jnp.float32),
            jax.ShapeDtypeStruct((2, KEY_VALUE_HEADS, 8, wide), jnp.float32),
        ],
        in_specs=[SMEM_SPEC] * 3 + [VMEM_SPEC] * 2,
        out_specs=[VMEM_SPEC] * 3,
        scratch_shapes=[
            pltpu.SMEM((order.shape[0],), jnp.int32),
            pltpu.VMEM((KEY_VALUE_HEADS, LANES, wide), jnp.float32),
            pltpu.VMEM((KEY_VALUE_HEADS, wide, LANES), jnp.bfloat16),
        ],
        name="attend",
    )(rank, order, starts, query, pair)


def attend_back_kernel(
    rank, order, starts, query, pair, grad, exact, log_sum, grad_query, grad_pair,
    stored_of, total, acc, queries, grads, delta,
):
    length = query.shape[0] // 2
    blocks = order.shape[0]
    invert_order(order, stored_of)
    total[...] = jnp.zeros_like(total)

    def one_block(which, carry):
        row = pl.multiple_of(which * length, length)
        block, first, place, begin = query_span(rank[0], order, starts, stored_of, which, length)
        for g in range(KEY_VALUE_HEADS):
            queries[g] = stack_heads(query, row, g, length, False).astype(jnp.bfloat16)
            upper = stack_heads(grad, row, g, length, True)
            grads[g] = upper.astype(jnp.bfloat16)
            product = upper * stack_heads(exact, row, g, length, True)
            delta[g] = jnp.broadcast_to(
                jnp.sum(product.T, axis=0, keepdims=True), delta.shape[1:]
            )
        acc[...] = jnp.zeros_like(acc)

        def step(t, carry):
            key_block = first + 2 * t
            rows = key_rows(stored_of, key_block, length, blocks)
            allowed = allowed_keys(key_block, place, begin, length)
            for g in range(KEY_VALUE_HEADS):
                cols = pl.ds(g * LANES, LANES)
                keys = jnp.concatenate([pair[r, cols] for r in rows], axis=0)
                scores = dot_last(keys, queries[g])
                probs = jnp.where(allowed, jnp.exp(scores - log_sum[which, g, 0:1]), 0.0)
                grad_probs = dot_last(keys, grads[g])
                grad_scores = (probs * (grad_probs - delta[g, 0:1])).astype(jnp.bfloat16)
                turned = keys.astype(jnp.float32).T.astype(jnp.bfloat16)
                acc[g] += dot_plain(turned, grad_scores)
                both = dot_plain(grad_scores, queries[g]) + dot_plain(
                    probs.astype(jnp.bfloat16), grads[g]
                )
                total[rows[0], cols] += both[:length]
                total[rows[1], cols] += both[length:]
            return carry

        lax.fori_loop(0, (block - first + 2) // 2, step, 0)
        for g in range(KEY_VALUE_HEADS):
            unstack_heads(grad_query, row, g, length, acc[g].T, False)
        return carry

    lax.fori_loop(0, 2, one_block, 0)

    def finish(t, carry):
        at = pl.ds(pl.multiple_of(t * length, length), length)
        grad_pair[at, :] = total[at, :].astype(grad_pair.dtype)
        return carry

    lax.fori_loop(0, blocks, finish, 0)


def attend_back(rank, order, starts, query, pair, grad, exact, log_sum):
    rows = query.shape[0]
    wide = GROUP * (rows // 2)
    return pl.pallas_call(
        attend_back_kernel,
        out_shape=[
            jax.ShapeDtypeStruct(query.shape, jnp.float32),
            jax.ShapeDtypeStruct(pair.shape, jnp.bfloat16),
        ],
        in_specs=[SMEM_SPEC] * 3 + [VMEM_SPEC] * 5,
        out_specs=[VMEM_SPEC] * 2,
        scratch_shapes=[
            pltpu.SMEM((order.shape[0],), jnp.int32),
            pltpu.VMEM(pair.shape, jnp.float32),
            pltpu.VMEM((KEY_VALUE_HEADS, LANES, wide), jnp.float32),
            pltpu.VMEM((KEY_VALUE_HEADS, wide, LANES), jnp.bfloat16),
            pltpu.VMEM((KEY_VALUE_HEADS, wide, LANES), jnp.bfloat16),
            pltpu.VMEM((KEY_VALUE_HEADS, 8, wide), jnp.float32),
        ],
        name="attend_back",
    )(rank, order, starts, query, pair, grad, exact, log_sum)


CHUNK = 256


def head_means(values):
    shape = (LANES, LANES)
    same = (
        lax.broadcasted_iota(jnp.int32, shape, 0) // HEAD_SIZE
        == lax.broadcasted_iota(jnp.int32, shape, 1) // HEAD_SIZE
    )
    ones = jnp.where(same, 1.0, 0.0).astype(jnp.bfloat16)
    high = values.astype(jnp.bfloat16)
    low = (values - high.astype(jnp.float32)).astype(jnp.bfloat16)
    return (dot_plain(high, ones) + dot_plain(low, ones)) * (1.0 / HEAD_SIZE)


def first_quarter(shape):
    return lax.broadcasted_iota(jnp.int32, shape, len(shape) - 1) % HEAD_SIZE < HEAD_SIZE // 2


def turn(values, cosines, sines, sign):
    half = HEAD_SIZE // 2
    ahead = pltpu.roll(values, LANES - half, 1)
    behind = pltpu.roll(values, half, 1)
    other = jnp.where(first_quarter(values.shape), -ahead, behind)
    return values * cosines + sign * other * sines


def row_inverse(ref, rows):
    total = jnp.zeros((rows, 1), jnp.float32)
    width = ref.shape[1]
    for j in range(0, width, CHUNK):
        value = ref[:, j : j + CHUNK].astype(jnp.float32)
        total = total + jnp.sum(value * value, axis=1, keepdims=True)
    return lax.rsqrt(total * (1.0 / width) + EPSILON)


def feed_kernel(
    tokens, cotangent, attended, gain, w_out, w_gate, w_up, w_down,
    mixed, normed_turned, hidden_turned, attended_turned, grad_gate, grad_up, grad_resid, grad_branch,
    grad_attended, gain_grad,
    out_v, gate_v, up_v, down_v, resid, normed, hidden, sems,
):
    rows, width = tokens.shape
    loads = [
        pltpu.make_async_copy(src, dst, sems.at[i])
        for i, (src, dst) in enumerate(
            ((w_out, out_v), (w_gate, gate_v), (w_up, up_v), (w_down, down_v))
        )
    ]
    for load in loads:
        load.start()
    loads[0].wait()
    for j in range(0, width, CHUNK):
        cols = pl.ds(j, CHUNK)
        resid[:, cols] = tokens[:, cols].astype(jnp.float32) + dot_plain(
            attended[...], out_v[:, cols]
        )
    inverse = row_inverse(resid, rows)
    for j in range(0, width, CHUNK):
        cols = pl.ds(j, CHUNK)
        value = resid[:, cols] * inverse * gain[:, cols]
        normed[:, cols] = value.astype(jnp.bfloat16)
        normed_turned[cols, :] = value.T.astype(jnp.bfloat16)
    for load in loads[1:]:
        load.wait()
    for j in range(0, gate_v.shape[1], CHUNK):
        cols = pl.ds(j, CHUNK)
        gate = dot_plain(normed[...], gate_v[:, cols])
        up = dot_plain(normed[...], up_v[:, cols])
        sigmoid = 1.0 / (1.0 + jnp.exp(-gate))
        inner = gate * sigmoid * up
        hidden[:, cols] = inner.astype(jnp.bfloat16)
        hidden_turned[cols, :] = inner.T.astype(jnp.bfloat16)
        grad_hidden = dot_last(cotangent[...], down_v[cols, :])
        grad_gate[:, cols] = (
            grad_hidden * up * sigmoid * (1.0 + gate * (1.0 - sigmoid))
        ).astype(jnp.bfloat16)
        grad_up[:, cols] = (grad_hidden * gate * sigmoid).astype(jnp.bfloat16)
    mean = jnp.zeros((rows, 1), jnp.float32)
    for j in range(0, width, CHUNK):
        cols = pl.ds(j, CHUNK)
        mixed[:, cols] = (resid[:, cols] + dot_plain(hidden[...], down_v[:, cols])).astype(
            jnp.bfloat16
        )
        grad = dot_last(grad_gate[...], gate_v[cols, :]) + dot_last(grad_up[...], up_v[cols, :])
        grad_resid[:, cols] = grad
        mean = mean + jnp.sum(grad * gain[:, cols] * resid[:, cols], axis=1, keepdims=True)
    mean = mean * (1.0 / width) * inverse * inverse
    for j in range(0, width, CHUNK):
        cols = pl.ds(j, CHUNK)
        grad = grad_resid[:, cols]
        value = resid[:, cols]
        gain_grad[:, cols] = jnp.sum(grad * value * inverse, axis=0, keepdims=True)
        total = cotangent[:, cols].astype(jnp.float32) + inverse * (
            grad * gain[:, cols] - value * mean
        )
        grad_resid[:, cols] = total
        grad_branch[:, cols] = total.astype(jnp.bfloat16)
    for j in range(0, attended.shape[1], CHUNK):
        cols = pl.ds(j, CHUNK)
        attended_turned[cols, :] = attended[:, cols].astype(jnp.float32).T.astype(jnp.bfloat16)
        grad_attended[:, cols] = dot_last(grad_branch[...], out_v[cols, :]).astype(jnp.bfloat16)


def feed(tokens, cotangent, attended, gain, w_out, w_gate, w_up, w_down):
    rows, width = tokens.shape
    inner = w_gate.shape[1]
    shape = jax.ShapeDtypeStruct
    low, full = jnp.bfloat16, jnp.float32
    return pl.pallas_call(
        feed_kernel,
        out_shape=[
            shape((rows, width), low),
            shape((width, rows), low),
            shape((inner, rows), low),
            shape((attended.shape[1], rows), low),
            shape((rows, inner), low),
            shape((rows, inner), low),
            shape((rows, width), full),
            shape((rows, width), low),
            shape(attended.shape, low),
            shape((1, width), full),
        ],
        in_specs=[VMEM_SPEC] * 4 + [HBM_SPEC] * 4,
        out_specs=[VMEM_SPEC] * 10,
        scratch_shapes=[pltpu.VMEM(w.shape, low) for w in (w_out, w_gate, w_up, w_down)]
        + [
            pltpu.VMEM((rows, width), full),
            pltpu.VMEM((rows, width), low),
            pltpu.VMEM((rows, inner), low),
            DMA((4,)),
        ],
        name="feed",
    )(tokens, cotangent, attended, gain, w_out, w_gate, w_up, w_down)


def pack_rows(arrays, multiple):
    flat = jnp.concatenate([a.astype(jnp.float32).reshape(-1) for a in arrays])
    size = multiple * 128
    return jnp.pad(flat, (0, -flat.shape[0] % size)).reshape(-1, 128)


def per_device(
    tokens,
    cotangent,
    doc_starts,
    deal_order,
    query_key_value_weight,
    w_out,
    w_gate,
    w_up,
    w_down,
    gain_attn,
    gain_ffn,
    gain_qk,
):
    ctx_count = lax.axis_size("ctx")
    fsdp_count = lax.axis_size("fsdp")
    ctx_rank = lax.axis_index("ctx")
    fsdp_rank = lax.axis_index("fsdp")
    model_shard = gain_attn.shape[0]
    qk_shard = gain_qk.shape[1]
    model = model_shard * fsdp_count
    pack_in = tokens[0]
    grad_mixed = cotangent[0]
    rank = ctx_rank.reshape(1).astype(jnp.int32)
    frequency = THETA ** (-jnp.arange(0, HEAD_SIZE // 2, dtype=jnp.float32) * 2.0 / HEAD_SIZE)
    frequency = jnp.concatenate([frequency] * (2 * LANES // HEAD_SIZE)).reshape(1, LANES)
    lane = jnp.arange(LANES) % HEAD_SIZE - fsdp_rank * qk_shard
    own_lanes = (lane >= 0) & (lane < qk_shard)
    qk_rows = jnp.where(own_lanes, jnp.tile(gain_qk, (1, LANES // qk_shard)), 0)
    gains = pack_rows([gain_attn, gain_ffn, qk_rows], 8)
    weights, (attn_gain, ffn_gain, qk_gain, normed, raw, query, cosines, sines), pair = (
        gather_weights(
            fsdp_count,
            ctx_count,
            [query_key_value_weight, w_out, w_gate, w_up, w_down],
            gains,
            pack_in,
            deal_order,
            doc_starts,
            frequency,
        )
    )
    qkv_full, out_full, gate_full, up_full, down_full = weights
    attended, exact, log_sum = attend(rank, deal_order, doc_starts, query, pair)
    (
        mixed_out,
        normed_ffn,
        hidden,
        attended_turned,
        grad_gate,
        grad_up,
        grad_resid,
        grad_branch,
        grad_attended,
        ffn_gain_part,
    ) = feed(pack_in, grad_mixed, attended, ffn_gain, out_full, gate_full, up_full, down_full)
    grad_query, grad_pair = attend_back(
        rank, deal_order, doc_starts, query, pair, grad_attended, exact, log_sum
    )
    (down_grad, gate_grad, up_grad, out_grad, qkv_grad), tokens_grad, gain_sums = reduce_gradients(
        fsdp_count,
        ctx_count,
        ((0, 0), (1, 1), (1, 2), (2, 3), (3, 4)),
        [hidden, normed_ffn, attended_turned, normed],
        [grad_mixed, grad_gate, grad_up, grad_branch],
        grad_pair,
        [
            pack_in,
            qkv_full,
            raw,
            grad_query,
            grad_resid,
            attn_gain,
            qk_gain,
            cosines,
            sines,
        ],
        ffn_gain_part,
    )
    qkv_grad, out_grad, gate_grad, up_grad, down_grad, tokens_grad = widen(
        [qkv_grad, out_grad, gate_grad, up_grad, down_grad, tokens_grad]
    )
    gain_sums = gain_sums.reshape(-1)
    attn_gain_grad = lax.dynamic_slice_in_dim(gain_sums, fsdp_rank * model_shard, model_shard)
    ffn_gain_grad = lax.dynamic_slice_in_dim(
        gain_sums, model + fsdp_rank * model_shard, model_shard
    )
    qk_gain_grad = lax.dynamic_slice_in_dim(
        gain_sums[2 * model : 2 * model + 2 * HEAD_SIZE].reshape(2, HEAD_SIZE),
        fsdp_rank * qk_shard,
        qk_shard,
        axis=1,
    )
    return (
        mixed_out[None],
        tokens_grad[None],
        qkv_grad,
        out_grad,
        gate_grad,
        up_grad,
        down_grad,
        attn_gain_grad,
        ffn_gain_grad,
        qk_gain_grad,
    )


def solution(mesh):
    return jax.shard_map(
        per_device,
        mesh=mesh,
        in_specs=(
            P("fsdp", "ctx", None),
            P("fsdp", "ctx", None),
            P("fsdp", None),
            P(),
            P("fsdp", None),
            P("fsdp", None),
            P("fsdp", None),
            P("fsdp", None),
            P("fsdp", None),
            P("fsdp"),
            P("fsdp"),
            P(None, "fsdp"),
        ),
        out_specs=(
            P("fsdp", "ctx", None),
            P("fsdp", "ctx", None),
            P("fsdp", None),
            P("fsdp", None),
            P("fsdp", None),
            P("fsdp", None),
            P("fsdp", None),
            P("fsdp"),
            P("fsdp"),
            P(None, "fsdp"),
        ),
        check_vma=False,
    )
```
